512 devices in a mesh: dp: 8 (over x, y_hi), ctx: 64 (over y_lo, z, core).
Axes of the slice: x: 4, y: 8 (y_hi: 2, y_lo: 4; y = y_hi * 4 + y_lo), z: 8, core: 2. Of those that a mesh axis runs over, the one named last changes fastest.
Arguments:
- tile_features: bfloat16 [8, 32768, 768], P('dp', 'ctx'), may hold values from -6 to 6
- flip_perm: int32 [8, 32768], P('dp', 'ctx'), may hold values from 0 to 32767, as said below
- head_offsets: int32 [6], replicated, may hold values from 0 to 15, as said below
- input_gain: float32 [768], replicated, may hold values from 0.1 to 1.9
- projection: bfloat16 [768, 1152], P('dp'), may hold values from -12 to 12
- output_gain: float32 [384], replicated, may hold values from 0.1 to 1.9
- output_weight: bfloat16 [384, 768], P('dp'), may hold values from -0.3125 to 0.3125
Outputs:
- plain_view: bfloat16 [8, 32768, 768], P('dp', 'ctx')
- flipped_view: bfloat16 [8, 32768, 768], P('dp', 'ctx')
The draws below stay inside these ranges and needn't reach their ends.
Inputs may be any that keep to these rules, and one draw needn't show every extreme that they name: For each slide, flip_perm is a permutation of 0 to 32767; the positions b * 512 to (b + 1) * 512 - 1 hold the tiles of block 63 - b in an order drawn from the seed. `head_offsets`: the 6 offsets are distinct.
All inputs are finite; a program needn't handle non-finite values.
Results may differ from the reference program's by a relative error of at most 0.0083.
Values may be sent and summed in bfloat16 or wider, within the bound.
No kernel may reach another device: no remote copies, remote signals or barrier semaphores. Data moves between devices by JAX's collectives and lax.ppermute only.
A program may use at most 64 MiB of HBM per device.

```python
import jax
import jax.numpy as jnp
from jax import lax

D = 768
HEADS = 6
HEAD_DIM = 64
INNER = 384
SEGMENT = 1024
RATIO = 16
TOK_DEV = 512
SLIDES = 8
SEQ = 32768


def draw_tile_features(key, part):
    base_key = jax.random.fold_in(key, 0)
    drawn = jax.random.normal(base_key, (SLIDES, SEQ, D), jnp.float32)
    return jnp.clip(drawn, -6.0, 6.0).astype(jnp.bfloat16)


def draw_projection(key, part):
    first_key = jax.random.fold_in(key, 0)
    drawn = jax.random.normal(first_key, (D, 3 * INNER), jnp.float32) * D ** (-0.5)
    return jnp.clip(drawn, -12.0, 12.0).astype(jnp.bfloat16)


def draw_flip_perm(key, part):
    blocks = SEQ // TOK_DEV
    drawn = jax.random.randint(key, (SLIDES, blocks, TOK_DEV), 0, 2 ** 20)
    scores = drawn * TOK_DEV + jnp.arange(TOK_DEV, dtype=jnp.int32)
    within = jnp.argsort(scores, axis=-1).astype(jnp.int32)
    owner_base = (blocks - 1 - jnp.arange(blocks, dtype=jnp.int32))[None, :, None] * TOK_DEV
    return (within + owner_base).reshape(SLIDES, SEQ)


def draw_head_offsets(key, part):
    middle_key = jax.random.fold_in(key, 11)
    order_key = jax.random.fold_in(key, 13)
    middle = 1 + jax.random.permutation(middle_key, RATIO - 2).astype(jnp.int32)
    ends = jnp.array([0, RATIO - 1], dtype=jnp.int32)
    values = jnp.concatenate([ends, middle])[:HEADS]
    return values[jax.random.permutation(order_key, HEADS)].astype(jnp.int32)


def steps_of(stream_key, extent, cuts, low, largest):
    gain = 1.0
    for dim, blocks in cuts:
        steps = jax.random.uniform(jax.random.fold_in(jax.random.fold_in(stream_key, 6), dim), (blocks,), jnp.float32, low / len(cuts), largest / len(cuts))
        gain = gain * jnp.repeat(jnp.exp(steps), extent[dim] // blocks).reshape((-1,) + (1,) * (len(extent) - 1 - dim))
    return gain


def gaussian(key, shape, scale, reach, pieces=(), kind=jnp.bfloat16):
    gain = steps_of(key, shape, pieces, -0.22, 0.18) if pieces else 1.0
    values = jax.random.normal(key, shape, jnp.float32) * scale * gain
    return jnp.minimum(jnp.maximum(values, -reach), reach).astype(kind)


def setup_inputs(seed: int = 0) -> dict:
    splits = jax.random.split(jax.random.key(seed), 8)
    return {
        "tile_features": draw_tile_features(jax.random.fold_in(splits[7], 71), 0),
        "flip_perm": draw_flip_perm(jax.random.fold_in(splits[7], 71), 0),
        "head_offsets": draw_head_offsets(jax.random.fold_in(splits[7], 71), 0),
        "input_gain": jnp.clip(1.0 + 0.18 * jax.random.normal(splits[3], (D,), jnp.float32), 0.1, 1.9),
        "projection": draw_projection(jax.random.fold_in(splits[7], 71), 0),
        "output_gain": jnp.clip(1.0 + 0.18 * jax.random.normal(splits[5], (INNER,), jnp.float32), 0.1, 1.9),
        "output_weight": gaussian(splits[6], (INNER, D), INNER ** -0.5, 0.3125, ((0, 8),)),
    }


eps_norm = 1e-05

def layer_norm(values, scale_gain):
    average = lax.optimization_barrier(jnp.mean(values, axis=-1, keepdims=True))
    centred = values - average
    variance = lax.optimization_barrier(jnp.mean(centred * centred, axis=-1, keepdims=True))
    return centred * lax.rsqrt(variance + eps_norm) * scale_gain

def attend(queries, key_rows, value_rows):

    def one_head(packed):
        head_query, head_key, head_value = packed
        scores = jnp.einsum('vqd,vkd->vqk', head_query.astype(jnp.float32), head_key.astype(jnp.float32), precision=lax.Precision.HIGHEST) * HEAD_DIM ** (-0.5)
        row_max = lax.optimization_barrier(jnp.max(scores, axis=-1))
        weights = jnp.exp(scores - row_max[..., None])
        row_total = lax.optimization_barrier(jnp.sum(weights, axis=-1))
        rounded = weights.astype(jnp.bfloat16).astype(jnp.float32)
        summed = jnp.einsum('vqk,vkd->vqd', rounded, head_value.astype(jnp.float32), precision=lax.Precision.HIGHEST)
        return (row_max, row_total, summed)
    return lax.map(one_head, (queries, key_rows, value_rows))

def combine(near_max, near_total, near_sum, far_max, far_total, far_sum, picked_rows):
    head_ids = jnp.arange(near_max.shape[0], dtype=jnp.int32)[:, None]
    far_max_rows = near_max.at[head_ids, picked_rows].set(far_max)
    far_total_rows = jnp.zeros_like(near_total).at[head_ids, picked_rows].set(far_total)
    far_sum_rows = jnp.zeros_like(near_sum).at[head_ids, picked_rows].set(far_sum)
    joint_max = jnp.maximum(near_max, far_max_rows)
    near_scale = jnp.exp(near_max - joint_max)
    far_scale = jnp.exp(far_max_rows - joint_max)
    numerator = near_scale[..., None] * near_sum + far_scale[..., None] * far_sum_rows
    denominator = near_scale * near_total + far_scale * far_total_rows
    attended = numerator / denominator[..., None]
    return jnp.transpose(attended, (1, 0, 2)).reshape(attended.shape[1], -1)

def reference(tile_features, flip_perm, head_offsets, input_gain, projection, output_gain, output_weight):
    segments = SEQ // SEGMENT
    sparse_count = SEQ // RATIO
    picked = head_offsets[:, None] + RATIO * jnp.arange(sparse_count, dtype=jnp.int32)[None, :]
    head_ids = jnp.arange(HEADS, dtype=jnp.int32)[None, :]

    def far_level(heads_split, picked_rows):
        chosen = heads_split[picked_rows.T, :, head_ids]
        heads_first = jnp.transpose(chosen, (2, 1, 0, 3))[:, :, None]
        return attend(heads_first[0], heads_first[1], heads_first[2])

    def one_segment(segment_block):
        return attend(segment_block[0], segment_block[1], segment_block[2])

    def one_slide(packed):
        slide_rows, slide_perm = packed
        normed = layer_norm(slide_rows.astype(jnp.float32), input_gain).astype(jnp.bfloat16)
        projected = jnp.dot(normed, projection, preferred_element_type=jnp.float32).astype(jnp.bfloat16)
        heads_split = projected.reshape(SEQ, 3, HEADS, HEAD_DIM)
        blocks = jnp.transpose(heads_split.reshape(segments, SEGMENT, 3, HEADS, HEAD_DIM), (0, 2, 3, 1, 4))[:, :, :, None]
        near_max, near_total, near_sum = lax.map(one_segment, blocks)
        near_max = jnp.transpose(near_max[:, :, 0], (1, 0, 2)).reshape(HEADS, SEQ)
        near_total = jnp.transpose(near_total[:, :, 0], (1, 0, 2)).reshape(HEADS, SEQ)
        near_sum = jnp.transpose(near_sum[:, :, 0], (1, 0, 2, 3)).reshape(HEADS, SEQ, HEAD_DIM)
        results = []
        for picked_rows in (picked, jnp.take(slide_perm, picked)):
            far_max, far_total, far_sum = far_level(heads_split, picked_rows)
            attended = combine(near_max, near_total, near_sum, far_max[:, 0], far_total[:, 0], far_sum[:, 0], picked_rows)
            mixed = layer_norm(attended, output_gain).astype(jnp.bfloat16)
            results.append(jnp.dot(mixed, output_weight, preferred_element_type=jnp.float32).astype(jnp.bfloat16))
        return (results[0], results[1])
    plain_view, flipped_view = lax.map(one_slide, (tile_features, flip_perm))
    return (plain_view, flipped_view)
```

```python
import functools

import jax
import jax.numpy as jnp
from jax import lax
from jax.experimental import pallas as pl
from jax.experimental.pallas import tpu as pltpu
from jax.sharding import Mesh, PartitionSpec as P

HEADS = 6
HEAD_DIM = 64
INNER = 384
D = 768
RATIO = 16
TOK = 512
SEG = 1024
HALF = 3
SPARSE = TOK // RATIO
POS = 32
INTERPRET = False

eps_norm = 1e-05
EXP_SCALE = HEAD_DIM ** (-0.5) * 1.4426950408889634
SCALE = HEAD_DIM ** (-0.5)

F32 = jnp.float32
BF16 = jnp.bfloat16
VMEM = pl.BlockSpec(memory_space=pltpu.VMEM)
SMEM = pl.BlockSpec(memory_space=pltpu.SMEM)


def call(kernel, out_shape, specs, scratch=(), flops=0, moved=0):
    single = not isinstance(out_shape, (list, tuple))
    return pl.pallas_call(
        kernel,
        out_shape=out_shape,
        in_specs=specs,
        out_specs=VMEM if single else [VMEM] * len(out_shape),
        scratch_shapes=list(scratch),
        cost_estimate=pl.CostEstimate(flops=flops, bytes_accessed=moved, transcendentals=0),
        interpret=INTERPRET,
    )


def shape_of(*dims, dtype=BF16):
    return jax.ShapeDtypeStruct(dims, dtype)


def swap_halves(block):
    return jnp.concatenate([block[:, HEAD_DIM:], block[:, :HEAD_DIM]], axis=1)


def parts3(value):
    high = value.astype(BF16)
    rest = value - high.astype(F32)
    middle = rest.astype(BF16)
    low = (rest - middle.astype(F32)).astype(BF16)
    return high, middle, low


def pack_kernel(core_ref, proj_ref, outw_ref, packed_ref):
    for core in range(2):

        @pl.when(core_ref[0] == core)
        def _():
            for head in range(HALF):
                col = (core * HALF + head) * HEAD_DIM
                lanes = slice(head * 128, head * 128 + 128)
                keys = proj_ref[:, INNER + col : INNER + col + HEAD_DIM].astype(F32)
                values = proj_ref[:, 2 * INNER + col : 2 * INNER + col + HEAD_DIM].astype(F32)
                queries = proj_ref[:, col : col + HEAD_DIM].astype(F32)
                pair = jnp.concatenate([keys, values], axis=1).astype(BF16)
                folded = jnp.concatenate([queries[:48], queries[48:]], axis=1).astype(BF16)
                for peer in range(packed_ref.shape[0]):
                    packed_ref[peer, 0:96, lanes] = pair
                    packed_ref[peer, 96:144, lanes] = folded
            half = outw_ref[:, core * INNER : (core + 1) * INNER]
            for peer in range(packed_ref.shape[0]):
                packed_ref[peer, 144:192, :] = half


def pack_weights(core, projection, output_weight, peers):
    return call(pack_kernel, shape_of(peers, 192, INNER), [SMEM, VMEM, VMEM])(
        core, projection, output_weight
    )


def gather_weights(core, projection, output_weight):
    packed = pack_weights(core, projection, output_weight, 8)
    return lax.all_to_all(packed, "dp", 0, 0, tiled=True)


def norm_kernel(x_ref, gain_ref, out_ref):
    for row in range(0, TOK, 128):
        values = x_ref[row : row + 128, :].astype(F32)
        average = jnp.mean(values, axis=-1, keepdims=True)
        centred = values - average
        variance = jnp.mean(centred * centred, axis=-1, keepdims=True)
        out_ref[row : row + 128, :] = (
            centred * lax.rsqrt(variance + eps_norm) * gain_ref[...]
        ).astype(BF16)


def one_hot(view, offset, base_ref, own_ref, other_ref):
    if view == 0:
        rows = lax.broadcasted_iota(jnp.int32, (SPARSE, 1), 0) * RATIO + offset
        index = jnp.concatenate([rows, rows + TOK], axis=0)
    else:
        lane = lax.broadcasted_iota(jnp.int32, (SPARSE, RATIO), 1)
        own = jnp.sum(jnp.where(lane == offset, own_ref[...], 0), axis=1, keepdims=True)
        other = jnp.sum(jnp.where(lane == offset, other_ref[...], 0), axis=1, keepdims=True)
        index = jnp.concatenate([own - base_ref[1], other - base_ref[2] + TOK], axis=0)
    token = lax.broadcasted_iota(jnp.int32, (2 * SPARSE, SEG), 1)
    return jnp.where(token == index, 1.0, 0.0).astype(BF16)


def project_kernel(
    base_ref, offset_ref, own_x, other_x, packed_ref, own_ref, other_ref,
    kv_ref, q_ref, send_ref, wkv_ref, wq_ref,
):
    lane = lax.broadcasted_iota(jnp.int32, (48, 128), 1)
    for shard in range(8):
        wkv_ref[shard * 96 : shard * 96 + 96, :] = packed_ref[shard, 0:96, :]
        for head in range(HALF):
            lanes = slice(head * 128, head * 128 + 128)
            folded = packed_ref[shard, 96:144, lanes].astype(F32)
            first = jnp.where(lane < HEAD_DIM, folded, 0.0)
            second = jnp.where(lane < HEAD_DIM, swap_halves(folded), 0.0)
            wq_ref[shard * 96 : shard * 96 + 48, lanes] = first.astype(BF16)
            wq_ref[shard * 96 + 48 : shard * 96 + 96, lanes] = second.astype(BF16)
    for part, x_ref in enumerate((own_x, other_x)):
        rows = slice(part * TOK, part * TOK + TOK)
        kv_ref[rows, :] = jnp.dot(
            x_ref[...], wkv_ref[...], preferred_element_type=F32
        ).astype(BF16)
        q_ref[rows, :] = jnp.dot(
            x_ref[...], wq_ref[...], preferred_element_type=F32
        ).astype(BF16)
    for view in range(2):
        for head in range(HALF):
            lanes = slice(head * 128, head * 128 + 128)
            offset = offset_ref[base_ref[0] * HALF + head]
            chosen = one_hot(view, offset, base_ref, own_ref, other_ref)
            far_kv = jnp.dot(chosen, kv_ref[:, lanes], preferred_element_type=F32).astype(BF16)
            far_q = jnp.dot(chosen, q_ref[:, lanes], preferred_element_type=F32)
            pair = (view * HALF + head) * 4
            for q_half in range(2):
                row = q_half * SPARSE
                folded = (
                    far_q[row : row + 16] + swap_halves(far_q[row + 16 : row + 32])
                ).astype(BF16)
                for k_half in range(2):
                    peer = pair + q_half * 2 + k_half
                    send_ref[peer, 0:32, :] = far_kv[k_half * SPARSE : k_half * SPARSE + 32]
                    send_ref[peer, 32:48, :] = folded
    for peer in range(4 * 2 * HALF, POS):
        send_ref[peer] = jnp.zeros((48, 128), BF16)


def near_kernel(q_ref, kv_ref, out_ref):
    keys = kv_ref[...]
    lane = lax.broadcasted_iota(jnp.int32, (SEG, 128), 1)
    values = jnp.where(lane < HEAD_DIM, swap_halves(keys.astype(F32)), 1.0).astype(BF16)
    scores = lax.dot_general(
        q_ref[...], keys, (((1,), (1,)), ((), ())), preferred_element_type=F32
    )
    row_max = jnp.max(scores, axis=1, keepdims=True)
    weights = jnp.exp2((scores - row_max) * EXP_SCALE).astype(BF16)
    summed = jnp.dot(weights, values, preferred_element_type=F32)
    swapped = swap_halves(summed)
    out_lane = lax.broadcasted_iota(jnp.int32, summed.shape, 1)
    out_ref[...] = jnp.where(
        out_lane < HEAD_DIM, summed / swapped, row_max * SCALE + jnp.log(summed)
    )


def near_level(queries, key_pairs):
    tile = 256
    return pl.pallas_call(
        near_kernel,
        out_shape=shape_of(SEG, HALF * 128, dtype=F32),
        grid=(HALF, SEG // tile),
        in_specs=[
            pl.BlockSpec((tile, 128), lambda h, i: (i, h)),
            pl.BlockSpec((SEG, 128), lambda h, i: (0, h)),
        ],
        out_specs=pl.BlockSpec((tile, 128), lambda h, i: (i, h)),
        cost_estimate=pl.CostEstimate(
            flops=4 * HALF * SEG * SEG * 128, bytes_accessed=3 << 20, transcendentals=HALF * SEG * SEG
        ),
        interpret=INTERPRET,
    )(queries, key_pairs)


def far_kernel(got_ref, back_ref):
    keys = got_ref[:, 0:32, :].reshape(POS * 32, 128)
    folded = got_ref[:, 32:48, :].reshape(POS * 16, 128)
    lane = lax.broadcasted_iota(jnp.int32, (POS * 32, 128), 1)
    turned = swap_halves(keys.astype(F32))
    lane_q = lax.broadcasted_iota(jnp.int32, (POS * 16, 128), 1)
    wide = folded.astype(F32)
    outputs, logs = [], []
    for part in range(2):
        queries = jnp.where(lane_q < HEAD_DIM, wide if part == 0 else swap_halves(wide), 0.0)
        scores = lax.dot_general(
            queries.astype(BF16), keys, (((1,), (1,)), ((), ())), preferred_element_type=F32
        )
        row_max = jnp.max(scores, axis=1, keepdims=True)
        weights = jnp.exp2((scores - row_max) * EXP_SCALE).astype(BF16)
        if part == 0:
            values = jnp.where(lane < HEAD_DIM, turned, 1.0).astype(BF16)
        else:
            values = jnp.where(lane < HEAD_DIM, 1.0, keys.astype(F32)).astype(BF16)
        summed = jnp.dot(weights, values, preferred_element_type=F32)
        swapped = swap_halves(summed)
        outputs.append(summed / swapped)
        logs.append(row_max * SCALE + jnp.log(swapped if part == 0 else summed))
    merged = jnp.where(lane_q < HEAD_DIM, outputs[0], outputs[1]).astype(BF16)
    back_ref[:, 0:16, :] = merged.reshape(POS, 16, 128)
    total = jnp.where(lane_q < HEAD_DIM, logs[0], swap_halves(logs[1]))
    high, middle, low = (part.astype(F32) for part in parts3(total))
    slot = jnp.bitwise_and(lane_q, HEAD_DIM - 1)
    stats = jnp.where(slot == 0, high, jnp.where(slot == 1, middle, low)).astype(BF16)
    back_ref[:, 16:32, :] = stats.reshape(POS, 16, 128)


def join_kernel(base_ref, offset_ref, near_ref, back_ref, own_ref, other_ref, keep_ref, give_ref):
    for view in range(2):
        for head in range(HALF):
            offset = offset_ref[base_ref[0] * HALF + head]
            chosen = one_hot(view, offset, base_ref, own_ref, other_ref)
            outs, logs = [], []
            for k_half in range(2):
                rows, stats = [], []
                for q_half in range(2):
                    peer = (view * HALF + head) * 4 + q_half * 2 + k_half
                    block = back_ref[peer, 0:16, :].astype(F32)
                    stat = back_ref[peer, 16:32, :].astype(F32)
                    rows += [block[:, :HEAD_DIM], block[:, HEAD_DIM:]]
                    for at in (0, HEAD_DIM):
                        stats.append(
                            stat[:, at : at + 1] + stat[:, at + 1 : at + 2] + stat[:, at + 2 : at + 3]
                        )
                outs.append(jnp.concatenate(rows, axis=0))
                logs.append(jnp.concatenate(stats, axis=0))
            top = jnp.maximum(logs[0], logs[1])
            weight0, weight1 = jnp.exp(logs[0] - top), jnp.exp(logs[1] - top)
            joint = weight0 + weight1
            far = (weight0 * outs[0] + weight1 * outs[1]) / joint
            far_log = jnp.broadcast_to(top + jnp.log(joint), (2 * SPARSE, HEAD_DIM))
            both = jnp.concatenate([far, far_log], axis=1)
            ones = jnp.ones((2 * SPARSE, 128), BF16)
            none = jnp.zeros((2 * SPARSE, 128), BF16)
            right = jnp.concatenate(
                [
                    jnp.concatenate([part, ones if i == 0 else none], axis=1)
                    for i, part in enumerate(parts3(both))
                ],
                axis=0,
            )
            left = jnp.concatenate([chosen, chosen, chosen], axis=0)
            spread = lax.dot_general(
                left, right, (((0,), (0,)), ((), ())), preferred_element_type=F32
            )
            near = near_ref[:, head * 128 : head * 128 + 128]
            gap = spread[:, :128] - near
            share = spread[:, 128:] / (1.0 + jnp.exp(-gap))
            attended = near + swap_halves(share) * gap
            cols = slice(head * HEAD_DIM, head * HEAD_DIM + HEAD_DIM)
            keep_ref[view * TOK : view * TOK + TOK, cols] = attended[:TOK, :HEAD_DIM]
            give_ref[view * TOK : view * TOK + TOK, cols] = attended[TOK:, :HEAD_DIM].astype(BF16)


def output_kernel(core_ref, keep_ref, got_ref, gain_ref, own_w, other_w, plain_ref, flip_ref):
    core = core_ref[0]
    width = HALF * HEAD_DIM
    for row in range(0, 2 * TOK, 256):
        first = keep_ref[row : row + 256, :]
        second = got_ref[row : row + 256, :].astype(F32)
        average = (
            jnp.sum(first, axis=-1, keepdims=True) + jnp.sum(second, axis=-1, keepdims=True)
        ) / INNER
        first, second = first - average, second - average
        variance = (
            jnp.sum(first * first, axis=-1, keepdims=True)
            + jnp.sum(second * second, axis=-1, keepdims=True)
        ) / INNER
        scale = lax.rsqrt(variance + eps_norm)
        first = (first * scale * gain_ref[pl.ds(core, 1), :]).astype(BF16)
        second = (second * scale * gain_ref[pl.ds(1 - core, 1), :]).astype(BF16)
        out_ref = plain_ref if row < TOK else flip_ref
        at = row % TOK
        own_rows = pl.ds(pl.multiple_of(core * width, width), width)
        other_rows = pl.ds(pl.multiple_of((1 - core) * width, width), width)
        for weights, place in ((own_w, core), (other_w, 1 - core)):
            result = jnp.dot(first, weights[own_rows, :], preferred_element_type=F32) + jnp.dot(
                second, weights[other_rows, :], preferred_element_type=F32
            )
            out_ref[at : at + 256, pl.ds(pl.multiple_of(place * INNER, 128), INNER)] = result.astype(
                BF16
            )


def core_swap(block):
    return lax.ppermute(block, "core", [(0, 1), (1, 0)])


def per_device(
    tile_features, flip_perm, head_offsets, input_gain, projection, output_gain, output_weight
):
    core = lax.axis_index("core").astype(jnp.int32)
    pos = lax.axis_index("pos").astype(jnp.int32)
    rank = pos * 2 + core
    core_id = core[None]
    base = jnp.stack([core, rank * TOK, (rank ^ 1) * TOK])

    perm = flip_perm.reshape(SPARSE, RATIO)
    last = 2 * POS - 1
    own_perm = lax.ppermute(perm, ("pos", "core"), [(last - r, r) for r in range(2 * POS)])
    other_perm = lax.ppermute(perm, ("pos", "core"), [(last - (r ^ 1), r) for r in range(2 * POS)])

    own_x = call(norm_kernel, shape_of(TOK, D), [VMEM, VMEM])(
        tile_features[0], input_gain[None, :]
    )
    other_x = core_swap(own_x)
    packed = gather_weights(core_id, projection, output_weight)

    key_pairs, queries, send = call(
        project_kernel,
        [shape_of(SEG, INNER), shape_of(SEG, INNER), shape_of(POS, 48, 128)],
        [SMEM, SMEM, VMEM, VMEM, VMEM, VMEM, VMEM],
        [pltpu.VMEM((D, INNER), BF16), pltpu.VMEM((D, INNER), BF16)],
        flops=2 * SEG * D * 768,
        moved=4 << 20,
    )(base, head_offsets, own_x, other_x, packed, own_perm, other_perm)

    own_w = packed[:, 144:192, :].reshape(INNER, INNER)
    other_w = core_swap(own_w)

    got = lax.all_to_all(send, "pos", 0, 0, tiled=True)
    near = near_level(queries, key_pairs)
    back = call(far_kernel, shape_of(POS, 32, 128), [VMEM], flops=4 * SEG * SEG * 128, moved=1 << 20)(
        got
    )
    back = lax.all_to_all(back, "pos", 0, 0, tiled=True)

    keep, give = call(
        join_kernel,
        [shape_of(2 * TOK, HALF * HEAD_DIM, dtype=F32), shape_of(2 * TOK, HALF * HEAD_DIM)],
        [SMEM, SMEM, VMEM, VMEM, VMEM, VMEM],
        flops=12 * SEG * 192 * 256,
        moved=3 << 20,
    )(base, head_offsets, near, back, own_perm, other_perm)
    taken = core_swap(give)

    plain_view, flipped_view = call(
        output_kernel,
        [shape_of(TOK, D), shape_of(TOK, D)],
        [SMEM, VMEM, VMEM, VMEM, VMEM, VMEM],
        flops=4 * SEG * INNER * D,
        moved=4 << 20,
    )(core_id, keep, taken, output_gain.reshape(2, HALF * HEAD_DIM), own_w, other_w)
    return (plain_view[None], flipped_view[None])


def solution(mesh):
    fine = Mesh(mesh.devices.reshape(mesh.shape["dp"], POS, 2), ("dp", "pos", "core"))
    ctx = ("pos", "core")
    placed = (
        P("dp", ctx, None), P("dp", ctx), P(), P(), P("dp", None), P(), P("dp", None),
    )
    return jax.shard_map(
        per_device,
        mesh=fine,
        in_specs=placed,
        out_specs=(P("dp", ctx, None), P("dp", ctx, None)),
        check_vma=False,
    )
```

```python
import jax
import jax.numpy as jnp
from jax import lax
from jax.experimental import pallas as pl
from jax.experimental.pallas import tpu as pltpu
from jax.sharding import Mesh, PartitionSpec as P


HEADS = 6
HEAD_DIM = 64
INNER = 384
D = 768
RATIO = 16
TOK = 512
SEG = 1024
HALF = 3
SPARSE = TOK // RATIO
POS = 32
DP_X, DP_Y = 4, 2
INTERPRET = False
LIMITS = [60 * 1024 * 1024, 60 * 1024 * 1024, 24 << 20, 24 << 20, 24 << 20]

eps_norm = 1e-05
EXP_SCALE = HEAD_DIM ** (-0.5) * 1.4426950408889634
SCALE = HEAD_DIM ** (-0.5)

F32 = jnp.float32
BF16 = jnp.bfloat16
VMEM = pl.BlockSpec(memory_space=pltpu.VMEM)
SMEM = pl.BlockSpec(memory_space=pltpu.SMEM)
HBM = pl.BlockSpec(memory_space=pltpu.HBM)


def call(kernel, out_shape, specs, scratch=(), flops=0, moved=0, limit=24 << 20, outs=None):
    single = not isinstance(out_shape, (list, tuple))
    return pl.pallas_call(
        kernel,
        out_shape=out_shape,
        in_specs=specs,
        out_specs=outs or (VMEM if single else [VMEM] * len(out_shape)),
        scratch_shapes=list(scratch),
        cost_estimate=pl.CostEstimate(flops=flops, bytes_accessed=moved, transcendentals=0),
        compiler_params=pltpu.CompilerParams(vmem_limit_bytes=limit),
        interpret=INTERPRET,
    )


def shape_of(*dims, dtype=BF16):
    return jax.ShapeDtypeStruct(dims, dtype)


def swap_halves(block):
    return jnp.concatenate([block[:, HEAD_DIM:], block[:, :HEAD_DIM]], axis=1)


def parts3(value):
    high = value.astype(BF16)
    rest = value - high.astype(F32)
    middle = rest.astype(BF16)
    low = (rest - middle.astype(F32)).astype(BF16)
    return high, middle, low


def pack_kernel(core_ref, proj_ref, outw_ref, packed_ref):
    for core in range(2):

        @pl.when(core_ref[0] == core)
        def _():
            for head in range(HALF):
                col = (core * HALF + head) * HEAD_DIM
                lanes = slice(head * 128, head * 128 + 128)
                keys = proj_ref[:, INNER + col : INNER + col + HEAD_DIM].astype(F32)
                values = proj_ref[:, 2 * INNER + col : 2 * INNER + col + HEAD_DIM].astype(F32)
                queries = proj_ref[:, col : col + HEAD_DIM].astype(F32)
                packed_ref[0:96, lanes] = jnp.concatenate([keys, values], axis=1).astype(BF16)
                packed_ref[96:144, lanes] = jnp.concatenate(
                    [queries[:48], queries[48:]], axis=1
                ).astype(BF16)
            packed_ref[144:192, :] = outw_ref[:, core * INNER : (core + 1) * INNER]


def pack_weights(core, projection, output_weight):
    return call(pack_kernel, shape_of(192, INNER), [SMEM, VMEM, VMEM])(
        core, projection, output_weight
    )


def fan_kernel(own_ref, other_ref, both_ref):
    for peer in range(DP_X):
        both_ref[peer, 0] = own_ref[...]
        both_ref[peer, 1] = other_ref[...]


def gather_weights(core, projection, output_weight):
    packed = pack_weights(core, projection, output_weight)
    other = lax.ppermute(packed, "yh", [(0, 1), (1, 0)])
    both = call(fan_kernel, shape_of(DP_X, DP_Y, 192, INNER), [VMEM, VMEM])(packed, other)
    got = lax.all_to_all(both, "x", 0, 0, tiled=True)
    return got.reshape(DP_X * DP_Y, 192, INNER)


def norm_kernel(x_ref, gain_ref, out_ref):
    gain = gain_ref[...].reshape(1, D)
    for row in range(0, TOK, 128):
        values = x_ref[row : row + 128, :].astype(F32)
        average = jnp.mean(values, axis=-1, keepdims=True)
        centred = values - average
        variance = jnp.mean(centred * centred, axis=-1, keepdims=True)
        out_ref[row : row + 128, :] = (
            centred * lax.rsqrt(variance + eps_norm) * gain
        ).astype(BF16)


def chosen_rows(view, offset, first, perm_ref):
    rows = lax.broadcasted_iota(jnp.int32, (SPARSE, 1), 0) * RATIO + offset
    if view == 0:
        return rows
    lane = lax.broadcasted_iota(jnp.int32, (SPARSE, TOK), 1)
    tiles = jnp.broadcast_to(perm_ref[...], (SPARSE, TOK))
    return jnp.sum(jnp.where(lane == rows, tiles, 0), axis=1, keepdims=True) - first


def one_hot(index, width):
    token = lax.broadcasted_iota(jnp.int32, (index.shape[0], width), 1)
    return jnp.where(token == index, 1.0, 0.0).astype(BF16)


def project_kernel(
    base_ref, offset_ref, own_x, other_x, packed_ref, own_ref, other_ref,
    kv_out, q_out, send_ref, outw_ref, w_ref, kv_ref, q_ref, sems,
):
    flip = base_ref[3]
    lane = lax.broadcasted_iota(jnp.int32, (48, 128), 1)
    for entry in range(8):
        shard = (entry - entry % 2) + (entry % 2 ^ flip)
        row = pl.multiple_of(shard * 96, 16)
        w_ref[pl.ds(row, 96), 0:INNER] = packed_ref[entry, 0:96, :]
        outw_ref[pl.ds(pl.multiple_of(shard * 48, 16), 48), :] = packed_ref[entry, 144:192, :]
        first, second = [], []
        for head in range(HALF):
            folded = packed_ref[entry, 96:144, head * 128 : head * 128 + 128].astype(F32)
            first.append(folded[:, :HEAD_DIM])
            second.append(folded[:, HEAD_DIM:])
        for at, pieces in ((0, first), (48, second)):
            w_ref[pl.ds(pl.multiple_of(row + at, 16), 48), INNER : INNER + 192] = jnp.concatenate(
                pieces, axis=1
            ).astype(BF16)
    q_lane = lax.broadcasted_iota(jnp.int32, (256, 128), 1)
    copies = []
    for part, x_ref in enumerate((own_x, other_x)):
        for step in range(0, TOK, 256):
            rows = slice(part * TOK + step, part * TOK + step + 256)
            out = jnp.dot(x_ref[step : step + 256, :], w_ref[...], preferred_element_type=F32)
            kv_ref[rows, :] = out[:, :INNER].astype(BF16)
            pair = out[:, INNER : INNER + 128]
            q_ref[rows, 0:128] = jnp.where(q_lane < HEAD_DIM, pair, 0.0).astype(BF16)
            q_ref[rows, 128:256] = jnp.where(q_lane < HEAD_DIM, swap_halves(pair), 0.0).astype(BF16)
            q_ref[rows, 256:384] = jnp.concatenate(
                [out[:, INNER + 128 :], jnp.zeros((256, HEAD_DIM), F32)], axis=1
            ).astype(BF16)
        rows = pl.ds(part * TOK, TOK)
        for at, (here, there) in enumerate(((kv_ref, kv_out), (q_ref, q_out))):
            copies.append(
                pltpu.make_async_copy(here.at[rows], there.at[rows], sems.at[part * 2 + at])
            )
            copies[-1].start()
    for view in range(2):
        for head in range(HALF):
            lanes = slice(head * 128, head * 128 + 128)
            offset = offset_ref[base_ref[0] * HALF + head]
            own = chosen_rows(view, offset, base_ref[1], own_ref)
            other = chosen_rows(view, offset, base_ref[2], other_ref) + TOK
            chosen = one_hot(jnp.concatenate([own, other], axis=0), SEG)
            far_kv = jnp.dot(chosen, kv_ref[:, lanes], preferred_element_type=F32).astype(BF16)
            far_q = jnp.dot(chosen, q_ref[:, lanes], preferred_element_type=F32)
            pair = (view * HALF + head) * 4
            for q_part in range(2):
                row = q_part * 16
                folded = (
                    far_q[row : row + 16] + swap_halves(far_q[SPARSE + row : SPARSE + row + 16])
                ).astype(BF16)
                for k_half in range(2):
                    peer = pair + q_part * 2 + k_half
                    send_ref[peer, 0:32, :] = far_kv[k_half * SPARSE : k_half * SPARSE + 32]
                    send_ref[peer, 32:48, :] = folded
    for peer in range(4 * 2 * HALF, POS):
        send_ref[peer] = jnp.zeros((48, 128), BF16)
    for copy in copies:
        copy.wait()


def near_kernel(q_ref, kv_ref, keep_ref, give_ref):
    keys = kv_ref[...]
    lane = lax.broadcasted_iota(jnp.int32, (SEG, 128), 1)
    values = jnp.where(lane < HEAD_DIM, swap_halves(keys.astype(F32)), 1.0).astype(BF16)
    scores = lax.dot_general(
        q_ref[...], keys, (((1,), (1,)), ((), ())), preferred_element_type=F32
    )
    row_max = jnp.max(scores, axis=1, keepdims=True)
    weights = jnp.exp2((scores - row_max) * EXP_SCALE).astype(BF16)
    summed = jnp.dot(weights, values, preferred_element_type=F32)
    out_lane = lax.broadcasted_iota(jnp.int32, summed.shape, 1)
    result = jnp.where(
        out_lane < HEAD_DIM, summed / swap_halves(summed), row_max * SCALE + jnp.log(summed)
    )

    @pl.when(pl.program_id(1) < 2)
    def _():
        keep_ref[...] = result

    @pl.when(pl.program_id(1) >= 2)
    def _():
        give_ref[...] = result


def near_level(queries, key_pairs):
    tile = 256
    half = shape_of(TOK, HALF * 128, dtype=F32)
    return pl.pallas_call(
        near_kernel,
        out_shape=[half, half],
        grid=(HALF, SEG // tile),
        in_specs=[
            pl.BlockSpec((tile, 128), lambda h, i: (i, h)),
            pl.BlockSpec((SEG, 128), lambda h, i: (0, h)),
        ],
        out_specs=[
            pl.BlockSpec((tile, 128), lambda h, i: (jnp.minimum(i, 1), h)),
            pl.BlockSpec((tile, 128), lambda h, i: (jnp.maximum(i - 2, 0), h)),
        ],
        cost_estimate=pl.CostEstimate(
            flops=4 * HALF * SEG * SEG * 128, bytes_accessed=3 << 20, transcendentals=HALF * SEG * SEG
        ),
        compiler_params=pltpu.CompilerParams(vmem_limit_bytes=LIMITS[1]),
        interpret=INTERPRET,
    )(queries, key_pairs)


def far_kernel(core_ref, got_ref, back_ref):
    core = core_ref[0]
    keys = got_ref[:, 0:32, :].reshape(POS * 32, 128)
    wide = got_ref[:, 32:48, :].reshape(POS * 16, 128).astype(F32)
    lane = lax.broadcasted_iota(jnp.int32, (POS * 32, 128), 1)
    values = jnp.where(lane < HEAD_DIM, swap_halves(keys.astype(F32)), 1.0).astype(BF16)
    q_lane = lax.broadcasted_iota(jnp.int32, (POS * 16, 128), 1)
    q_row = lax.broadcasted_iota(jnp.int32, (POS * 16, 128), 0)
    place = jnp.right_shift(q_lane, 4)
    mine = jnp.bitwise_and(q_lane, 15) == jnp.bitwise_and(q_row, 15)
    source = lax.broadcasted_iota(jnp.int32, (POS, POS * 16), 0)
    member = jnp.right_shift(lax.broadcasted_iota(jnp.int32, (POS, POS * 16), 1), 4)
    spread = jnp.where(source == member, 1.0, 0.0).astype(BF16)
    for part in range(2):
        queries = jnp.where(q_lane < HEAD_DIM, wide if part == 0 else swap_halves(wide), 0.0)
        scores = lax.dot_general(
            queries.astype(BF16), keys, (((1,), (1,)), ((), ())), preferred_element_type=F32
        )
        row_max = jnp.max(scores, axis=1, keepdims=True)
        weights = jnp.exp2((scores - row_max) * EXP_SCALE).astype(BF16)
        summed = jnp.dot(weights, values, preferred_element_type=F32)
        swapped = swap_halves(summed)
        out = (summed / swapped).reshape(POS, 16, 128)
        packed = jnp.concatenate([out[:, 0:8, :HEAD_DIM], out[:, 8:16, :HEAD_DIM]], axis=2)
        high, middle, low = parts3(row_max * SCALE + jnp.log(swapped))
        stats = jnp.where(
            place == 0, high, jnp.where(place == 1, middle, jnp.where(place == 2, low, 0.0))
        )
        stats = jnp.where(mine, stats, 0.0).astype(BF16)
        rows = jnp.dot(spread, stats, preferred_element_type=F32)
        rows = jnp.broadcast_to(rows[:, None, :], (POS, 8, 128))
        block = jnp.concatenate([packed, rows], axis=1).astype(BF16)
        back_ref[:, pl.ds(core if part == 0 else 1 - core, 1)] = block[:, None]


def prepare_kernel(
    base_ref, offset_ref, keep_ref, got_ref, own_ref, gain_ref, own_w, other_w,
    dense_ref, rows_ref, spread_ref, order_ref, weight_ref,
):
    core = base_ref[0]
    width = HALF * HEAD_DIM
    hots = [[], []]
    for group, near_ref in enumerate((keep_ref, got_ref)):
        dense_ref[:, group * width : (group + 1) * width] = jnp.concatenate(
            [near_ref[:, head * 128 : head * 128 + HEAD_DIM] for head in range(HALF)], axis=1
        )
        heads = core if group == 0 else 1 - core
        for head in range(HALF):
            pieces = jnp.concatenate(parts3(near_ref[:, head * 128 : head * 128 + 128]), axis=1)
            offset = offset_ref[heads * HALF + head]
            for view in range(2):
                chosen = one_hot(chosen_rows(view, offset, base_ref[1], own_ref), TOK)
                hots[view].append(chosen)
                taken = jnp.dot(chosen, pieces, preferred_element_type=F32)
                at = group * 192 + (view * HALF + head) * SPARSE
                rows_ref[at : at + SPARSE, :] = taken[:, :128] + taken[:, 128:256] + taken[:, 256:]
    for view in range(2):
        spread_ref[view] = jnp.concatenate(hots[view], axis=0).astype(F32).T.astype(BF16)
    gain = gain_ref[...].reshape(1, INNER)
    order_ref[...] = jnp.where(
        core == 0, gain, jnp.concatenate([gain[:, width:], gain[:, :width]], axis=1)
    )
    own_rows = pl.ds(pl.multiple_of(core * width, 64), width)
    other_rows = pl.ds(pl.multiple_of((1 - core) * width, 64), width)
    for part, place in ((own_w, core), (other_w, 1 - core)):
        cols = pl.ds(pl.multiple_of(place * INNER, 128), INNER)
        weight_ref[0:width, cols] = part[own_rows, :]
        weight_ref[width:INNER, cols] = part[other_rows, :]


def output_kernel(
    core_ref, far_ref, dense_ref, rows_ref, spread_ref, gain_ref, weight_ref, plain_ref, flip_ref
):
    core = core_ref[0]
    lane = lax.broadcasted_iota(jnp.int32, (192, 128), 1)
    mine = jnp.bitwise_and(lane, 15) == jnp.bitwise_and(
        lax.broadcasted_iota(jnp.int32, (192, 128), 0), 15
    )
    deltas = []
    for group in range(2):
        outs, logs = [], []
        for k_half in range(2):
            blocks, stats = [], []
            for pair in range(2 * HALF):
                for q_part in range(2):
                    peer = (pair * 4 + q_part * 2 + k_half) * 2
                    block = far_ref[peer + (core if group == 0 else 1 - core)].astype(F32)
                    blocks += [block[0:8, :HEAD_DIM], block[0:8, HEAD_DIM:]]
                    stats += [block[8:16], block[8:16]]
            outs.append(jnp.concatenate(blocks, axis=0))
            found = jnp.where(mine, jnp.concatenate(stats, axis=0), 0.0)
            logs.append(jnp.sum(found, axis=1, keepdims=True))
        top = jnp.maximum(logs[0], logs[1])
        weight0, weight1 = jnp.exp(logs[0] - top), jnp.exp(logs[1] - top)
        joint = weight0 + weight1
        far = (weight0 * outs[0] + weight1 * outs[1]) / joint
        near = rows_ref[group * 192 : group * 192 + 192, :]
        gap = near[:, HEAD_DIM : HEAD_DIM + 1] - (top + jnp.log(joint))
        deltas.append((far - near[:, :HEAD_DIM]) / (1.0 + jnp.exp(gap)))
    row = jnp.right_shift(lax.broadcasted_iota(jnp.int32, (192, INNER), 0), 5)
    col = jnp.right_shift(lax.broadcasted_iota(jnp.int32, (192, INNER), 1), 6)
    for view, out_ref in enumerate((plain_ref, flip_ref)):
        delta = jnp.concatenate([d[view * 96 : view * 96 + 96] for d in deltas], axis=0)
        blocks = jnp.where(row == col, jnp.concatenate([delta] * HEADS, axis=1), 0.0).astype(BF16)
        for at in range(0, TOK, 256):
            attended = dense_ref[at : at + 256, :] + jnp.dot(
                spread_ref[view, at : at + 256, :], blocks, preferred_element_type=F32
            )
            average = jnp.mean(attended, axis=-1, keepdims=True)
            centred = attended - average
            variance = jnp.mean(centred * centred, axis=-1, keepdims=True)
            mixed = (centred * lax.rsqrt(variance + eps_norm) * gain_ref[...]).astype(BF16)
            out_ref[at : at + 256, :] = jnp.dot(
                mixed, weight_ref[...], preferred_element_type=F32
            ).astype(BF16)


def core_swap(block):
    return lax.ppermute(block, "core", [(0, 1), (1, 0)])


def layer(
    tile_features, flip_perm, head_offsets, input_gain, projection, output_gain, output_weight
):
    core = lax.axis_index("core").astype(jnp.int32)
    pos = lax.axis_index("pos").astype(jnp.int32)
    rank = pos * 2 + core
    core_id = core[None]
    base = jnp.stack([core, rank * TOK, (rank ^ 1) * TOK, lax.axis_index("yh").astype(jnp.int32)])

    packed = gather_weights(core_id, projection, output_weight)
    own_x = call(norm_kernel, shape_of(TOK, D), [VMEM, VMEM], moved=2 << 20)(
        tile_features[0], input_gain
    )
    other_x = core_swap(own_x)
    last = 2 * POS - 1
    ctx = ("pos", "core")
    own_perm = lax.ppermute(flip_perm, ctx, [(last - r, r) for r in range(2 * POS)])
    other_perm = lax.ppermute(flip_perm, ctx, [(last - (r ^ 1), r) for r in range(2 * POS)])

    key_pairs, queries, send, own_w = call(
        project_kernel,
        [
            shape_of(SEG, INNER),
            shape_of(SEG, INNER),
            shape_of(POS, 48, 128),
            shape_of(INNER, INNER),
        ],
        [SMEM, SMEM, VMEM, VMEM, VMEM, VMEM, VMEM],
        [
            pltpu.VMEM((D, INNER + 192), BF16),
            pltpu.VMEM((SEG, INNER), BF16),
            pltpu.VMEM((SEG, INNER), BF16),
            pltpu.SemaphoreType.DMA((4,)),
        ],
        outs=[HBM, HBM, VMEM, VMEM],
        flops=2 * SEG * D * 576,
        moved=4 << 20,
        limit=LIMITS[0],
    )(base, head_offsets, own_x, other_x, packed, own_perm, other_perm)

    got = lax.all_to_all(send, "pos", 0, 0, tiled=True)
    keep, give = near_level(queries, key_pairs)
    near_got = core_swap(give)
    back = call(
        far_kernel, shape_of(POS, 2, 16, 128), [SMEM, VMEM], flops=4 * SEG * SEG * 128, moved=1 << 20,
        limit=LIMITS[2],
    )(core_id, got)
    far = lax.all_to_all(back.reshape(2 * POS, 16, 128), ctx, 0, 0, tiled=True)

    other_w = core_swap(own_w)
    prepared = call(
        prepare_kernel,
        [
            shape_of(TOK, INNER, dtype=F32),
            shape_of(INNER, 128, dtype=F32),
            shape_of(2, TOK, 192),
            shape_of(1, INNER, dtype=F32),
            shape_of(INNER, D),
        ],
        [SMEM, SMEM, VMEM, VMEM, VMEM, VMEM, VMEM, VMEM],
        flops=1 << 28,
        moved=4 << 20,
        limit=LIMITS[3],
    )(base, head_offsets, keep, near_got, own_perm, output_gain, own_w, other_w)

    plain_view, flipped_view = call(
        output_kernel,
        [shape_of(TOK, D), shape_of(TOK, D)],
        [SMEM, VMEM, VMEM, VMEM, VMEM, VMEM, VMEM],
        flops=4 * SEG * INNER * D,
        moved=4 << 20,
        limit=LIMITS[4],
    )(core_id, far, *prepared)
    return (plain_view[None], flipped_view[None])


def solution(mesh):
    fine = Mesh(mesh.devices.reshape(DP_X, DP_Y, POS, 2), ("x", "yh", "pos", "core"))
    dp, ctx = ("x", "yh"), ("pos", "core")
    placed = (P(dp, ctx, None), P(dp, ctx), P(), P(), P(dp, None), P(), P(dp, None))
    return jax.shard_map(
        layer,
        mesh=fine,
        in_specs=placed,
        out_specs=(P(dp, ctx, None), P(dp, ctx, None)),
        check_vma=False,
    )
```

```python
import jax
import jax.numpy as jnp
from jax import lax
from jax.experimental import pallas as pl
from jax.experimental.pallas import tpu as pltpu
from jax.sharding import Mesh, PartitionSpec as P


HEADS = 6
HEAD_DIM = 64
INNER = 384
D = 768
RATIO = 16
TOK = 512
SEG = 1024
HALF = 3
SPARSE = TOK // RATIO
POS = 32
DP_X, DP_Y = 4, 2
INTERPRET = False
NEAR_TILE = 256
LIMITS = [60 * 1024 * 1024, 60 * 1024 * 1024, 24 << 20, 24 << 20, 24 << 20]

eps_norm = 1e-05
EXP_SCALE = HEAD_DIM ** (-0.5) * 1.4426950408889634
SCALE = HEAD_DIM ** (-0.5)

F32 = jnp.float32
BF16 = jnp.bfloat16
VMEM = pl.BlockSpec(memory_space=pltpu.VMEM)
SMEM = pl.BlockSpec(memory_space=pltpu.SMEM)
HBM = pl.BlockSpec(memory_space=pltpu.HBM)


def call(kernel, out_shape, specs, scratch=(), flops=0, moved=0, limit=24 << 20, outs=None):
    single = not isinstance(out_shape, (list, tuple))
    return pl.pallas_call(
        kernel,
        out_shape=out_shape,
        in_specs=specs,
        out_specs=outs or (VMEM if single else [VMEM] * len(out_shape)),
        scratch_shapes=list(scratch),
        cost_estimate=pl.CostEstimate(flops=flops, bytes_accessed=moved, transcendentals=0),
        compiler_params=pltpu.CompilerParams(vmem_limit_bytes=limit),
        interpret=INTERPRET,
    )


def shape_of(*dims, dtype=BF16):
    return jax.ShapeDtypeStruct(dims, dtype)


def swap_halves(block):
    return jnp.concatenate([block[:, HEAD_DIM:], block[:, :HEAD_DIM]], axis=1)


def parts3(value):
    high = value.astype(BF16)
    rest = value - high.astype(F32)
    middle = rest.astype(BF16)
    low = (rest - middle.astype(F32)).astype(BF16)
    return high, middle, low


def pack_kernel(core_ref, proj_ref, outw_ref, packed_ref):
    for core in range(2):

        @pl.when(core_ref[0] == core)
        def _():
            for head in range(HALF):
                col = (core * HALF + head) * HEAD_DIM
                lanes = slice(head * 128, head * 128 + 128)
                keys = proj_ref[:, INNER + col : INNER + col + HEAD_DIM].astype(F32)
                values = proj_ref[:, 2 * INNER + col : 2 * INNER + col + HEAD_DIM].astype(F32)
                queries = proj_ref[:, col : col + HEAD_DIM].astype(F32)
                packed_ref[0:96, lanes] = jnp.concatenate([keys, values], axis=1).astype(BF16)
                packed_ref[96:144, lanes] = jnp.concatenate(
                    [queries[:48], queries[48:]], axis=1
                ).astype(BF16)
            packed_ref[144:192, :] = outw_ref[:, core * INNER : (core + 1) * INNER]


def pack_weights(core, projection, output_weight):
    return call(pack_kernel, shape_of(192, INNER), [SMEM, VMEM, VMEM], limit=60 * 1024 * 1024)(
        core, projection, output_weight
    )


def fan_kernel(own_ref, other_ref, both_ref):
    for peer in range(DP_X):
        both_ref[peer, 0] = own_ref[...]
        both_ref[peer, 1] = other_ref[...]


def gather_weights(core, projection, output_weight):
    packed = pack_weights(core, projection, output_weight)
    other = lax.ppermute(packed, "yh", [(0, 1), (1, 0)])
    both = call(fan_kernel, shape_of(DP_X, DP_Y, 192, INNER), [VMEM, VMEM])(packed, other)
    got = lax.all_to_all(both, "x", 0, 0, tiled=True)
    return got.reshape(DP_X * DP_Y, 192, INNER)


def norm_kernel(base_ref, x_ref, gain_ref, perm_ref, out_ref, order_ref):
    gain = gain_ref[...].reshape(1, D)
    for row in range(0, TOK, 128):
        values = x_ref[row : row + 128, :].astype(F32)
        average = jnp.mean(values, axis=-1, keepdims=True)
        centred = values - average
        variance = jnp.mean(centred * centred, axis=-1, keepdims=True)
        out_ref[row : row + 128, :] = (
            centred * lax.rsqrt(variance + eps_norm) * gain
        ).astype(BF16)
    order_ref[...] = (perm_ref[...] - base_ref[1]).astype(F32)
    local = jnp.broadcast_to(perm_ref[...] - base_ref[1], (16, TOK))
    row = lax.broadcasted_iota(jnp.int32, (16, TOK), 0)
    parts = jnp.where(row == 0, jnp.right_shift(local, 4), jnp.bitwise_and(local, 15))
    out_ref[TOK : TOK + 16, 0:TOK] = parts.astype(F32).astype(BF16)
    out_ref[TOK : TOK + 16, TOK:] = jnp.zeros((16, D - TOK), BF16)


def order_of(x_ref):
    parts = x_ref[TOK : TOK + 16, 0:TOK].astype(F32)
    return parts[0:1, :] * 16.0 + parts[1:2, :]


def chosen_rows(view, offset, order):
    rows = lax.broadcasted_iota(jnp.int32, (SPARSE, 1), 0) * RATIO + offset
    if view == 0:
        return rows
    lane = lax.broadcasted_iota(jnp.int32, (SPARSE, TOK), 1)
    tiles = jnp.broadcast_to(order, (SPARSE, TOK))
    picked = jnp.sum(jnp.where(lane == rows, tiles, 0.0), axis=1, keepdims=True)
    return picked.astype(jnp.int32)


def one_hot(index, width):
    token = lax.broadcasted_iota(jnp.int32, (index.shape[0], width), 1)
    return jnp.where(token == index, 1.0, 0.0).astype(BF16)


def project_kernel(
    base_ref, offset_ref, own_x, other_x, packed_ref,
    kv_out, q_out, send_ref, outw_ref, w_ref, kv_ref, q_ref, sems,
):
    flip = base_ref[3]
    lane = lax.broadcasted_iota(jnp.int32, (48, 128), 1)
    for entry in range(8):
        shard = (entry - entry % 2) + (entry % 2 ^ flip)
        row = pl.multiple_of(shard * 96, 16)
        w_ref[pl.ds(row, 96), 0:INNER] = packed_ref[entry, 0:96, :]
        outw_ref[pl.ds(pl.multiple_of(shard * 48, 16), 48), :] = packed_ref[entry, 144:192, :]
        first, second = [], []
        for head in range(HALF):
            folded = packed_ref[entry, 96:144, head * 128 : head * 128 + 128].astype(F32)
            first.append(folded[:, :HEAD_DIM])
            second.append(folded[:, HEAD_DIM:])
        for at, pieces in ((0, first), (48, second)):
            w_ref[pl.ds(pl.multiple_of(row + at, 16), 48), INNER : INNER + 192] = jnp.concatenate(
                pieces, axis=1
            ).astype(BF16)
    q_lane = lax.broadcasted_iota(jnp.int32, (256, 128), 1)
    copies = []
    for part, x_ref in enumerate((own_x, other_x)):
        for step in range(0, TOK, 256):
            rows = slice(part * TOK + step, part * TOK + step + 256)
            out = jnp.dot(x_ref[step : step + 256, :], w_ref[...], preferred_element_type=F32)
            kv_ref[rows, :] = out[:, :INNER].astype(BF16)
            pair = out[:, INNER : INNER + 128]
            q_ref[rows, 0:128] = jnp.where(q_lane < HEAD_DIM, pair, 0.0).astype(BF16)
            q_ref[rows, 128:256] = jnp.where(q_lane < HEAD_DIM, swap_halves(pair), 0.0).astype(BF16)
            q_ref[rows, 256:384] = jnp.concatenate(
                [out[:, INNER + 128 :], jnp.zeros((256, HEAD_DIM), F32)], axis=1
            ).astype(BF16)
        rows = pl.ds(part * TOK, TOK)
        for at, (here, there) in enumerate(((kv_ref, kv_out), (q_ref, q_out))):
            copies.append(
                pltpu.make_async_copy(here.at[rows], there.at[rows], sems.at[part * 2 + at])
            )
            copies[-1].start()
    own_order, other_order = order_of(own_x), order_of(other_x)
    for view in range(2):
        for head in range(HALF):
            lanes = slice(head * 128, head * 128 + 128)
            offset = offset_ref[base_ref[0] * HALF + head]
            own = chosen_rows(view, offset, own_order)
            other = chosen_rows(view, offset, other_order) + TOK
            chosen = one_hot(jnp.concatenate([own, other], axis=0), SEG)
            far_kv = jnp.dot(chosen, kv_ref[:, lanes], preferred_element_type=F32).astype(BF16)
            far_q = jnp.dot(chosen, q_ref[:, lanes], preferred_element_type=F32)
            pair = (view * HALF + head) * 4
            for q_part in range(2):
                row = q_part * 16
                folded = (
                    far_q[row : row + 16] + swap_halves(far_q[SPARSE + row : SPARSE + row + 16])
                ).astype(BF16)
                for k_half in range(2):
                    peer = pair + q_part * 2 + k_half
                    send_ref[peer, 0:32, :] = far_kv[k_half * SPARSE : k_half * SPARSE + 32]
                    send_ref[peer, 32:48, :] = folded
    for peer in range(4 * 2 * HALF, POS):
        send_ref[peer] = jnp.zeros((48, 128), BF16)
    for copy in copies:
        copy.wait()


def near_kernel(q_ref, kv_ref, keep_ref, give_ref):
    keys = kv_ref[...]
    lane = lax.broadcasted_iota(jnp.int32, (SEG, 128), 1)
    values = jnp.where(lane < HEAD_DIM, swap_halves(keys.astype(F32)), 1.0).astype(BF16)
    tile = NEAR_TILE
    out_lane = lax.broadcasted_iota(jnp.int32, (tile, 128), 1)
    for at in range(0, SEG, tile):
        scores = lax.dot_general(
            q_ref[at : at + tile, :], keys, (((1,), (1,)), ((), ())), preferred_element_type=F32
        )
        row_max = jnp.max(scores, axis=1, keepdims=True)
        weights = jnp.exp2((scores - row_max) * EXP_SCALE).astype(BF16)
        summed = jnp.dot(weights, values, preferred_element_type=F32)
        result = jnp.where(
            out_lane < HEAD_DIM, summed / swap_halves(summed), row_max * SCALE + jnp.log(summed)
        )
        out_ref = keep_ref if at < TOK else give_ref
        out_ref[at % TOK : at % TOK + tile, :] = result


def near_level(queries, key_pairs):
    half = shape_of(TOK, HALF * 128, dtype=F32)
    whole = pl.BlockSpec((SEG, 128), lambda h: (0, h))
    part = pl.BlockSpec((TOK, 128), lambda h: (0, h))
    return pl.pallas_call(
        near_kernel,
        out_shape=[half, half],
        grid=(HALF,),
        in_specs=[whole, whole],
        out_specs=[part, part],
        cost_estimate=pl.CostEstimate(
            flops=4 * HALF * SEG * SEG * 128, bytes_accessed=3 << 20, transcendentals=HALF * SEG * SEG
        ),
        compiler_params=pltpu.CompilerParams(vmem_limit_bytes=LIMITS[1]),
        interpret=INTERPRET,
    )(queries, key_pairs)


def far_kernel(core_ref, got_ref, back_ref):
    core = core_ref[0]
    keys = got_ref[:, 0:32, :].reshape(POS * 32, 128)
    wide = got_ref[:, 32:48, :].reshape(POS * 16, 128).astype(F32)
    lane = lax.broadcasted_iota(jnp.int32, (POS * 32, 128), 1)
    values = jnp.where(lane < HEAD_DIM, swap_halves(keys.astype(F32)), 1.0).astype(BF16)
    q_lane = lax.broadcasted_iota(jnp.int32, (POS * 16, 128), 1)
    q_row = lax.broadcasted_iota(jnp.int32, (POS * 16, 128), 0)
    place = jnp.right_shift(q_lane, 4)
    mine = jnp.bitwise_and(q_lane, 15) == jnp.bitwise_and(q_row, 15)
    source = lax.broadcasted_iota(jnp.int32, (POS, POS * 16), 0)
    member = jnp.right_shift(lax.broadcasted_iota(jnp.int32, (POS, POS * 16), 1), 4)
    spread = jnp.where(source == member, 1.0, 0.0).astype(BF16)
    for part in range(2):
        queries = jnp.where(q_lane < HEAD_DIM, wide if part == 0 else swap_halves(wide), 0.0)
        scores = lax.dot_general(
            queries.astype(BF16), keys, (((1,), (1,)), ((), ())), preferred_element_type=F32
        )
        row_max = jnp.max(scores, axis=1, keepdims=True)
        weights = jnp.exp2((scores - row_max) * EXP_SCALE).astype(BF16)
        summed = jnp.dot(weights, values, preferred_element_type=F32)
        swapped = swap_halves(summed)
        out = (summed / swapped).reshape(POS, 16, 128)
        packed = jnp.concatenate([out[:, 0:8, :HEAD_DIM], out[:, 8:16, :HEAD_DIM]], axis=2)
        high, middle, low = parts3(row_max * SCALE + jnp.log(swapped))
        stats = jnp.where(
            place == 0, high, jnp.where(place == 1, middle, jnp.where(place == 2, low, 0.0))
        )
        stats = jnp.where(mine, stats, 0.0).astype(BF16)
        rows = jnp.dot(spread, stats, preferred_element_type=F32)
        rows = jnp.broadcast_to(rows[:, None, :], (POS, 8, 128))
        block = jnp.concatenate([packed, rows], axis=1).astype(BF16)
        back_ref[:, pl.ds(core if part == 0 else 1 - core, 1)] = block[:, None]


def prepare_kernel(
    base_ref, offset_ref, keep_ref, got_ref, order_ref, gain_ref, own_w, other_w,
    dense_ref, rows_ref, spread_ref, scale_ref, weight_ref,
):
    core = base_ref[0]
    width = HALF * HEAD_DIM
    hots = [[], []]
    order = order_ref[...]
    for group, near_ref in enumerate((keep_ref, got_ref)):
        dense_ref[:, group * width : (group + 1) * width] = jnp.concatenate(
            [near_ref[:, head * 128 : head * 128 + HEAD_DIM] for head in range(HALF)], axis=1
        )
        heads = core if group == 0 else 1 - core
        for head in range(HALF):
            pieces = jnp.concatenate(parts3(near_ref[:, head * 128 : head * 128 + 128]), axis=1)
            offset = offset_ref[heads * HALF + head]
            for view in range(2):
                chosen = one_hot(chosen_rows(view, offset, order), TOK)
                hots[view].append(chosen)
                taken = jnp.dot(chosen, pieces, preferred_element_type=F32)
                at = group * 192 + (view * HALF + head) * SPARSE
                rows_ref[at : at + SPARSE, :] = taken[:, :128] + taken[:, 128:256] + taken[:, 256:]
    for view in range(2):
        spread_ref[view] = jnp.concatenate(hots[view], axis=0).astype(F32).T.astype(BF16)
    gain = gain_ref[...].reshape(1, INNER)
    scale_ref[...] = jnp.where(
        core == 0, gain, jnp.concatenate([gain[:, width:], gain[:, :width]], axis=1)
    )
    own_rows = pl.ds(pl.multiple_of(core * width, 64), width)
    other_rows = pl.ds(pl.multiple_of((1 - core) * width, 64), width)
    for part, place in ((own_w, core), (other_w, 1 - core)):
        cols = pl.ds(pl.multiple_of(place * INNER, 128), INNER)
        weight_ref[0:width, cols] = part[own_rows, :]
        weight_ref[width:INNER, cols] = part[other_rows, :]


def output_kernel(
    core_ref, far_ref, dense_ref, rows_ref, spread_ref, gain_ref, weight_ref, plain_ref, flip_ref
):
    core = core_ref[0]
    lane = lax.broadcasted_iota(jnp.int32, (192, 128), 1)
    mine = jnp.bitwise_and(lane, 15) == jnp.bitwise_and(
        lax.broadcasted_iota(jnp.int32, (192, 128), 0), 15
    )
    deltas = []
    for group in range(2):
        outs, logs = [], []
        for k_half in range(2):
            blocks, stats = [], []
            for pair in range(2 * HALF):
                for q_part in range(2):
                    peer = (pair * 4 + q_part * 2 + k_half) * 2
                    block = far_ref[peer + (core if group == 0 else 1 - core)].astype(F32)
                    blocks += [block[0:8, :HEAD_DIM], block[0:8, HEAD_DIM:]]
                    stats += [block[8:16], block[8:16]]
            outs.append(jnp.concatenate(blocks, axis=0))
            found = jnp.where(mine, jnp.concatenate(stats, axis=0), 0.0)
            logs.append(jnp.sum(found, axis=1, keepdims=True))
        top = jnp.maximum(logs[0], logs[1])
        weight0, weight1 = jnp.exp(logs[0] - top), jnp.exp(logs[1] - top)
        joint = weight0 + weight1
        far = (weight0 * outs[0] + weight1 * outs[1]) / joint
        near = rows_ref[group * 192 : group * 192 + 192, :]
        gap = near[:, HEAD_DIM : HEAD_DIM + 1] - (top + jnp.log(joint))
        deltas.append((far - near[:, :HEAD_DIM]) / (1.0 + jnp.exp(gap)))
    row = jnp.right_shift(lax.broadcasted_iota(jnp.int32, (192, INNER), 0), 5)
    col = jnp.right_shift(lax.broadcasted_iota(jnp.int32, (192, INNER), 1), 6)
    for view, out_ref in enumerate((plain_ref, flip_ref)):
        delta = jnp.concatenate([d[view * 96 : view * 96 + 96] for d in deltas], axis=0)
        blocks = jnp.where(row == col, jnp.concatenate([delta] * HEADS, axis=1), 0.0).astype(BF16)
        for at in range(0, TOK, 256):
            attended = dense_ref[at : at + 256, :] + jnp.dot(
                spread_ref[view, at : at + 256, :], blocks, preferred_element_type=F32
            )
            average = jnp.mean(attended, axis=-1, keepdims=True)
            centred = attended - average
            variance = jnp.mean(centred * centred, axis=-1, keepdims=True)
            mixed = (centred * lax.rsqrt(variance + eps_norm) * gain_ref[...]).astype(BF16)
            out_ref[at : at + 256, :] = jnp.dot(
                mixed, weight_ref[...], preferred_element_type=F32
            ).astype(BF16)


def core_swap(block):
    return lax.ppermute(block, "core", [(0, 1), (1, 0)])


def layer(
    tile_features, flip_perm, head_offsets, input_gain, projection, output_gain, output_weight
):
    core = lax.axis_index("core").astype(jnp.int32)
    pos = lax.axis_index("pos").astype(jnp.int32)
    rank = pos * 2 + core
    core_id = core[None]
    base = jnp.stack([core, rank * TOK, (rank ^ 1) * TOK, lax.axis_index("yh").astype(jnp.int32)])

    packed = gather_weights(core_id, projection, output_weight)
    last = 2 * POS - 1
    ctx = ("pos", "core")
    own_perm = lax.ppermute(flip_perm, ctx, [(last - r, r) for r in range(2 * POS)])
    own_x, own_order = call(
        norm_kernel,
        [shape_of(TOK + 16, D), shape_of(1, TOK, dtype=F32)],
        [SMEM, VMEM, VMEM, VMEM],
        moved=2 << 20,
    )(base, tile_features[0], input_gain, own_perm)
    other_x = core_swap(own_x)

    key_pairs, queries, send, own_w = call(
        project_kernel,
        [
            shape_of(SEG, INNER),
            shape_of(SEG, INNER),
            shape_of(POS, 48, 128),
            shape_of(INNER, INNER),
        ],
        [SMEM, SMEM, VMEM, VMEM, VMEM],
        [
            pltpu.VMEM((D, INNER + 192), BF16),
            pltpu.VMEM((SEG, INNER), BF16),
            pltpu.VMEM((SEG, INNER), BF16),
            pltpu.SemaphoreType.DMA((4,)),
        ],
        outs=[HBM, HBM, VMEM, VMEM],
        flops=2 * SEG * D * 576,
        moved=4 << 20,
        limit=LIMITS[0],
    )(base, head_offsets, own_x, other_x, packed)

    got = lax.all_to_all(send, "pos", 0, 0, tiled=True)
    keep, give = near_level(queries, key_pairs)
    near_got = core_swap(give)
    back = call(
        far_kernel, shape_of(POS, 2, 16, 128), [SMEM, VMEM], flops=4 * SEG * SEG * 128, moved=1 << 20,
        limit=LIMITS[2],
    )(core_id, got)
    far = lax.all_to_all(back.reshape(2 * POS, 16, 128), ctx, 0, 0, tiled=True)

    other_w = core_swap(own_w)
    prepared = call(
        prepare_kernel,
        [
            shape_of(TOK, INNER, dtype=F32),
            shape_of(INNER, 128, dtype=F32),
            shape_of(2, TOK, 192),
            shape_of(1, INNER, dtype=F32),
            shape_of(INNER, D),
        ],
        [SMEM, SMEM, VMEM, VMEM, VMEM, VMEM, VMEM, VMEM],
        flops=1 << 28,
        moved=4 << 20,
        limit=LIMITS[3],
    )(base, head_offsets, keep, near_got, own_order, output_gain, own_w, other_w)

    plain_view, flipped_view = call(
        output_kernel,
        [shape_of(TOK, D), shape_of(TOK, D)],
        [SMEM, VMEM, VMEM, VMEM, VMEM, VMEM, VMEM],
        flops=4 * SEG * INNER * D,
        moved=4 << 20,
        limit=LIMITS[4],
    )(core_id, far, *prepared)
    return (plain_view[None], flipped_view[None])


def solution(mesh):
    fine = Mesh(mesh.devices.reshape(DP_X, DP_Y, POS, 2), ("x", "yh", "pos", "core"))
    dp, ctx = ("x", "yh"), ("pos", "core")
    placed = (P(dp, ctx, None), P(dp, ctx), P(), P(), P(dp, None), P(), P(dp, None))
    return jax.shard_map(
        layer,
        mesh=fine,
        in_specs=placed,
        out_specs=(P(dp, ctx, None), P(dp, ctx, None)),
        check_vma=False,
    )
```

```python
import jax
import jax.numpy as jnp
from jax import lax
from jax.experimental import pallas as pl
from jax.experimental.pallas import tpu as pltpu
from jax.sharding import Mesh, PartitionSpec as P


HEADS = 6
HEAD_DIM = 64
INNER = 384
D = 768
RATIO = 16
TOK = 512
SEG = 1024
HALF = 3
SPARSE = TOK // RATIO
POS = 32
DP_X, DP_Y = 4, 2
INTERPRET = False
NEAR_TILE = 256
LIMITS = [60 * 1024 * 1024, 60 * 1024 * 1024, 24 << 20, 24 << 20, 24 << 20]

eps_norm = 1e-05
EXP_SCALE = HEAD_DIM ** (-0.5) * 1.4426950408889634
SCALE = HEAD_DIM ** (-0.5)

F32 = jnp.float32
BF16 = jnp.bfloat16
VMEM = pl.BlockSpec(memory_space=pltpu.VMEM)
SMEM = pl.BlockSpec(memory_space=pltpu.SMEM)
HBM = pl.BlockSpec(memory_space=pltpu.HBM)


def call(kernel, out_shape, specs, scratch=(), flops=0, moved=0, limit=24 << 20, outs=None):
    single = not isinstance(out_shape, (list, tuple))
    return pl.pallas_call(
        kernel,
        out_shape=out_shape,
        in_specs=specs,
        out_specs=outs or (VMEM if single else [VMEM] * len(out_shape)),
        scratch_shapes=list(scratch),
        cost_estimate=pl.CostEstimate(flops=flops, bytes_accessed=moved, transcendentals=0),
        compiler_params=pltpu.CompilerParams(vmem_limit_bytes=limit),
        interpret=INTERPRET,
    )


def shape_of(*dims, dtype=BF16):
    return jax.ShapeDtypeStruct(dims, dtype)


def swap_halves(block):
    return jnp.concatenate([block[:, HEAD_DIM:], block[:, :HEAD_DIM]], axis=1)


def parts3(value):
    high = value.astype(BF16)
    rest = value - high.astype(F32)
    middle = rest.astype(BF16)
    low = (rest - middle.astype(F32)).astype(BF16)
    return high, middle, low


def pack_kernel(core_ref, proj_ref, outw_ref, packed_ref):
    for core in range(2):

        @pl.when(core_ref[0] == core)
        def _():
            for head in range(HALF):
                col = (core * HALF + head) * HEAD_DIM
                lanes = slice(head * 128, head * 128 + 128)
                keys = proj_ref[:, INNER + col : INNER + col + HEAD_DIM].astype(F32)
                values = proj_ref[:, 2 * INNER + col : 2 * INNER + col + HEAD_DIM].astype(F32)
                queries = proj_ref[:, col : col + HEAD_DIM].astype(F32)
                packed_ref[0:96, lanes] = jnp.concatenate([keys, values], axis=1).astype(BF16)
                packed_ref[96:144, lanes] = jnp.concatenate(
                    [queries[:48], queries[48:]], axis=1
                ).astype(BF16)
            packed_ref[144:192, :] = outw_ref[:, core * INNER : (core + 1) * INNER]


def pack_weights(core, projection, output_weight):
    return call(pack_kernel, shape_of(192, INNER), [SMEM, VMEM, VMEM], limit=60 * 1024 * 1024)(
        core, projection, output_weight
    )


def fan_kernel(own_ref, other_ref, both_ref):
    for peer in range(DP_X):
        both_ref[peer, 0] = own_ref[...]
        both_ref[peer, 1] = other_ref[...]


def gather_weights(core, projection, output_weight):
    packed = pack_weights(core, projection, output_weight)
    other = lax.ppermute(packed, "yh", [(0, 1), (1, 0)])
    both = call(fan_kernel, shape_of(DP_X, DP_Y, 192, INNER), [VMEM, VMEM])(packed, other)
    got = lax.all_to_all(both, "x", 0, 0, tiled=True)
    return got.reshape(DP_X * DP_Y, 192, INNER)


def norm_kernel(base_ref, x_ref, gain_ref, perm_ref, out_ref, order_ref):
    gain = gain_ref[...].reshape(1, D)
    for row in range(0, TOK, 128):
        values = x_ref[row : row + 128, :].astype(F32)
        average = jnp.mean(values, axis=-1, keepdims=True)
        centred = values - average
        variance = jnp.mean(centred * centred, axis=-1, keepdims=True)
        out_ref[row : row + 128, :] = (
            centred * lax.rsqrt(variance + eps_norm) * gain
        ).astype(BF16)
    order_ref[...] = (perm_ref[...] - base_ref[1]).astype(F32)
    local = jnp.broadcast_to(perm_ref[...] - base_ref[1], (16, TOK))
    row = lax.broadcasted_iota(jnp.int32, (16, TOK), 0)
    parts = jnp.where(row == 0, jnp.right_shift(local, 4), jnp.bitwise_and(local, 15))
    out_ref[TOK : TOK + 16, 0:TOK] = parts.astype(F32).astype(BF16)
    out_ref[TOK : TOK + 16, TOK:] = jnp.zeros((16, D - TOK), BF16)


def order_of(x_ref):
    parts = x_ref[TOK : TOK + 16, 0:TOK].astype(F32)
    return parts[0:1, :] * 16.0 + parts[1:2, :]


def chosen_rows(view, offset, order):
    rows = lax.broadcasted_iota(jnp.int32, (SPARSE, 1), 0) * RATIO + offset
    if view == 0:
        return rows
    lane = lax.broadcasted_iota(jnp.int32, (SPARSE, TOK), 1)
    tiles = jnp.broadcast_to(order, (SPARSE, TOK))
    picked = jnp.sum(jnp.where(lane == rows, tiles, 0.0), axis=1, keepdims=True)
    return picked.astype(jnp.int32)


def one_hot(index, width):
    token = lax.broadcasted_iota(jnp.int32, (index.shape[0], width), 1)
    return jnp.where(token == index, 1.0, 0.0).astype(BF16)


def project_kernel(
    base_ref, offset_ref, own_x, other_x, packed_ref,
    all_out, send_ref, outw_ref, w_ref, all_ref, sems,
):
    flip = base_ref[3]
    lane = lax.broadcasted_iota(jnp.int32, (48, 128), 1)
    for entry in range(8):
        shard = (entry - entry % 2) + (entry % 2 ^ flip)
        row = pl.multiple_of(shard * 96, 16)
        for head in range(HALF):
            at = head * 256
            w_ref[pl.ds(row, 96), at : at + 128] = packed_ref[
                entry, 0:96, head * 128 : head * 128 + 128
            ]
            folded = packed_ref[entry, 96:144, head * 128 : head * 128 + 128].astype(F32)
            for first, part in ((0, folded), (48, swap_halves(folded))):
                w_ref[pl.ds(pl.multiple_of(row + first, 16), 48), at + 128 : at + 256] = jnp.where(
                    lane < HEAD_DIM, part, 0.0
                ).astype(BF16)
        outw_ref[pl.ds(pl.multiple_of(shard * 48, 16), 48), :] = packed_ref[entry, 144:192, :]
    copies = []
    for part, x_ref in enumerate((own_x, other_x)):
        for step in range(0, TOK, 256):
            at = part * TOK + step
            all_ref[at : at + 256, :] = jnp.dot(
                x_ref[step : step + 256, :], w_ref[...], preferred_element_type=F32
            ).astype(BF16)
        rows = pl.ds(part * TOK, TOK)
        copies.append(pltpu.make_async_copy(all_ref.at[rows], all_out.at[rows], sems.at[part]))
        copies[-1].start()
    own_order, other_order = order_of(own_x), order_of(other_x)
    for head in range(HALF):
        offset = offset_ref[base_ref[0] * HALF + head]
        index = []
        for view in range(2):
            index.append(chosen_rows(view, offset, own_order))
            index.append(chosen_rows(view, offset, other_order) + TOK)
        chosen = one_hot(jnp.concatenate(index, axis=0), SEG)
        far_rows = jnp.dot(
            chosen, all_ref[:, head * 256 : head * 256 + 256], preferred_element_type=F32
        )
        far_kv, far_q = far_rows[:, 0:128].astype(BF16), far_rows[:, 128:256]
        for view in range(2):
            pair = (view * HALF + head) * 4
            for q_part in range(2):
                row = view * 2 * SPARSE + q_part * 16
                folded = (
                    far_q[row : row + 16] + swap_halves(far_q[SPARSE + row : SPARSE + row + 16])
                ).astype(BF16)
                for k_half in range(2):
                    peer = pair + q_part * 2 + k_half
                    at = view * 2 * SPARSE + k_half * SPARSE
                    send_ref[peer, 0:32, :] = far_kv[at : at + SPARSE]
                    send_ref[peer, 32:48, :] = folded
    for peer in range(4 * 2 * HALF, POS):
        send_ref[peer] = jnp.zeros((48, 128), BF16)
    for copy in copies:
        copy.wait()


def near_kernel(q_ref, kv_ref, keep_ref, give_ref):
    keys = kv_ref[...]
    lane = lax.broadcasted_iota(jnp.int32, (SEG, 128), 1)
    values = jnp.where(lane < HEAD_DIM, swap_halves(keys.astype(F32)), 1.0).astype(BF16)
    tile = NEAR_TILE
    out_lane = lax.broadcasted_iota(jnp.int32, (tile, 128), 1)
    for at in range(0, SEG, tile):
        scores = lax.dot_general(
            q_ref[at : at + tile, :], keys, (((1,), (1,)), ((), ())), preferred_element_type=F32
        )
        row_max = jnp.max(scores, axis=1, keepdims=True)
        weights = jnp.exp2((scores - row_max) * EXP_SCALE).astype(BF16)
        summed = jnp.dot(weights, values, preferred_element_type=F32)
        result = jnp.where(
            out_lane < HEAD_DIM, summed / swap_halves(summed), row_max * SCALE + jnp.log(summed)
        )
        out_ref = keep_ref if at < TOK else give_ref
        out_ref[at % TOK : at % TOK + tile, :] = result


def near_level(both):
    half = shape_of(TOK, HALF * 128, dtype=F32)
    keys = pl.BlockSpec((SEG, 128), lambda h: (0, 2 * h))
    queries = pl.BlockSpec((SEG, 128), lambda h: (0, 2 * h + 1))
    part = pl.BlockSpec((TOK, 128), lambda h: (0, h))
    return pl.pallas_call(
        near_kernel,
        out_shape=[half, half],
        grid=(HALF,),
        in_specs=[queries, keys],
        out_specs=[part, part],
        cost_estimate=pl.CostEstimate(
            flops=4 * HALF * SEG * SEG * 128, bytes_accessed=3 << 20, transcendentals=HALF * SEG * SEG
        ),
        compiler_params=pltpu.CompilerParams(vmem_limit_bytes=LIMITS[1]),
        interpret=INTERPRET,
    )(both, both)


def far_kernel(core_ref, got_ref, back_ref):
    core = core_ref[0]
    keys = got_ref[:, 0:32, :].reshape(POS * 32, 128)
    wide = got_ref[:, 32:48, :].reshape(POS * 16, 128).astype(F32)
    lane = lax.broadcasted_iota(jnp.int32, (POS * 32, 128), 1)
    values = jnp.where(lane < HEAD_DIM, swap_halves(keys.astype(F32)), 1.0).astype(BF16)
    q_lane = lax.broadcasted_iota(jnp.int32, (POS * 16, 128), 1)
    q_row = lax.broadcasted_iota(jnp.int32, (POS * 16, 128), 0)
    place = jnp.right_shift(q_lane, 4)
    mine = jnp.bitwise_and(q_lane, 15) == jnp.bitwise_and(q_row, 15)
    source = lax.broadcasted_iota(jnp.int32, (POS, POS * 16), 0)
    member = jnp.right_shift(lax.broadcasted_iota(jnp.int32, (POS, POS * 16), 1), 4)
    spread = jnp.where(source == member, 1.0, 0.0).astype(BF16)
    for part in range(2):
        queries = jnp.where(q_lane < HEAD_DIM, wide if part == 0 else swap_halves(wide), 0.0)
        scores = lax.dot_general(
            queries.astype(BF16), keys, (((1,), (1,)), ((), ())), preferred_element_type=F32
        )
        row_max = jnp.max(scores, axis=1, keepdims=True)
        weights = jnp.exp2((scores - row_max) * EXP_SCALE).astype(BF16)
        summed = jnp.dot(weights, values, preferred_element_type=F32)
        swapped = swap_halves(summed)
        out = (summed / swapped).reshape(POS, 16, 128)
        packed = jnp.concatenate([out[:, 0:8, :HEAD_DIM], out[:, 8:16, :HEAD_DIM]], axis=2)
        high, middle, low = parts3(row_max * SCALE + jnp.log(swapped))
        stats = jnp.where(
            place == 0, high, jnp.where(place == 1, middle, jnp.where(place == 2, low, 0.0))
        )
        stats = jnp.where(mine, stats, 0.0).astype(BF16)
        rows = jnp.dot(spread, stats, preferred_element_type=F32)
        rows = jnp.broadcast_to(rows[:, None, :], (POS, 8, 128))
        block = jnp.concatenate([packed, rows], axis=1).astype(BF16)
        back_ref[:, pl.ds(core if part == 0 else 1 - core, 1)] = block[:, None]


def prepare_kernel(
    base_ref, offset_ref, keep_ref, got_ref, order_ref, gain_ref,
    dense_ref, rows_ref, spread_ref, scale_ref,
):
    core = base_ref[0]
    width = HALF * HEAD_DIM
    hots = [[], []]
    order = order_ref[...]
    for group, near_ref in enumerate((keep_ref, got_ref)):
        dense_ref[:, group * width : (group + 1) * width] = jnp.concatenate(
            [near_ref[:, head * 128 : head * 128 + HEAD_DIM] for head in range(HALF)], axis=1
        )
        heads = core if group == 0 else 1 - core
        for head in range(HALF):
            pieces = jnp.concatenate(parts3(near_ref[:, head * 128 : head * 128 + 128]), axis=1)
            offset = offset_ref[heads * HALF + head]
            for view in range(2):
                chosen = one_hot(chosen_rows(view, offset, order), TOK)
                hots[view].append(chosen)
                taken = jnp.dot(chosen, pieces, preferred_element_type=F32)
                at = group * 192 + (view * HALF + head) * SPARSE
                rows_ref[at : at + SPARSE, :] = taken[:, :128] + taken[:, 128:256] + taken[:, 256:]
    hots = [jnp.concatenate(part, axis=0) for part in hots]
    for at, part in enumerate(
        (hots[0][:128], jnp.concatenate([hots[0][128:], hots[1][128:]], axis=0), hots[1][:128])
    ):
        spread_ref[:, at * 128 : at * 128 + 128] = part.astype(F32).T.astype(BF16)
    gain = gain_ref[...].reshape(1, INNER)
    scale_ref[...] = jnp.where(
        core == 0, gain, jnp.concatenate([gain[:, width:], gain[:, :width]], axis=1)
    )


def output_kernel(
    core_ref, far_ref, dense_ref, rows_ref, spread_ref, gain_ref, own_w, other_w, plain_ref, flip_ref
):
    core = core_ref[0]
    lane = lax.broadcasted_iota(jnp.int32, (192, 128), 1)
    mine = jnp.bitwise_and(lane, 15) == jnp.bitwise_and(
        lax.broadcasted_iota(jnp.int32, (192, 128), 0), 15
    )
    deltas = []
    for group in range(2):
        outs, logs = [], []
        for k_half in range(2):
            blocks, stats = [], []
            for pair in range(2 * HALF):
                for q_part in range(2):
                    peer = (pair * 4 + q_part * 2 + k_half) * 2
                    block = far_ref[peer + (core if group == 0 else 1 - core)].astype(F32)
                    blocks += [block[0:8, :HEAD_DIM], block[0:8, HEAD_DIM:]]
                    stats += [block[8:16], block[8:16]]
            outs.append(jnp.concatenate(blocks, axis=0))
            found = jnp.where(mine, jnp.concatenate(stats, axis=0), 0.0)
            logs.append(jnp.sum(found, axis=1, keepdims=True))
        top = jnp.maximum(logs[0], logs[1])
        weight0, weight1 = jnp.exp(logs[0] - top), jnp.exp(logs[1] - top)
        joint = weight0 + weight1
        far = (weight0 * outs[0] + weight1 * outs[1]) / joint
        near = rows_ref[group * 192 : group * 192 + 192, :]
        gap = near[:, HEAD_DIM : HEAD_DIM + 1] - (top + jnp.log(joint))
        deltas.append((far - near[:, :HEAD_DIM]) / (1.0 + jnp.exp(gap)))
    width = HALF * HEAD_DIM
    row = jnp.right_shift(lax.broadcasted_iota(jnp.int32, (192, INNER), 0), 5)
    col = jnp.right_shift(lax.broadcasted_iota(jnp.int32, (192, INNER), 1), 6)
    none = jnp.zeros((HEAD_DIM, INNER), BF16)
    own_rows = pl.ds(pl.multiple_of(core * width, 64), width)
    other_rows = pl.ds(pl.multiple_of((1 - core) * width, 64), width)
    weights = [
        jnp.concatenate([part[own_rows, :], part[other_rows, :]], axis=0) for part in (own_w, other_w)
    ]
    for view, out_ref in enumerate((plain_ref, flip_ref)):
        delta = jnp.concatenate([d[view * 96 : view * 96 + 96] for d in deltas], axis=0)
        blocks = jnp.where(row == col, jnp.concatenate([delta] * HEADS, axis=1), 0.0).astype(BF16)
        if view == 0:
            blocks = jnp.concatenate([blocks, none], axis=0)
        else:
            blocks = jnp.concatenate([none, blocks[128:], blocks[:128]], axis=0)
        for at in range(0, TOK, 256):
            attended = dense_ref[at : at + 256, :] + jnp.dot(
                spread_ref[at : at + 256, view * 128 : view * 128 + 256],
                blocks,
                preferred_element_type=F32,
            )
            average = jnp.mean(attended, axis=-1, keepdims=True)
            centred = attended - average
            variance = jnp.mean(centred * centred, axis=-1, keepdims=True)
            mixed = (centred * lax.rsqrt(variance + eps_norm) * gain_ref[...]).astype(BF16)
            for part, place in zip(weights, (core, 1 - core)):
                out_ref[at : at + 256, pl.ds(pl.multiple_of(place * INNER, 128), INNER)] = jnp.dot(
                    mixed, part, preferred_element_type=F32
                ).astype(BF16)


def core_swap(block):
    return lax.ppermute(block, "core", [(0, 1), (1, 0)])


def layer(
    tile_features, flip_perm, head_offsets, input_gain, projection, output_gain, output_weight
):
    core = lax.axis_index("core").astype(jnp.int32)
    pos = lax.axis_index("pos").astype(jnp.int32)
    rank = pos * 2 + core
    core_id = core[None]
    base = jnp.stack([core, rank * TOK, (rank ^ 1) * TOK, lax.axis_index("yh").astype(jnp.int32)])

    last = 2 * POS - 1
    ctx = ("pos", "core")
    own_perm = lax.ppermute(flip_perm, ctx, [(last - r, r) for r in range(2 * POS)])
    packed = gather_weights(core_id, projection, output_weight)
    own_x, own_order = call(
        norm_kernel,
        [shape_of(TOK + 16, D), shape_of(1, TOK, dtype=F32)],
        [SMEM, VMEM, VMEM, VMEM],
        moved=2 << 20,
    )(base, tile_features[0], input_gain, own_perm)
    other_x = core_swap(own_x)

    both, send, own_w = call(
        project_kernel,
        [
            shape_of(SEG, D),
            shape_of(POS, 48, 128),
            shape_of(INNER, INNER),
        ],
        [SMEM, SMEM, VMEM, VMEM, VMEM],
        [
            pltpu.VMEM((D, D), BF16),
            pltpu.VMEM((SEG, D), BF16),
            pltpu.SemaphoreType.DMA((2,)),
        ],
        outs=[HBM, VMEM, VMEM],
        flops=2 * SEG * D * D,
        moved=4 << 20,
        limit=LIMITS[0],
    )(base, head_offsets, own_x, other_x, packed)

    got = lax.all_to_all(send, "pos", 0, 0, tiled=True)
    keep, give = near_level(both)
    near_got = core_swap(give)
    back = call(
        far_kernel, shape_of(POS, 2, 16, 128), [SMEM, VMEM], flops=4 * SEG * SEG * 128, moved=1 << 20,
        limit=LIMITS[2],
    )(core_id, got)
    far = lax.all_to_all(back.reshape(2 * POS, 16, 128), ctx, 0, 0, tiled=True)

    other_w = core_swap(own_w)
    prepared = call(
        prepare_kernel,
        [
            shape_of(TOK, INNER, dtype=F32),
            shape_of(INNER, 128, dtype=F32),
            shape_of(TOK, INNER),
            shape_of(1, INNER, dtype=F32),
        ],
        [SMEM, SMEM, VMEM, VMEM, VMEM, VMEM],
        flops=1 << 28,
        moved=4 << 20,
        limit=LIMITS[3],
    )(base, head_offsets, keep, near_got, own_order, output_gain)

    plain_view, flipped_view = call(
        output_kernel,
        [shape_of(TOK, D), shape_of(TOK, D)],
        [SMEM] + [VMEM] * 7,
        flops=4 * SEG * INNER * D,
        moved=4 << 20,
        limit=LIMITS[4],
    )(core_id, far, *prepared, own_w, other_w)
    return (plain_view[None], flipped_view[None])


def solution(mesh):
    fine = Mesh(mesh.devices.reshape(DP_X, DP_Y, POS, 2), ("x", "yh", "pos", "core"))
    dp, ctx = ("x", "yh"), ("pos", "core")
    placed = (P(dp, ctx, None), P(dp, ctx), P(), P(), P(dp, None), P(), P(dp, None))
    return jax.shard_map(
        layer,
        mesh=fine,
        in_specs=placed,
        out_specs=(P(dp, ctx, None), P(dp, ctx, None)),
        check_vma=False,
    )
```

```python
import jax
import jax.numpy as jnp
from jax import lax
from jax.experimental import pallas as pl
from jax.experimental.pallas import tpu as pltpu
from jax.sharding import Mesh, PartitionSpec as P


HEADS = 6
HEAD_DIM = 64
INNER = 384
D = 768
RATIO = 16
TOK = 512
SEG = 1024
HALF = 3
SPARSE = TOK // RATIO
POS = 32
DP_X, DP_Y = 4, 2
INTERPRET = False
NEAR_TILE = 256
LIMITS = [24 << 20, 60 * 1024 * 1024, 24 << 20, 24 << 20, 24 << 20]

eps_norm = 1e-05
EXP_SCALE = HEAD_DIM ** (-0.5) * 1.4426950408889634
SCALE = HEAD_DIM ** (-0.5)

F32 = jnp.float32
BF16 = jnp.bfloat16
VMEM = pl.BlockSpec(memory_space=pltpu.VMEM)
SMEM = pl.BlockSpec(memory_space=pltpu.SMEM)
ANY = pl.BlockSpec(memory_space=pl.ANY)


def call(kernel, out_shape, specs, scratch=(), flops=0, moved=0, limit=24 << 20, outs=None):
    single = not isinstance(out_shape, (list, tuple))
    return pl.pallas_call(
        kernel,
        out_shape=out_shape,
        in_specs=specs,
        out_specs=outs or (VMEM if single else [VMEM] * len(out_shape)),
        scratch_shapes=list(scratch),
        cost_estimate=pl.CostEstimate(flops=flops, bytes_accessed=moved, transcendentals=0),
        compiler_params=pltpu.CompilerParams(vmem_limit_bytes=limit),
        interpret=INTERPRET,
    )


def shape_of(*dims, dtype=BF16):
    return jax.ShapeDtypeStruct(dims, dtype)


def swap_halves(block):
    return jnp.concatenate([block[:, HEAD_DIM:], block[:, :HEAD_DIM]], axis=1)


def parts3(value):
    high = value.astype(BF16)
    rest = value - high.astype(F32)
    middle = rest.astype(BF16)
    low = (rest - middle.astype(F32)).astype(BF16)
    return high, middle, low


def pack_kernel(core_ref, proj_ref, outw_ref, packed_ref):
    for core in range(2):

        @pl.when(core_ref[0] == core)
        def _():
            for head in range(HALF):
                col = (core * HALF + head) * HEAD_DIM
                lanes = slice(head * 128, head * 128 + 128)
                keys = proj_ref[:, INNER + col : INNER + col + HEAD_DIM].astype(F32)
                values = proj_ref[:, 2 * INNER + col : 2 * INNER + col + HEAD_DIM].astype(F32)
                queries = proj_ref[:, col : col + HEAD_DIM].astype(F32)
                packed_ref[0:96, lanes] = jnp.concatenate([keys, values], axis=1).astype(BF16)
                packed_ref[96:144, lanes] = jnp.concatenate(
                    [queries[:48], queries[48:]], axis=1
                ).astype(BF16)
            packed_ref[144:192, :] = outw_ref[:, core * INNER : (core + 1) * INNER]


def pack_weights(core, projection, output_weight):
    return call(pack_kernel, shape_of(192, INNER), [SMEM, VMEM, VMEM], limit=60 * 1024 * 1024)(
        core, projection, output_weight
    )


def fan_kernel(own_ref, other_ref, both_ref):
    for peer in range(DP_X):
        both_ref[peer, 0] = own_ref[...]
        both_ref[peer, 1] = other_ref[...]


def gather_weights(core, projection, output_weight):
    packed = pack_weights(core, projection, output_weight)
    other = lax.ppermute(packed, "yh", [(0, 1), (1, 0)])
    both = call(fan_kernel, shape_of(DP_X, DP_Y, 192, INNER), [VMEM, VMEM], limit=60 * 1024 * 1024)(
        packed, other
    )
    got = lax.all_to_all(both, "x", 0, 0, tiled=True)
    return got.reshape(DP_X * DP_Y, 192, INNER)


def norm_kernel(base_ref, x_ref, gain_ref, perm_ref, out_ref, order_ref):
    gain = gain_ref[...].reshape(1, D)
    for row in range(0, TOK, 128):
        values = x_ref[row : row + 128, :].astype(F32)
        average = jnp.mean(values, axis=-1, keepdims=True)
        centred = values - average
        variance = jnp.mean(centred * centred, axis=-1, keepdims=True)
        out_ref[row : row + 128, :] = (
            centred * lax.rsqrt(variance + eps_norm) * gain
        ).astype(BF16)
    order_ref[...] = (perm_ref[...] - base_ref[1]).astype(F32)
    local = jnp.broadcast_to(perm_ref[...] - base_ref[1], (16, TOK))
    row = lax.broadcasted_iota(jnp.int32, (16, TOK), 0)
    parts = jnp.where(row == 0, jnp.right_shift(local, 4), jnp.bitwise_and(local, 15))
    out_ref[TOK : TOK + 16, 0:TOK] = parts.astype(F32).astype(BF16)
    out_ref[TOK : TOK + 16, TOK:] = jnp.zeros((16, D - TOK), BF16)


def order_of(x_ref):
    parts = x_ref[TOK : TOK + 16, 0:TOK].astype(F32)
    return parts[0:1, :] * 16.0 + parts[1:2, :]


def chosen_rows(view, offset, order):
    rows = lax.broadcasted_iota(jnp.int32, (SPARSE, 1), 0) * RATIO + offset
    if view == 0:
        return rows
    lane = lax.broadcasted_iota(jnp.int32, (SPARSE, TOK), 1)
    tiles = jnp.broadcast_to(order, (SPARSE, TOK))
    picked = jnp.sum(jnp.where(lane == rows, tiles, 0.0), axis=1, keepdims=True)
    return picked.astype(jnp.int32)


def one_hot(index, width):
    token = lax.broadcasted_iota(jnp.int32, (index.shape[0], width), 1)
    return jnp.where(token == index, 1.0, 0.0).astype(BF16)


def pick_kernel(base_ref, offset_ref, own_x, other_x, picked_ref):
    orders = order_of(own_x), order_of(other_x)
    hots = [[], []]
    for head in range(HALF):
        offset = offset_ref[base_ref[0] * HALF + head]
        for view in range(2):
            for part in range(2):
                chosen = one_hot(chosen_rows(view, offset, orders[part]), TOK)
                hots[part].append(chosen)
    for part, x_ref in enumerate((own_x, other_x)):
        rows = jnp.dot(
            jnp.concatenate(hots[part], axis=0), x_ref[0:TOK, :], preferred_element_type=F32
        ).astype(BF16)
        for block in range(2 * HALF):
            at = block * 2 * SPARSE + part * SPARSE
            picked_ref[at : at + SPARSE, :] = rows[block * SPARSE : block * SPARSE + SPARSE]


def unpack_head(flip, packed_ref, lanes, w_ref, at):
    lane = lax.broadcasted_iota(jnp.int32, (48, 128), 1)
    for entry in range(8):
        shard = (entry - entry % 2) + (entry % 2 ^ flip)
        row = pl.multiple_of(shard * 96, 16)
        w_ref[pl.ds(row, 96), at : at + 128] = packed_ref[entry, 0:96, lanes]
        folded = packed_ref[entry, 96:144, lanes].astype(F32)
        for first, part in ((0, folded), (48, swap_halves(folded))):
            w_ref[pl.ds(pl.multiple_of(row + first, 16), 48), at + 128 : at + 256] = jnp.where(
                lane < HEAD_DIM, part, 0.0
            ).astype(BF16)


def send_kernel(base_ref, picked_ref, packed_ref, send_ref, w_ref):
    for head in range(HALF):
        at = head * 256
        unpack_head(base_ref[3], packed_ref, slice(head * 128, head * 128 + 128), w_ref, at)
        far_rows = jnp.dot(
            picked_ref[head * 128 : head * 128 + 128, :],
            w_ref[:, at : at + 256],
            preferred_element_type=F32,
        ).astype(BF16)
        far_kv, far_q = far_rows[:, 0:128], far_rows[:, 128:256].astype(F32)
        for view in range(2):
            pair = (view * HALF + head) * 4
            for q_part in range(2):
                row = view * 2 * SPARSE + q_part * 16
                folded = (
                    far_q[row : row + 16] + swap_halves(far_q[SPARSE + row : SPARSE + row + 16])
                ).astype(BF16)
                for k_half in range(2):
                    peer = pair + q_part * 2 + k_half
                    first = view * 2 * SPARSE + k_half * SPARSE
                    send_ref[peer, 0:32, :] = far_kv[first : first + SPARSE]
                    send_ref[peer, 32:48, :] = folded
    for peer in range(4 * 2 * HALF, POS):
        send_ref[peer] = jnp.zeros((48, 128), BF16)


def near_kernel(base_ref, own_x, other_x, packed_ref, keep_ref, give_ref, outw_ref, w_ref, all_ref):
    flip = base_ref[3]

    @pl.when(pl.program_id(0) == 0)
    def _():
        for entry in range(8):
            shard = (entry - entry % 2) + (entry % 2 ^ flip)
            outw_ref[pl.ds(pl.multiple_of(shard * 48, 16), 48), :] = packed_ref[entry, 144:192, :]

    lanes = pl.ds(pl.multiple_of(pl.program_id(0) * 128, 128), 128)
    unpack_head(flip, packed_ref, lanes, w_ref, 0)
    for part, x_ref in enumerate((own_x, other_x)):
        all_ref[part * TOK : part * TOK + TOK, :] = jnp.dot(
            x_ref[0:TOK, :], w_ref[...], preferred_element_type=F32
        ).astype(BF16)
    keys = all_ref[:, 0:128]
    lane = lax.broadcasted_iota(jnp.int32, (SEG, 128), 1)
    values = jnp.where(lane < HEAD_DIM, swap_halves(keys.astype(F32)), 1.0).astype(BF16)
    tile = NEAR_TILE
    out_lane = lax.broadcasted_iota(jnp.int32, (tile, 128), 1)
    for at in range(0, SEG, tile):
        scores = lax.dot_general(
            all_ref[at : at + tile, 128:256],
            keys,
            (((1,), (1,)), ((), ())),
            preferred_element_type=F32,
        )
        row_max = jnp.max(scores, axis=1, keepdims=True)
        weights = jnp.exp2((scores - row_max) * EXP_SCALE).astype(BF16)
        summed = jnp.dot(weights, values, preferred_element_type=F32)
        result = jnp.where(
            out_lane < HEAD_DIM, summed / swap_halves(summed), row_max * SCALE + jnp.log(summed)
        )
        out_ref = keep_ref if at < TOK else give_ref
        out_ref[at % TOK : at % TOK + tile, :] = result


def near_level(base, own_x, other_x, packed):
    half = shape_of(TOK, HALF * 128, dtype=F32)
    tiles = pl.BlockSpec((TOK + 16, D), lambda h: (0, 0))
    part = pl.BlockSpec((TOK, 128), lambda h: (0, h))
    return pl.pallas_call(
        near_kernel,
        out_shape=[half, half, shape_of(INNER, INNER)],
        grid=(HALF,),
        in_specs=[SMEM, tiles, tiles, pl.BlockSpec((8, 192, INNER), lambda h: (0, 0, 0))],
        out_specs=[part, part, pl.BlockSpec((INNER, INNER), lambda h: (0, 0))],
        scratch_shapes=[pltpu.VMEM((D, 256), BF16), pltpu.VMEM((SEG, 256), BF16)],
        cost_estimate=pl.CostEstimate(
            flops=4 * HALF * SEG * SEG * 128, bytes_accessed=5 << 20, transcendentals=HALF * SEG * SEG
        ),
        compiler_params=pltpu.CompilerParams(vmem_limit_bytes=LIMITS[1]),
        interpret=INTERPRET,
    )(base, own_x, other_x, packed)


def far_kernel(core_ref, got_ref, back_ref):
    core = core_ref[0]
    keys = got_ref[:, 0:32, :].reshape(POS * 32, 128)
    wide = got_ref[:, 32:48, :].reshape(POS * 16, 128).astype(F32)
    lane = lax.broadcasted_iota(jnp.int32, (POS * 32, 128), 1)
    values = jnp.where(lane < HEAD_DIM, swap_halves(keys.astype(F32)), 1.0).astype(BF16)
    q_lane = lax.broadcasted_iota(jnp.int32, (POS * 16, 128), 1)
    q_row = lax.broadcasted_iota(jnp.int32, (POS * 16, 128), 0)
    place = jnp.right_shift(q_lane, 4)
    mine = jnp.bitwise_and(q_lane, 15) == jnp.bitwise_and(q_row, 15)
    source = lax.broadcasted_iota(jnp.int32, (POS, POS * 16), 0)
    member = jnp.right_shift(lax.broadcasted_iota(jnp.int32, (POS, POS * 16), 1), 4)
    spread = jnp.where(source == member, 1.0, 0.0).astype(BF16)
    for part in range(2):
        queries = jnp.where(q_lane < HEAD_DIM, wide if part == 0 else swap_halves(wide), 0.0)
        scores = lax.dot_general(
            queries.astype(BF16), keys, (((1,), (1,)), ((), ())), preferred_element_type=F32
        )
        row_max = jnp.max(scores, axis=1, keepdims=True)
        weights = jnp.exp2((scores - row_max) * EXP_SCALE).astype(BF16)
        summed = jnp.dot(weights, values, preferred_element_type=F32)
        swapped = swap_halves(summed)
        out = (summed / swapped).reshape(POS, 16, 128)
        packed = jnp.concatenate([out[:, 0:8, :HEAD_DIM], out[:, 8:16, :HEAD_DIM]], axis=2)
        high, middle, low = parts3(row_max * SCALE + jnp.log(swapped))
        stats = jnp.where(
            place == 0, high, jnp.where(place == 1, middle, jnp.where(place == 2, low, 0.0))
        )
        stats = jnp.where(mine, stats, 0.0).astype(BF16)
        rows = jnp.dot(spread, stats, preferred_element_type=F32)
        rows = jnp.broadcast_to(rows[:, None, :], (POS, 8, 128))
        block = jnp.concatenate([packed, rows], axis=1).astype(BF16)
        back_ref[:, pl.ds(core if part == 0 else 1 - core, 1)] = block[:, None]


def prepare_kernel(
    base_ref, offset_ref, keep_ref, got_ref, order_ref, gain_ref,
    dense_ref, rows_ref, spread_ref, scale_ref,
):
    core = base_ref[0]
    width = HALF * HEAD_DIM
    hots = [[], []]
    order = order_ref[...]
    for group, near_ref in enumerate((keep_ref, got_ref)):
        dense_ref[:, group * width : (group + 1) * width] = jnp.concatenate(
            [near_ref[:, head * 128 : head * 128 + HEAD_DIM] for head in range(HALF)], axis=1
        )
        heads = core if group == 0 else 1 - core
        for head in range(HALF):
            pieces = jnp.concatenate(parts3(near_ref[:, head * 128 : head * 128 + 128]), axis=1)
            offset = offset_ref[heads * HALF + head]
            for view in range(2):
                chosen = one_hot(chosen_rows(view, offset, order), TOK)
                hots[view].append(chosen)
                taken = jnp.dot(chosen, pieces, preferred_element_type=F32)
                at = group * 192 + (view * HALF + head) * SPARSE
                rows_ref[at : at + SPARSE, :] = taken[:, :128] + taken[:, 128:256] + taken[:, 256:]
    hots = [jnp.concatenate(part, axis=0) for part in hots]
    for at, part in enumerate(
        (hots[0][:128], jnp.concatenate([hots[0][128:], hots[1][128:]], axis=0), hots[1][:128])
    ):
        spread_ref[:, at * 128 : at * 128 + 128] = part.astype(F32).T.astype(BF16)
    gain = gain_ref[...].reshape(1, INNER)
    scale_ref[...] = jnp.where(
        core == 0, gain, jnp.concatenate([gain[:, width:], gain[:, :width]], axis=1)
    )


def output_kernel(
    core_ref, far_ref, dense_ref, rows_ref, spread_ref, gain_ref, own_w, other_w, plain_out, flip_out,
    plain_ref, flip_ref, sems,
):
    core = core_ref[0]
    lane = lax.broadcasted_iota(jnp.int32, (192, 128), 1)
    mine = jnp.bitwise_and(lane, 15) == jnp.bitwise_and(
        lax.broadcasted_iota(jnp.int32, (192, 128), 0), 15
    )
    deltas = []
    for group in range(2):
        outs, logs = [], []
        for k_half in range(2):
            blocks, stats = [], []
            for pair in range(2 * HALF):
                for q_part in range(2):
                    peer = (pair * 4 + q_part * 2 + k_half) * 2
                    block = far_ref[peer + (core if group == 0 else 1 - core)].astype(F32)
                    blocks += [block[0:8, :HEAD_DIM], block[0:8, HEAD_DIM:]]
                    stats += [block[8:16], block[8:16]]
            outs.append(jnp.concatenate(blocks, axis=0))
            found = jnp.where(mine, jnp.concatenate(stats, axis=0), 0.0)
            logs.append(jnp.sum(found, axis=1, keepdims=True))
        top = jnp.maximum(logs[0], logs[1])
        weight0, weight1 = jnp.exp(logs[0] - top), jnp.exp(logs[1] - top)
        joint = weight0 + weight1
        far = (weight0 * outs[0] + weight1 * outs[1]) / joint
        near = rows_ref[group * 192 : group * 192 + 192, :]
        gap = near[:, HEAD_DIM : HEAD_DIM + 1] - (top + jnp.log(joint))
        deltas.append((far - near[:, :HEAD_DIM]) / (1.0 + jnp.exp(gap)))
    width = HALF * HEAD_DIM
    row = jnp.right_shift(lax.broadcasted_iota(jnp.int32, (192, INNER), 0), 5)
    col = jnp.right_shift(lax.broadcasted_iota(jnp.int32, (192, INNER), 1), 6)
    none = jnp.zeros((HEAD_DIM, INNER), BF16)
    own_rows = pl.ds(pl.multiple_of(core * width, 64), width)
    other_rows = pl.ds(pl.multiple_of((1 - core) * width, 64), width)
    weights = [
        jnp.concatenate([part[own_rows, :], part[other_rows, :]], axis=0) for part in (own_w, other_w)
    ]
    copies = []
    for view, (out_ref, hbm_ref) in enumerate(((plain_ref, plain_out), (flip_ref, flip_out))):
        delta = jnp.concatenate([d[view * 96 : view * 96 + 96] for d in deltas], axis=0)
        blocks = jnp.where(row == col, jnp.concatenate([delta] * HEADS, axis=1), 0.0).astype(BF16)
        if view == 0:
            blocks = jnp.concatenate([blocks, none], axis=0)
        else:
            blocks = jnp.concatenate([none, blocks[128:], blocks[:128]], axis=0)
        for at in range(0, TOK, 256):
            attended = dense_ref[at : at + 256, :] + jnp.dot(
                spread_ref[at : at + 256, view * 128 : view * 128 + 256],
                blocks,
                preferred_element_type=F32,
            )
            average = jnp.mean(attended, axis=-1, keepdims=True)
            centred = attended - average
            variance = jnp.mean(centred * centred, axis=-1, keepdims=True)
            mixed = (centred * lax.rsqrt(variance + eps_norm) * gain_ref[...]).astype(BF16)
            for part, place in zip(weights, (core, 1 - core)):
                out_ref[at : at + 256, pl.ds(pl.multiple_of(place * INNER, 128), INNER)] = jnp.dot(
                    mixed, part, preferred_element_type=F32
                ).astype(BF16)
            rows = pl.ds(at, 256)
            copies.append(
                pltpu.make_async_copy(
                    out_ref.at[rows], hbm_ref.at[rows], sems.at[view * 2 + at // 256]
                )
            )
            copies[-1].start()
    for copy in copies:
        copy.wait()


def core_swap(block):
    return lax.ppermute(block, "core", [(0, 1), (1, 0)])


def layer(
    tile_features, flip_perm, head_offsets, input_gain, projection, output_gain, output_weight
):
    core = lax.axis_index("core").astype(jnp.int32)
    pos = lax.axis_index("pos").astype(jnp.int32)
    rank = pos * 2 + core
    core_id = core[None]
    base = jnp.stack([core, rank * TOK, (rank ^ 1) * TOK, lax.axis_index("yh").astype(jnp.int32)])

    last = 2 * POS - 1
    ctx = ("pos", "core")
    own_perm = lax.ppermute(flip_perm, ctx, [(last - r, r) for r in range(2 * POS)])
    packed = gather_weights(core_id, projection, output_weight)
    own_x, own_order = call(
        norm_kernel,
        [shape_of(TOK + 16, D), shape_of(1, TOK, dtype=F32)],
        [SMEM, VMEM, VMEM, VMEM],
        moved=2 << 20,
    )(base, tile_features[0], input_gain, own_perm)
    other_x = core_swap(own_x)

    picked = call(
        pick_kernel,
        shape_of(HALF * 128, D),
        [SMEM, SMEM, VMEM, VMEM],
        flops=2 * HALF * 128 * SEG * D,
        moved=3 << 20,
    )(base, head_offsets, own_x, other_x)
    send = call(
        send_kernel,
        shape_of(POS, 48, 128),
        [SMEM, VMEM, VMEM],
        [pltpu.VMEM((D, D), BF16)],
        flops=2 * HALF * 128 * D * 256,
        moved=2 << 20,
        limit=LIMITS[0],
    )(base, picked, packed)

    got = lax.all_to_all(send, "pos", 0, 0, tiled=True)
    keep, give, own_w = near_level(base, own_x, other_x, packed)
    near_got = core_swap(give)
    back = call(
        far_kernel, shape_of(POS, 2, 16, 128), [SMEM, VMEM], flops=4 * SEG * SEG * 128, moved=1 << 20,
        limit=LIMITS[2],
    )(core_id, got)
    far = lax.all_to_all(back.reshape(2 * POS, 16, 128), ctx, 0, 0, tiled=True)

    other_w = core_swap(own_w)
    prepared = call(
        prepare_kernel,
        [
            shape_of(TOK, INNER, dtype=F32),
            shape_of(INNER, 128, dtype=F32),
            shape_of(TOK, INNER),
            shape_of(1, INNER, dtype=F32),
        ],
        [SMEM, SMEM, VMEM, VMEM, VMEM, VMEM],
        flops=1 << 28,
        moved=4 << 20,
        limit=LIMITS[3],
    )(base, head_offsets, keep, near_got, own_order, output_gain)

    plain_view, flipped_view = call(
        output_kernel,
        [shape_of(TOK, D), shape_of(TOK, D)],
        [SMEM] + [VMEM] * 7,
        [pltpu.VMEM((TOK, D), BF16), pltpu.VMEM((TOK, D), BF16), pltpu.SemaphoreType.DMA((4,))],
        outs=[ANY, ANY],
        flops=4 * SEG * INNER * D,
        moved=4 << 20,
        limit=LIMITS[4],
    )(core_id, far, *prepared, own_w, other_w)
    return (plain_view[None], flipped_view[None])


def solution(mesh):
    fine = Mesh(mesh.devices.reshape(DP_X, DP_Y, POS, 2), ("x", "yh", "pos", "core"))
    dp, ctx = ("x", "yh"), ("pos", "core")
    placed = (P(dp, ctx, None), P(dp, ctx), P(), P(), P(dp, None), P(), P(dp, None))
    return jax.shard_map(
        layer,
        mesh=fine,
        in_specs=placed,
        out_specs=(P(dp, ctx, None), P(dp, ctx, None)),
        check_vma=False,
    )
```

```python
import jax
import jax.numpy as jnp
from jax import lax
from jax.experimental import pallas as pl
from jax.experimental.pallas import tpu as pltpu
from jax.sharding import Mesh, PartitionSpec as P


HEADS = 6
HEAD_DIM = 64
INNER = 384
D = 768
RATIO = 16
TOK = 512
SEG = 1024
HALF = 3
SPARSE = TOK // RATIO
POS = 32
DP_X, DP_Y = 4, 2
INTERPRET = False
NEAR_TILE = 512
LIMITS = [24 << 20, 60 * 1024 * 1024, 24 << 20, 24 << 20, 24 << 20]

eps_norm = 1e-05
EXP_SCALE = HEAD_DIM ** (-0.5) * 1.4426950408889634
SCALE = HEAD_DIM ** (-0.5)

F32 = jnp.float32
BF16 = jnp.bfloat16
VMEM = pl.BlockSpec(memory_space=pltpu.VMEM)
SMEM = pl.BlockSpec(memory_space=pltpu.SMEM)
ANY = pl.BlockSpec(memory_space=pl.ANY)


def call(kernel, out_shape, specs, scratch=(), flops=0, moved=0, limit=24 << 20, outs=None):
    single = not isinstance(out_shape, (list, tuple))
    return pl.pallas_call(
        kernel,
        out_shape=out_shape,
        in_specs=specs,
        out_specs=outs or (VMEM if single else [VMEM] * len(out_shape)),
        scratch_shapes=list(scratch),
        cost_estimate=pl.CostEstimate(flops=flops, bytes_accessed=moved, transcendentals=0),
        compiler_params=pltpu.CompilerParams(vmem_limit_bytes=limit),
        interpret=INTERPRET,
    )


def shape_of(*dims, dtype=BF16):
    return jax.ShapeDtypeStruct(dims, dtype)


def swap_halves(block):
    return jnp.concatenate([block[:, HEAD_DIM:], block[:, :HEAD_DIM]], axis=1)


def parts3(value):
    high = value.astype(BF16)
    rest = value - high.astype(F32)
    middle = rest.astype(BF16)
    low = (rest - middle.astype(F32)).astype(BF16)
    return high, middle, low


def pack_kernel(core_ref, proj_ref, outw_ref, packed_ref):
    for core in range(2):

        @pl.when(core_ref[0] == core)
        def _():
            for head in range(HALF):
                col = (core * HALF + head) * HEAD_DIM
                lanes = slice(head * 128, head * 128 + 128)
                keys = proj_ref[:, INNER + col : INNER + col + HEAD_DIM].astype(F32)
                values = proj_ref[:, 2 * INNER + col : 2 * INNER + col + HEAD_DIM].astype(F32)
                queries = proj_ref[:, col : col + HEAD_DIM].astype(F32)
                packed_ref[0:96, lanes] = jnp.concatenate([keys, values], axis=1).astype(BF16)
                packed_ref[96:144, lanes] = jnp.concatenate(
                    [queries[:48], queries[48:]], axis=1
                ).astype(BF16)
            packed_ref[144:192, :] = outw_ref[:, core * INNER : (core + 1) * INNER]


def pack_weights(core, projection, output_weight):
    return call(pack_kernel, shape_of(192, INNER), [SMEM, VMEM, VMEM], limit=60 * 1024 * 1024)(
        core, projection, output_weight
    )


def fan_kernel(own_ref, other_ref, both_ref):
    for peer in range(DP_X):
        both_ref[peer, 0] = own_ref[...]
        both_ref[peer, 1] = other_ref[...]


def gather_weights(core, projection, output_weight):
    packed = pack_weights(core, projection, output_weight)
    other = lax.ppermute(packed, "yh", [(0, 1), (1, 0)])
    both = call(fan_kernel, shape_of(DP_X, DP_Y, 192, INNER), [VMEM, VMEM], limit=60 * 1024 * 1024)(
        packed, other
    )
    got = lax.all_to_all(both, "x", 0, 0, tiled=True)
    return got.reshape(DP_X * DP_Y, 192, INNER)


def norm_kernel(base_ref, x_ref, gain_ref, perm_ref, out_ref, order_ref):
    gain = gain_ref[...].reshape(1, D)
    for row in range(0, TOK, 128):
        values = x_ref[row : row + 128, :].astype(F32)
        average = jnp.mean(values, axis=-1, keepdims=True)
        centred = values - average
        variance = jnp.mean(centred * centred, axis=-1, keepdims=True)
        out_ref[row : row + 128, :] = (
            centred * lax.rsqrt(variance + eps_norm) * gain
        ).astype(BF16)
    order_ref[...] = (perm_ref[...] - base_ref[1]).astype(F32)
    local = jnp.broadcast_to(perm_ref[...] - base_ref[1], (16, TOK))
    row = lax.broadcasted_iota(jnp.int32, (16, TOK), 0)
    parts = jnp.where(row == 0, jnp.right_shift(local, 4), jnp.bitwise_and(local, 15))
    out_ref[TOK : TOK + 16, 0:TOK] = parts.astype(F32).astype(BF16)
    out_ref[TOK : TOK + 16, TOK:] = jnp.zeros((16, D - TOK), BF16)


def order_of(x_ref):
    parts = x_ref[TOK : TOK + 16, 0:TOK].astype(F32)
    return parts[0:1, :] * 16.0 + parts[1:2, :]


def chosen_rows(view, offset, order):
    rows = lax.broadcasted_iota(jnp.int32, (SPARSE, 1), 0) * RATIO + offset
    if view == 0:
        return rows
    lane = lax.broadcasted_iota(jnp.int32, (SPARSE, TOK), 1)
    tiles = jnp.broadcast_to(order, (SPARSE, TOK))
    picked = jnp.sum(jnp.where(lane == rows, tiles, 0.0), axis=1, keepdims=True)
    return picked.astype(jnp.int32)


def one_hot(index, width):
    token = lax.broadcasted_iota(jnp.int32, (index.shape[0], width), 1)
    return jnp.where(token == index, 1.0, 0.0).astype(BF16)


def pick_kernel(base_ref, offset_ref, own_x, other_x, picked_ref):
    orders = order_of(own_x), order_of(other_x)
    hots = [[], []]
    for head in range(HALF):
        offset = offset_ref[base_ref[0] * HALF + head]
        for view in range(2):
            for part in range(2):
                chosen = one_hot(chosen_rows(view, offset, orders[part]), TOK)
                hots[part].append(chosen)
    for part, x_ref in enumerate((own_x, other_x)):
        rows = jnp.dot(
            jnp.concatenate(hots[part], axis=0), x_ref[0:TOK, :], preferred_element_type=F32
        ).astype(BF16)
        for block in range(2 * HALF):
            at = block * 2 * SPARSE + part * SPARSE
            picked_ref[at : at + SPARSE, :] = rows[block * SPARSE : block * SPARSE + SPARSE]


def unpack_head(flip, packed_ref, lanes, w_ref, at):
    lane = lax.broadcasted_iota(jnp.int32, (48, 128), 1)
    for entry in range(8):
        shard = (entry - entry % 2) + (entry % 2 ^ flip)
        row = pl.multiple_of(shard * 96, 16)
        w_ref[pl.ds(row, 96), at : at + 128] = packed_ref[entry, 0:96, lanes]
        folded = packed_ref[entry, 96:144, lanes].astype(F32)
        for first, part in ((0, folded), (48, swap_halves(folded))):
            w_ref[pl.ds(pl.multiple_of(row + first, 16), 48), at + 128 : at + 256] = jnp.where(
                lane < HEAD_DIM, part, 0.0
            ).astype(BF16)


def send_kernel(base_ref, picked_ref, packed_ref, send_ref, w_ref):
    for head in range(HALF):
        at = head * 256
        unpack_head(base_ref[3], packed_ref, slice(head * 128, head * 128 + 128), w_ref, at)
        far_rows = jnp.dot(
            picked_ref[head * 128 : head * 128 + 128, :],
            w_ref[:, at : at + 256],
            preferred_element_type=F32,
        ).astype(BF16)
        far_kv, far_q = far_rows[:, 0:128], far_rows[:, 128:256].astype(F32)
        for view in range(2):
            pair = (view * HALF + head) * 4
            for q_part in range(2):
                row = view * 2 * SPARSE + q_part * 16
                folded = (
                    far_q[row : row + 16] + swap_halves(far_q[SPARSE + row : SPARSE + row + 16])
                ).astype(BF16)
                for k_half in range(2):
                    peer = pair + q_part * 2 + k_half
                    first = view * 2 * SPARSE + k_half * SPARSE
                    send_ref[peer, 0:32, :] = far_kv[first : first + SPARSE]
                    send_ref[peer, 32:48, :] = folded
    for peer in range(4 * 2 * HALF, POS):
        send_ref[peer] = jnp.zeros((48, 128), BF16)


def near_kernel(base_ref, own_x, other_x, packed_ref, keep_ref, give_ref, outw_ref, w_ref, all_ref):
    flip = base_ref[3]

    @pl.when(pl.program_id(0) == 0)
    def _():
        for entry in range(8):
            shard = (entry - entry % 2) + (entry % 2 ^ flip)
            outw_ref[pl.ds(pl.multiple_of(shard * 48, 16), 48), :] = packed_ref[entry, 144:192, :]

    lanes = pl.ds(pl.multiple_of(pl.program_id(0) * 128, 128), 128)
    unpack_head(flip, packed_ref, lanes, w_ref, 0)
    for part, x_ref in enumerate((own_x, other_x)):
        all_ref[part * TOK : part * TOK + TOK, :] = jnp.dot(
            x_ref[0:TOK, :], w_ref[...], preferred_element_type=F32
        ).astype(BF16)
    keys = all_ref[:, 0:128]
    lane = lax.broadcasted_iota(jnp.int32, (SEG, 128), 1)
    values = jnp.where(lane < HEAD_DIM, swap_halves(keys.astype(F32)), 1.0).astype(BF16)
    tile = NEAR_TILE
    out_lane = lax.broadcasted_iota(jnp.int32, (tile, 128), 1)
    for at in range(0, SEG, tile):
        scores = lax.dot_general(
            all_ref[at : at + tile, 128:256],
            keys,
            (((1,), (1,)), ((), ())),
            preferred_element_type=F32,
        )
        row_max = jnp.max(scores, axis=1, keepdims=True)
        weights = jnp.exp2((scores - row_max) * EXP_SCALE).astype(BF16)
        summed = jnp.dot(weights, values, preferred_element_type=F32)
        result = jnp.where(
            out_lane < HEAD_DIM, summed / swap_halves(summed), row_max * SCALE + jnp.log(summed)
        )
        if tile == SEG:
            keep_ref[...] = result[:TOK]
            give_ref[...] = result[TOK:]
        else:
            out_ref = keep_ref if at < TOK else give_ref
            out_ref[at % TOK : at % TOK + tile, :] = result


def near_level(base, own_x, other_x, packed):
    half = shape_of(TOK, HALF * 128, dtype=F32)
    tiles = pl.BlockSpec((TOK + 16, D), lambda h: (0, 0))
    part = pl.BlockSpec((TOK, 128), lambda h: (0, h))
    return pl.pallas_call(
        near_kernel,
        out_shape=[half, half, shape_of(INNER, INNER)],
        grid=(HALF,),
        in_specs=[SMEM, tiles, tiles, pl.BlockSpec((8, 192, INNER), lambda h: (0, 0, 0))],
        out_specs=[part, part, pl.BlockSpec((INNER, INNER), lambda h: (0, 0))],
        scratch_shapes=[pltpu.VMEM((D, 256), BF16), pltpu.VMEM((SEG, 256), BF16)],
        cost_estimate=pl.CostEstimate(
            flops=4 * HALF * SEG * SEG * 128, bytes_accessed=5 << 20, transcendentals=HALF * SEG * SEG
        ),
        compiler_params=pltpu.CompilerParams(vmem_limit_bytes=LIMITS[1]),
        interpret=INTERPRET,
    )(base, own_x, other_x, packed)


def far_kernel(core_ref, got_ref, back_ref):
    core = core_ref[0]
    keys = got_ref[:, 0:32, :].reshape(POS * 32, 128)
    wide = got_ref[:, 32:48, :].reshape(POS * 16, 128).astype(F32)
    lane = lax.broadcasted_iota(jnp.int32, (POS * 32, 128), 1)
    values = jnp.where(lane < HEAD_DIM, swap_halves(keys.astype(F32)), 1.0).astype(BF16)
    q_lane = lax.broadcasted_iota(jnp.int32, (POS * 16, 128), 1)
    q_row = lax.broadcasted_iota(jnp.int32, (POS * 16, 128), 0)
    place = jnp.right_shift(q_lane, 4)
    mine = jnp.bitwise_and(q_lane, 15) == jnp.bitwise_and(q_row, 15)
    source = lax.broadcasted_iota(jnp.int32, (POS, POS * 16), 0)
    member = jnp.right_shift(lax.broadcasted_iota(jnp.int32, (POS, POS * 16), 1), 4)
    spread = jnp.where(source == member, 1.0, 0.0).astype(BF16)
    queries = jnp.concatenate(
        [jnp.where(q_lane < HEAD_DIM, part, 0.0) for part in (wide, swap_halves(wide))], axis=0
    ).astype(BF16)
    scores = lax.dot_general(queries, keys, (((1,), (1,)), ((), ())), preferred_element_type=F32)
    row_max = jnp.max(scores, axis=1, keepdims=True)
    weights = jnp.exp2((scores - row_max) * EXP_SCALE).astype(BF16)
    summed = jnp.dot(weights, values, preferred_element_type=F32)
    swapped = swap_halves(summed)
    outs = summed / swapped
    logs = row_max * SCALE + jnp.log(swapped)
    for part in range(2):
        rows = slice(part * POS * 16, (part + 1) * POS * 16)
        out = outs[rows].reshape(POS, 16, 128)
        packed = jnp.concatenate([out[:, 0:8, :HEAD_DIM], out[:, 8:16, :HEAD_DIM]], axis=2)
        high, middle, low = parts3(logs[rows])
        stats = jnp.where(
            place == 0, high, jnp.where(place == 1, middle, jnp.where(place == 2, low, 0.0))
        )
        stats = jnp.where(mine, stats, 0.0).astype(BF16)
        means = jnp.dot(spread, stats, preferred_element_type=F32)
        means = jnp.broadcast_to(means[:, None, :], (POS, 8, 128))
        block = jnp.concatenate([packed, means], axis=1).astype(BF16)
        back_ref[:, pl.ds(core if part == 0 else 1 - core, 1)] = block[:, None]


def prepare_kernel(
    base_ref, offset_ref, keep_ref, got_ref, order_ref, gain_ref,
    dense_ref, rows_ref, spread_ref, scale_ref,
):
    core = base_ref[0]
    width = HALF * HEAD_DIM
    hots = [[], []]
    order = order_ref[...]
    for group, near_ref in enumerate((keep_ref, got_ref)):
        dense_ref[:, group * width : (group + 1) * width] = jnp.concatenate(
            [near_ref[:, head * 128 : head * 128 + HEAD_DIM] for head in range(HALF)], axis=1
        )
        heads = core if group == 0 else 1 - core
        for head in range(HALF):
            pieces = jnp.concatenate(parts3(near_ref[:, head * 128 : head * 128 + 128]), axis=1)
            offset = offset_ref[heads * HALF + head]
            for view in range(2):
                chosen = one_hot(chosen_rows(view, offset, order), TOK)
                hots[view].append(chosen)
                taken = jnp.dot(chosen, pieces, preferred_element_type=F32)
                at = group * 192 + (view * HALF + head) * SPARSE
                rows_ref[at : at + SPARSE, :] = taken[:, :128] + taken[:, 128:256] + taken[:, 256:]
    hots = [jnp.concatenate(part, axis=0) for part in hots]
    for at, part in enumerate(
        (hots[0][:128], jnp.concatenate([hots[0][128:], hots[1][128:]], axis=0), hots[1][:128])
    ):
        spread_ref[:, at * 128 : at * 128 + 128] = part.astype(F32).T.astype(BF16)
    gain = gain_ref[...].reshape(1, INNER)
    scale_ref[...] = jnp.where(
        core == 0, gain, jnp.concatenate([gain[:, width:], gain[:, :width]], axis=1)
    )


def output_kernel(
    core_ref, far_ref, dense_ref, rows_ref, spread_ref, gain_ref, own_w, other_w, plain_out, flip_out,
    plain_ref, flip_ref, sems,
):
    core = core_ref[0]
    lane = lax.broadcasted_iota(jnp.int32, (192, 128), 1)
    mine = jnp.bitwise_and(lane, 15) == jnp.bitwise_and(
        lax.broadcasted_iota(jnp.int32, (192, 128), 0), 15
    )
    deltas = []
    for group in range(2):
        outs, logs = [], []
        for k_half in range(2):
            blocks, stats = [], []
            for pair in range(2 * HALF):
                for q_part in range(2):
                    peer = (pair * 4 + q_part * 2 + k_half) * 2
                    block = far_ref[peer + (core if group == 0 else 1 - core)].astype(F32)
                    blocks += [block[0:8, :HEAD_DIM], block[0:8, HEAD_DIM:]]
                    stats += [block[8:16], block[8:16]]
            outs.append(jnp.concatenate(blocks, axis=0))
            found = jnp.where(mine, jnp.concatenate(stats, axis=0), 0.0)
            logs.append(jnp.sum(found, axis=1, keepdims=True))
        top = jnp.maximum(logs[0], logs[1])
        weight0, weight1 = jnp.exp(logs[0] - top), jnp.exp(logs[1] - top)
        joint = weight0 + weight1
        far = (weight0 * outs[0] + weight1 * outs[1]) / joint
        near = rows_ref[group * 192 : group * 192 + 192, :]
        gap = near[:, HEAD_DIM : HEAD_DIM + 1] - (top + jnp.log(joint))
        deltas.append((far - near[:, :HEAD_DIM]) / (1.0 + jnp.exp(gap)))
    width = HALF * HEAD_DIM
    row = jnp.right_shift(lax.broadcasted_iota(jnp.int32, (192, INNER), 0), 5)
    col = jnp.right_shift(lax.broadcasted_iota(jnp.int32, (192, INNER), 1), 6)
    none = jnp.zeros((HEAD_DIM, INNER), BF16)
    own_rows = pl.ds(pl.multiple_of(core * width, 64), width)
    other_rows = pl.ds(pl.multiple_of((1 - core) * width, 64), width)
    weights = [
        jnp.concatenate([part[own_rows, :], part[other_rows, :]], axis=0) for part in (own_w, other_w)
    ]
    copies = []
    for view, (out_ref, hbm_ref) in enumerate(((plain_ref, plain_out), (flip_ref, flip_out))):
        delta = jnp.concatenate([d[view * 96 : view * 96 + 96] for d in deltas], axis=0)
        blocks = jnp.where(row == col, jnp.concatenate([delta] * HEADS, axis=1), 0.0).astype(BF16)
        if view == 0:
            blocks = jnp.concatenate([blocks, none], axis=0)
        else:
            blocks = jnp.concatenate([none, blocks[128:], blocks[:128]], axis=0)
        for at in range(0, TOK, 256):
            attended = dense_ref[at : at + 256, :] + jnp.dot(
                spread_ref[at : at + 256, view * 128 : view * 128 + 256],
                blocks,
                preferred_element_type=F32,
            )
            average = jnp.mean(attended, axis=-1, keepdims=True)
            centred = attended - average
            variance = jnp.mean(centred * centred, axis=-1, keepdims=True)
            mixed = (centred * lax.rsqrt(variance + eps_norm) * gain_ref[...]).astype(BF16)
            for part, place in zip(weights, (core, 1 - core)):
                out_ref[at : at + 256, pl.ds(pl.multiple_of(place * INNER, 128), INNER)] = jnp.dot(
                    mixed, part, preferred_element_type=F32
                ).astype(BF16)
            rows = pl.ds(at, 256)
            copies.append(
                pltpu.make_async_copy(
                    out_ref.at[rows], hbm_ref.at[rows], sems.at[view * 2 + at // 256]
                )
            )
            copies[-1].start()
    for copy in copies:
        copy.wait()


def core_swap(block):
    return lax.ppermute(block, "core", [(0, 1), (1, 0)])


def layer(
    tile_features, flip_perm, head_offsets, input_gain, projection, output_gain, output_weight
):
    core = lax.axis_index("core").astype(jnp.int32)
    pos = lax.axis_index("pos").astype(jnp.int32)
    rank = pos * 2 + core
    core_id = core[None]
    base = jnp.stack([core, rank * TOK, (rank ^ 1) * TOK, lax.axis_index("yh").astype(jnp.int32)])

    last = 2 * POS - 1
    ctx = ("pos", "core")
    own_perm = lax.ppermute(flip_perm, ctx, [(last - r, r) for r in range(2 * POS)])
    packed = gather_weights(core_id, projection, output_weight)
    own_x, own_order = call(
        norm_kernel,
        [shape_of(TOK + 16, D), shape_of(1, TOK, dtype=F32)],
        [SMEM, VMEM, VMEM, VMEM],
        moved=2 << 20,
    )(base, tile_features[0], input_gain, own_perm)
    other_x = core_swap(own_x)

    picked = call(
        pick_kernel,
        shape_of(HALF * 128, D),
        [SMEM, SMEM, VMEM, VMEM],
        flops=2 * HALF * 128 * SEG * D,
        moved=3 << 20,
    )(base, head_offsets, own_x, other_x)
    send = call(
        send_kernel,
        shape_of(POS, 48, 128),
        [SMEM, VMEM, VMEM],
        [pltpu.VMEM((D, D), BF16)],
        flops=2 * HALF * 128 * D * 256,
        moved=2 << 20,
        limit=LIMITS[0],
    )(base, picked, packed)

    got = lax.all_to_all(send, "pos", 0, 0, tiled=True)
    keep, give, own_w = near_level(base, own_x, other_x, packed)
    near_got = core_swap(give)
    back = call(
        far_kernel, shape_of(POS, 2, 16, 128), [SMEM, VMEM], flops=4 * SEG * SEG * 128, moved=1 << 20,
        limit=LIMITS[2],
    )(core_id, got)
    far = lax.all_to_all(back.reshape(2 * POS, 16, 128), ctx, 0, 0, tiled=True)

    other_w = core_swap(own_w)
    prepared = call(
        prepare_kernel,
        [
            shape_of(TOK, INNER, dtype=F32),
            shape_of(INNER, 128, dtype=F32),
            shape_of(TOK, INNER),
            shape_of(1, INNER, dtype=F32),
        ],
        [SMEM, SMEM, VMEM, VMEM, VMEM, VMEM],
        flops=1 << 28,
        moved=4 << 20,
        limit=LIMITS[3],
    )(base, head_offsets, keep, near_got, own_order, output_gain)

    plain_view, flipped_view = call(
        output_kernel,
        [shape_of(TOK, D), shape_of(TOK, D)],
        [SMEM] + [VMEM] * 7,
        [pltpu.VMEM((TOK, D), BF16), pltpu.VMEM((TOK, D), BF16), pltpu.SemaphoreType.DMA((4,))],
        outs=[ANY, ANY],
        flops=4 * SEG * INNER * D,
        moved=4 << 20,
        limit=LIMITS[4],
    )(core_id, far, *prepared, own_w, other_w)
    return (plain_view[None], flipped_view[None])


def solution(mesh):
    fine = Mesh(mesh.devices.reshape(DP_X, DP_Y, POS, 2), ("x", "yh", "pos", "core"))
    dp, ctx = ("x", "yh"), ("pos", "core")
    placed = (P(dp, ctx, None), P(dp, ctx), P(), P(), P(dp, None), P(), P(dp, None))
    return jax.shard_map(
        layer,
        mesh=fine,
        in_specs=placed,
        out_specs=(P(dp, ctx, None), P(dp, ctx, None)),
        check_vma=False,
    )
```

```python
import jax
import jax.numpy as jnp
from jax import lax
from jax.experimental import pallas as pl
from jax.experimental.pallas import tpu as pltpu
from jax.sharding import Mesh, PartitionSpec as P


HEADS = 6
HEAD_DIM = 64
INNER = 384
D = 768
RATIO = 16
TOK = 512
SEG = 1024
HALF = 3
SPARSE = TOK // RATIO
POS = 32
DP_X, DP_Y = 4, 2
INTERPRET = False
NEAR_TILE = 512
LIMITS = [24 << 20, 60 * 1024 * 1024, 24 << 20, 24 << 20, 24 << 20]

eps_norm = 1e-05
EXP_SCALE = HEAD_DIM ** (-0.5) * 1.4426950408889634
SCALE = HEAD_DIM ** (-0.5)

F32 = jnp.float32
BF16 = jnp.bfloat16
VMEM = pl.BlockSpec(memory_space=pltpu.VMEM)
SMEM = pl.BlockSpec(memory_space=pltpu.SMEM)
ANY = pl.BlockSpec(memory_space=pl.ANY)


def call(kernel, out_shape, specs, scratch=(), flops=0, moved=0, limit=24 << 20, outs=None):
    single = not isinstance(out_shape, (list, tuple))
    return pl.pallas_call(
        kernel,
        out_shape=out_shape,
        in_specs=specs,
        out_specs=outs or (VMEM if single else [VMEM] * len(out_shape)),
        scratch_shapes=list(scratch),
        cost_estimate=pl.CostEstimate(flops=flops, bytes_accessed=moved, transcendentals=0),
        compiler_params=pltpu.CompilerParams(vmem_limit_bytes=limit),
        interpret=INTERPRET,
    )


def shape_of(*dims, dtype=BF16):
    return jax.ShapeDtypeStruct(dims, dtype)


def swap_halves(block):
    return jnp.concatenate([block[:, HEAD_DIM:], block[:, :HEAD_DIM]], axis=1)


def parts3(value):
    high = value.astype(BF16)
    rest = value - high.astype(F32)
    middle = rest.astype(BF16)
    low = (rest - middle.astype(F32)).astype(BF16)
    return high, middle, low


def pack_kernel(core_ref, proj_ref, outw_ref, packed_ref):
    for core in range(2):

        @pl.when(core_ref[0] == core)
        def _():
            for head in range(HALF):
                col = (core * HALF + head) * HEAD_DIM
                lanes = slice(head * 128, head * 128 + 128)
                keys = proj_ref[:, INNER + col : INNER + col + HEAD_DIM].astype(F32)
                values = proj_ref[:, 2 * INNER + col : 2 * INNER + col + HEAD_DIM].astype(F32)
                queries = proj_ref[:, col : col + HEAD_DIM].astype(F32)
                packed_ref[0:96, lanes] = jnp.concatenate([keys, values], axis=1).astype(BF16)
                packed_ref[96:144, lanes] = jnp.concatenate(
                    [queries[:48], queries[48:]], axis=1
                ).astype(BF16)
            packed_ref[144:192, :] = outw_ref[:, core * INNER : (core + 1) * INNER]


def pack_weights(core, projection, output_weight):
    return call(pack_kernel, shape_of(192, INNER), [SMEM, VMEM, VMEM])(
        core, projection, output_weight
    )


def fan_kernel(own_ref, other_ref, both_ref, sems):
    copies = []
    for peer in range(DP_X):
        for at, part in enumerate((own_ref, other_ref)):
            copies.append(
                pltpu.make_async_copy(part, both_ref.at[peer, at], sems.at[peer * 2 + at])
            )
            copies[-1].start()
    for copy in copies:
        copy.wait()


def gather_weights(core, projection, output_weight):
    packed = pack_weights(core, projection, output_weight)
    other = lax.ppermute(packed, "yh", [(0, 1), (1, 0)])
    both = call(
        fan_kernel,
        shape_of(DP_X, DP_Y, 192, INNER),
        [VMEM, VMEM],
        [pltpu.SemaphoreType.DMA((2 * DP_X,))],
        outs=ANY,
    )(packed, other)
    got = lax.all_to_all(both, "x", 0, 0, tiled=True)
    return got.reshape(DP_X * DP_Y, 192, INNER)


def norm_kernel(base_ref, x_ref, gain_ref, perm_ref, out_ref, order_ref):
    gain = gain_ref[...].reshape(1, D)
    for row in range(0, TOK, 128):
        values = x_ref[row : row + 128, :].astype(F32)
        average = jnp.mean(values, axis=-1, keepdims=True)
        centred = values - average
        variance = jnp.mean(centred * centred, axis=-1, keepdims=True)
        out_ref[row : row + 128, :] = (
            centred * lax.rsqrt(variance + eps_norm) * gain
        ).astype(BF16)
    order_ref[...] = (perm_ref[...] - base_ref[1]).astype(F32)
    local = jnp.broadcast_to(perm_ref[...] - base_ref[1], (16, TOK))
    row = lax.broadcasted_iota(jnp.int32, (16, TOK), 0)
    parts = jnp.where(row == 0, jnp.right_shift(local, 4), jnp.bitwise_and(local, 15))
    out_ref[TOK : TOK + 16, 0:TOK] = parts.astype(F32).astype(BF16)
    out_ref[TOK : TOK + 16, TOK:] = jnp.zeros((16, D - TOK), BF16)


def order_of(x_ref):
    parts = x_ref[TOK : TOK + 16, 0:TOK].astype(F32)
    return parts[0:1, :] * 16.0 + parts[1:2, :]


def chosen_rows(view, offset, order):
    rows = lax.broadcasted_iota(jnp.int32, (SPARSE, 1), 0) * RATIO + offset
    if view == 0:
        return rows
    lane = lax.broadcasted_iota(jnp.int32, (SPARSE, TOK), 1)
    tiles = jnp.broadcast_to(order, (SPARSE, TOK))
    picked = jnp.sum(jnp.where(lane == rows, tiles, 0.0), axis=1, keepdims=True)
    return picked.astype(jnp.int32)


def one_hot(index, width):
    token = lax.broadcasted_iota(jnp.int32, (index.shape[0], width), 1)
    return jnp.where(token == index, 1.0, 0.0).astype(BF16)


def pick_kernel(base_ref, offset_ref, own_x, other_x, picked_ref):
    orders = order_of(own_x), order_of(other_x)
    hots = [[], []]
    for head in range(HALF):
        offset = offset_ref[base_ref[0] * HALF + head]
        for view in range(2):
            for part in range(2):
                chosen = one_hot(chosen_rows(view, offset, orders[part]), TOK)
                hots[part].append(chosen)
    for part, x_ref in enumerate((own_x, other_x)):
        rows = jnp.dot(
            jnp.concatenate(hots[part], axis=0), x_ref[0:TOK, :], preferred_element_type=F32
        ).astype(BF16)
        for block in range(2 * HALF):
            at = block * 2 * SPARSE + part * SPARSE
            picked_ref[at : at + SPARSE, :] = rows[block * SPARSE : block * SPARSE + SPARSE]


def unpack_head(flip, packed_ref, lanes, w_ref, at):
    lane = lax.broadcasted_iota(jnp.int32, (48, 128), 1)
    for entry in range(8):
        shard = (entry - entry % 2) + (entry % 2 ^ flip)
        row = pl.multiple_of(shard * 96, 16)
        w_ref[pl.ds(row, 96), at : at + 128] = packed_ref[entry, 0:96, lanes]
        folded = packed_ref[entry, 96:144, lanes].astype(F32)
        for first, part in ((0, folded), (48, swap_halves(folded))):
            w_ref[pl.ds(pl.multiple_of(row + first, 16), 48), at + 128 : at + 256] = jnp.where(
                lane < HEAD_DIM, part, 0.0
            ).astype(BF16)


def send_kernel(base_ref, picked_ref, packed_ref, send_ref, w_ref):
    for head in range(HALF):
        at = head * 256
        unpack_head(base_ref[3], packed_ref, slice(head * 128, head * 128 + 128), w_ref, at)
        far_rows = jnp.dot(
            picked_ref[head * 128 : head * 128 + 128, :],
            w_ref[:, at : at + 256],
            preferred_element_type=F32,
        ).astype(BF16)
        far_kv, far_q = far_rows[:, 0:128], far_rows[:, 128:256].astype(F32)
        for view in range(2):
            pair = (view * HALF + head) * 4
            for q_part in range(2):
                row = view * 2 * SPARSE + q_part * 16
                folded = (
                    far_q[row : row + 16] + swap_halves(far_q[SPARSE + row : SPARSE + row + 16])
                ).astype(BF16)
                for k_half in range(2):
                    peer = pair + q_part * 2 + k_half
                    first = view * 2 * SPARSE + k_half * SPARSE
                    send_ref[peer, 0:32, :] = far_kv[first : first + SPARSE]
                    send_ref[peer, 32:48, :] = folded
    for peer in range(4 * 2 * HALF, POS):
        send_ref[peer] = jnp.zeros((48, 128), BF16)


def near_kernel(base_ref, own_x, other_x, packed_ref, keep_ref, give_ref, outw_ref, w_ref, all_ref):
    flip = base_ref[3]

    @pl.when(pl.program_id(0) == 0)
    def _():
        for entry in range(8):
            shard = (entry - entry % 2) + (entry % 2 ^ flip)
            outw_ref[pl.ds(pl.multiple_of(shard * 48, 16), 48), :] = packed_ref[entry, 144:192, :]

    lanes = pl.ds(pl.multiple_of(pl.program_id(0) * 128, 128), 128)
    unpack_head(flip, packed_ref, lanes, w_ref, 0)
    for part, x_ref in enumerate((own_x, other_x)):
        all_ref[part * TOK : part * TOK + TOK, :] = jnp.dot(
            x_ref[0:TOK, :], w_ref[...], preferred_element_type=F32
        ).astype(BF16)
    keys = all_ref[:, 0:128]
    lane = lax.broadcasted_iota(jnp.int32, (SEG, 128), 1)
    values = jnp.where(lane < HEAD_DIM, swap_halves(keys.astype(F32)), 1.0).astype(BF16)
    tile = NEAR_TILE
    out_lane = lax.broadcasted_iota(jnp.int32, (tile, 128), 1)
    for at in range(0, SEG, tile):
        scores = lax.dot_general(
            all_ref[at : at + tile, 128:256],
            keys,
            (((1,), (1,)), ((), ())),
            preferred_element_type=F32,
        )
        row_max = jnp.max(scores, axis=1, keepdims=True)
        weights = jnp.exp2((scores - row_max) * EXP_SCALE).astype(BF16)
        summed = jnp.dot(weights, values, preferred_element_type=F32)
        result = jnp.where(
            out_lane < HEAD_DIM, summed / swap_halves(summed), row_max * SCALE + jnp.log(summed)
        )
        if tile == SEG:
            keep_ref[...] = result[:TOK]
            give_ref[...] = result[TOK:]
        else:
            out_ref = keep_ref if at < TOK else give_ref
            out_ref[at % TOK : at % TOK + tile, :] = result


def near_level(base, own_x, other_x, packed):
    half = shape_of(TOK, HALF * 128, dtype=F32)
    tiles = pl.BlockSpec((TOK + 16, D), lambda h: (0, 0))
    part = pl.BlockSpec((TOK, 128), lambda h: (0, h))
    return pl.pallas_call(
        near_kernel,
        out_shape=[half, half, shape_of(INNER, INNER)],
        grid=(HALF,),
        in_specs=[SMEM, tiles, tiles, pl.BlockSpec((8, 192, INNER), lambda h: (0, 0, 0))],
        out_specs=[part, part, pl.BlockSpec((INNER, INNER), lambda h: (0, 0))],
        scratch_shapes=[pltpu.VMEM((D, 256), BF16), pltpu.VMEM((SEG, 256), BF16)],
        cost_estimate=pl.CostEstimate(
            flops=4 * HALF * SEG * SEG * 128, bytes_accessed=5 << 20, transcendentals=HALF * SEG * SEG
        ),
        compiler_params=pltpu.CompilerParams(vmem_limit_bytes=LIMITS[1]),
        interpret=INTERPRET,
    )(base, own_x, other_x, packed)


def far_kernel(core_ref, got_ref, back_ref):
    core = core_ref[0]
    keys = got_ref[:, 0:32, :].reshape(POS * 32, 128)
    wide = got_ref[:, 32:48, :].reshape(POS * 16, 128).astype(F32)
    lane = lax.broadcasted_iota(jnp.int32, (POS * 32, 128), 1)
    values = jnp.where(lane < HEAD_DIM, swap_halves(keys.astype(F32)), 1.0).astype(BF16)
    q_lane = lax.broadcasted_iota(jnp.int32, (POS * 16, 128), 1)
    q_row = lax.broadcasted_iota(jnp.int32, (POS * 16, 128), 0)
    place = jnp.right_shift(q_lane, 4)
    mine = jnp.bitwise_and(q_lane, 15) == jnp.bitwise_and(q_row, 15)
    source = lax.broadcasted_iota(jnp.int32, (POS, POS * 16), 0)
    member = jnp.right_shift(lax.broadcasted_iota(jnp.int32, (POS, POS * 16), 1), 4)
    spread = jnp.where(source == member, 1.0, 0.0).astype(BF16)
    queries = jnp.concatenate(
        [jnp.where(q_lane < HEAD_DIM, part, 0.0) for part in (wide, swap_halves(wide))], axis=0
    ).astype(BF16)
    scores = lax.dot_general(queries, keys, (((1,), (1,)), ((), ())), preferred_element_type=F32)
    row_max = jnp.max(scores, axis=1, keepdims=True)
    weights = jnp.exp2((scores - row_max) * EXP_SCALE).astype(BF16)
    summed = jnp.dot(weights, values, preferred_element_type=F32)
    swapped = swap_halves(summed)
    outs = summed / swapped
    logs = row_max * SCALE + jnp.log(swapped)
    for part in range(2):
        rows = slice(part * POS * 16, (part + 1) * POS * 16)
        out = outs[rows].reshape(POS, 16, 128)
        packed = jnp.concatenate([out[:, 0:8, :HEAD_DIM], out[:, 8:16, :HEAD_DIM]], axis=2)
        high, middle, low = parts3(logs[rows])
        stats = jnp.where(
            place == 0, high, jnp.where(place == 1, middle, jnp.where(place == 2, low, 0.0))
        )
        stats = jnp.where(mine, stats, 0.0).astype(BF16)
        means = jnp.dot(spread, stats, preferred_element_type=F32)
        means = jnp.broadcast_to(means[:, None, :], (POS, 8, 128))
        block = jnp.concatenate([packed, means], axis=1).astype(BF16)
        back_ref[:, pl.ds(core if part == 0 else 1 - core, 1)] = block[:, None]


def prepare_kernel(
    base_ref, offset_ref, keep_ref, got_ref, order_ref, gain_ref,
    dense_ref, rows_ref, spread_ref, scale_ref,
):
    core = base_ref[0]
    width = HALF * HEAD_DIM
    hots = [[], []]
    order = order_ref[...]
    for group, near_ref in enumerate((keep_ref, got_ref)):
        dense_ref[:, group * width : (group + 1) * width] = jnp.concatenate(
            [near_ref[:, head * 128 : head * 128 + HEAD_DIM] for head in range(HALF)], axis=1
        )
        heads = core if group == 0 else 1 - core
        for head in range(HALF):
            pieces = jnp.concatenate(parts3(near_ref[:, head * 128 : head * 128 + 128]), axis=1)
            offset = offset_ref[heads * HALF + head]
            for view in range(2):
                chosen = one_hot(chosen_rows(view, offset, order), TOK)
                hots[view].append(chosen)
                taken = jnp.dot(chosen, pieces, preferred_element_type=F32)
                at = group * 192 + (view * HALF + head) * SPARSE
                rows_ref[at : at + SPARSE, :] = taken[:, :128] + taken[:, 128:256] + taken[:, 256:]
    hots = [jnp.concatenate(part, axis=0) for part in hots]
    for at, part in enumerate(
        (hots[0][:128], jnp.concatenate([hots[0][128:], hots[1][128:]], axis=0), hots[1][:128])
    ):
        spread_ref[:, at * 128 : at * 128 + 128] = part.astype(F32).T.astype(BF16)
    gain = gain_ref[...].reshape(1, INNER)
    scale_ref[...] = jnp.where(
        core == 0, gain, jnp.concatenate([gain[:, width:], gain[:, :width]], axis=1)
    )


def output_kernel(
    core_ref, far_ref, dense_ref, rows_ref, spread_ref, gain_ref, own_w, other_w, plain_out, flip_out,
    plain_ref, flip_ref, sems,
):
    core = core_ref[0]
    lane = lax.broadcasted_iota(jnp.int32, (192, 128), 1)
    mine = jnp.bitwise_and(lane, 15) == jnp.bitwise_and(
        lax.broadcasted_iota(jnp.int32, (192, 128), 0), 15
    )
    deltas = []
    for group in range(2):
        outs, logs = [], []
        for k_half in range(2):
            blocks, stats = [], []
            for pair in range(2 * HALF):
                for q_part in range(2):
                    peer = (pair * 4 + q_part * 2 + k_half) * 2
                    block = far_ref[peer + (core if group == 0 else 1 - core)].astype(F32)
                    blocks += [block[0:8, :HEAD_DIM], block[0:8, HEAD_DIM:]]
                    stats += [block[8:16], block[8:16]]
            outs.append(jnp.concatenate(blocks, axis=0))
            found = jnp.where(mine, jnp.concatenate(stats, axis=0), 0.0)
            logs.append(jnp.sum(found, axis=1, keepdims=True))
        top = jnp.maximum(logs[0], logs[1])
        weight0, weight1 = jnp.exp(logs[0] - top), jnp.exp(logs[1] - top)
        joint = weight0 + weight1
        far = (weight0 * outs[0] + weight1 * outs[1]) / joint
        near = rows_ref[group * 192 : group * 192 + 192, :]
        gap = near[:, HEAD_DIM : HEAD_DIM + 1] - (top + jnp.log(joint))
        deltas.append((far - near[:, :HEAD_DIM]) / (1.0 + jnp.exp(gap)))
    width = HALF * HEAD_DIM
    row = jnp.right_shift(lax.broadcasted_iota(jnp.int32, (192, INNER), 0), 5)
    col = jnp.right_shift(lax.broadcasted_iota(jnp.int32, (192, INNER), 1), 6)
    none = jnp.zeros((HEAD_DIM, INNER), BF16)
    own_rows = pl.ds(pl.multiple_of(core * width, 64), width)
    other_rows = pl.ds(pl.multiple_of((1 - core) * width, 64), width)
    weights = [
        jnp.concatenate([part[own_rows, :], part[other_rows, :]], axis=0) for part in (own_w, other_w)
    ]
    copies = []
    for view, (out_ref, hbm_ref) in enumerate(((plain_ref, plain_out), (flip_ref, flip_out))):
        delta = jnp.concatenate([d[view * 96 : view * 96 + 96] for d in deltas], axis=0)
        blocks = jnp.where(row == col, jnp.concatenate([delta] * HEADS, axis=1), 0.0).astype(BF16)
        if view == 0:
            blocks = jnp.concatenate([blocks, none], axis=0)
        else:
            blocks = jnp.concatenate([none, blocks[128:], blocks[:128]], axis=0)
        for at in range(0, TOK, 256):
            attended = dense_ref[at : at + 256, :] + jnp.dot(
                spread_ref[at : at + 256, view * 128 : view * 128 + 256],
                blocks,
                preferred_element_type=F32,
            )
            average = jnp.mean(attended, axis=-1, keepdims=True)
            centred = attended - average
            variance = jnp.mean(centred * centred, axis=-1, keepdims=True)
            mixed = (centred * lax.rsqrt(variance + eps_norm) * gain_ref[...]).astype(BF16)
            for part, place in zip(weights, (core, 1 - core)):
                out_ref[at : at + 256, pl.ds(pl.multiple_of(place * INNER, 128), INNER)] = jnp.dot(
                    mixed, part, preferred_element_type=F32
                ).astype(BF16)
            rows = pl.ds(at, 256)
            copies.append(
                pltpu.make_async_copy(
                    out_ref.at[rows], hbm_ref.at[rows], sems.at[view * 2 + at // 256]
                )
            )
            copies[-1].start()
    for copy in copies:
        copy.wait()


def core_swap(block):
    return lax.ppermute(block, "core", [(0, 1), (1, 0)])


def layer(
    tile_features, flip_perm, head_offsets, input_gain, projection, output_gain, output_weight
):
    core = lax.axis_index("core").astype(jnp.int32)
    pos = lax.axis_index("pos").astype(jnp.int32)
    rank = pos * 2 + core
    core_id = core[None]
    base = jnp.stack([core, rank * TOK, (rank ^ 1) * TOK, lax.axis_index("yh").astype(jnp.int32)])

    last = 2 * POS - 1
    ctx = ("pos", "core")
    own_perm = lax.ppermute(flip_perm, ctx, [(last - r, r) for r in range(2 * POS)])
    packed = gather_weights(core_id, projection, output_weight)
    own_x, own_order = call(
        norm_kernel,
        [shape_of(TOK + 16, D), shape_of(1, TOK, dtype=F32)],
        [SMEM, VMEM, VMEM, VMEM],
        moved=2 << 20,
    )(base, tile_features[0], input_gain, own_perm)
    other_x = core_swap(own_x)

    picked = call(
        pick_kernel,
        shape_of(HALF * 128, D),
        [SMEM, SMEM, VMEM, VMEM],
        flops=2 * HALF * 128 * SEG * D,
        moved=3 << 20,
    )(base, head_offsets, own_x, other_x)
    send = call(
        send_kernel,
        shape_of(POS, 48, 128),
        [SMEM, VMEM, VMEM],
        [pltpu.VMEM((D, D), BF16)],
        flops=2 * HALF * 128 * D * 256,
        moved=2 << 20,
        limit=LIMITS[0],
    )(base, picked, packed)

    got = lax.all_to_all(send, "pos", 0, 0, tiled=True)
    keep, give, own_w = near_level(base, own_x, other_x, packed)
    near_got = core_swap(give)
    back = call(
        far_kernel, shape_of(POS, 2, 16, 128), [SMEM, VMEM], flops=4 * SEG * SEG * 128, moved=1 << 20,
        limit=LIMITS[2],
    )(core_id, got)
    far = lax.all_to_all(back.reshape(2 * POS, 16, 128), ctx, 0, 0, tiled=True)

    other_w = core_swap(own_w)
    prepared = call(
        prepare_kernel,
        [
            shape_of(TOK, INNER, dtype=F32),
            shape_of(INNER, 128, dtype=F32),
            shape_of(TOK, INNER),
            shape_of(1, INNER, dtype=F32),
        ],
        [SMEM, SMEM, VMEM, VMEM, VMEM, VMEM],
        flops=1 << 28,
        moved=4 << 20,
        limit=LIMITS[3],
    )(base, head_offsets, keep, near_got, own_order, output_gain)

    plain_view, flipped_view = call(
        output_kernel,
        [shape_of(TOK, D), shape_of(TOK, D)],
        [SMEM] + [VMEM] * 7,
        [pltpu.VMEM((TOK, D), BF16), pltpu.VMEM((TOK, D), BF16), pltpu.SemaphoreType.DMA((4,))],
        outs=[ANY, ANY],
        flops=4 * SEG * INNER * D,
        moved=4 << 20,
        limit=LIMITS[4],
    )(core_id, far, *prepared, own_w, other_w)
    return (plain_view[None], flipped_view[None])


def solution(mesh):
    fine = Mesh(mesh.devices.reshape(DP_X, DP_Y, POS, 2), ("x", "yh", "pos", "core"))
    dp, ctx = ("x", "yh"), ("pos", "core")
    placed = (P(dp, ctx, None), P(dp, ctx), P(), P(), P(dp, None), P(), P(dp, None))
    return jax.shard_map(
        layer,
        mesh=fine,
        in_specs=placed,
        out_specs=(P(dp, ctx, None), P(dp, ctx, None)),
        check_vma=False,
    )
```

```python
import jax
import jax.numpy as jnp
from jax import lax
from jax.experimental import pallas as pl
from jax.experimental.pallas import tpu as pltpu
from jax.sharding import Mesh, PartitionSpec as P


HEADS = 6
HEAD_DIM = 64
INNER = 384
D = 768
RATIO = 16
TOK = 512
SEG = 1024
HALF = 3
SPARSE = TOK // RATIO
POS = 32
DP_X, DP_Y = 4, 2
INTERPRET = False
NEAR_TILE = 512
LIMITS = [24 << 20, 60 * 1024 * 1024, 24 << 20, 24 << 20, 24 << 20]

eps_norm = 1e-05
EXP_SCALE = HEAD_DIM ** (-0.5) * 1.4426950408889634
SCALE = HEAD_DIM ** (-0.5)

F32 = jnp.float32
BF16 = jnp.bfloat16
VMEM = pl.BlockSpec(memory_space=pltpu.VMEM)
SMEM = pl.BlockSpec(memory_space=pltpu.SMEM)
ANY = pl.BlockSpec(memory_space=pl.ANY)


def call(kernel, out_shape, specs, scratch=(), flops=0, moved=0, limit=24 << 20, outs=None):
    single = not isinstance(out_shape, (list, tuple))
    return pl.pallas_call(
        kernel,
        out_shape=out_shape,
        in_specs=specs,
        out_specs=outs or (VMEM if single else [VMEM] * len(out_shape)),
        scratch_shapes=list(scratch),
        cost_estimate=pl.CostEstimate(flops=flops, bytes_accessed=moved, transcendentals=0),
        compiler_params=pltpu.CompilerParams(vmem_limit_bytes=limit),
        interpret=INTERPRET,
    )


def shape_of(*dims, dtype=BF16):
    return jax.ShapeDtypeStruct(dims, dtype)


def swap_halves(block):
    return jnp.concatenate([block[:, HEAD_DIM:], block[:, :HEAD_DIM]], axis=1)


def parts3(value):
    high = value.astype(BF16)
    rest = value - high.astype(F32)
    middle = rest.astype(BF16)
    low = (rest - middle.astype(F32)).astype(BF16)
    return high, middle, low


def pack_kernel(core_ref, proj_ref, outw_ref, packed_ref):
    for core in range(2):

        @pl.when(core_ref[0] == core)
        def _():
            for head in range(HALF):
                col = (core * HALF + head) * HEAD_DIM
                lanes = slice(head * 128, head * 128 + 128)
                keys = proj_ref[:, INNER + col : INNER + col + HEAD_DIM].astype(F32)
                values = proj_ref[:, 2 * INNER + col : 2 * INNER + col + HEAD_DIM].astype(F32)
                queries = proj_ref[:, col : col + HEAD_DIM].astype(F32)
                packed_ref[0:96, lanes] = jnp.concatenate([keys, values], axis=1).astype(BF16)
                packed_ref[96:144, lanes] = jnp.concatenate(
                    [queries[:48], queries[48:]], axis=1
                ).astype(BF16)
            packed_ref[144:192, :] = outw_ref[:, core * INNER : (core + 1) * INNER]


def pack_weights(core, projection, output_weight):
    return call(pack_kernel, shape_of(192, INNER), [SMEM, VMEM, VMEM])(
        core, projection, output_weight
    )


def fan_kernel(own_ref, other_ref, both_ref, sems):
    copies = []
    for peer in range(DP_X):
        for at, part in enumerate((own_ref, other_ref)):
            copies.append(
                pltpu.make_async_copy(part, both_ref.at[peer, at], sems.at[peer * 2 + at])
            )
            copies[-1].start()
    for copy in copies:
        copy.wait()


def gather_weights(core, projection, output_weight):
    packed = pack_weights(core, projection, output_weight)
    other = lax.ppermute(packed, "yh", [(0, 1), (1, 0)])
    both = call(
        fan_kernel,
        shape_of(DP_X, DP_Y, 192, INNER),
        [VMEM, VMEM],
        [pltpu.SemaphoreType.DMA((2 * DP_X,))],
        outs=ANY,
    )(packed, other)
    got = lax.all_to_all(both, "x", 0, 0, tiled=True)
    return got.reshape(DP_X * DP_Y, 192, INNER)


def norm_kernel(x_ref, gain_ref, out_ref):
    gain = gain_ref[...].reshape(1, D)
    for row in range(0, TOK, 128):
        values = x_ref[row : row + 128, :].astype(F32)
        average = jnp.mean(values, axis=-1, keepdims=True)
        centred = values - average
        variance = jnp.mean(centred * centred, axis=-1, keepdims=True)
        out_ref[row : row + 128, :] = (
            centred * lax.rsqrt(variance + eps_norm) * gain
        ).astype(BF16)


def chosen_rows(view, offset, order):
    rows = lax.broadcasted_iota(jnp.int32, (SPARSE, 1), 0) * RATIO + offset
    if view == 0:
        return rows
    lane = lax.broadcasted_iota(jnp.int32, (SPARSE, TOK), 1)
    tiles = jnp.broadcast_to(order, (SPARSE, TOK))
    picked = jnp.sum(jnp.where(lane == rows, tiles, 0.0), axis=1, keepdims=True)
    return picked.astype(jnp.int32)


def one_hot(index, width):
    token = lax.broadcasted_iota(jnp.int32, (index.shape[0], width), 1)
    return jnp.where(token == index, 1.0, 0.0).astype(BF16)


def pick_kernel(base_ref, offset_ref, own_x, other_x, own_perm, other_perm, picked_ref):
    orders = [
        (perm[...] - base_ref[at]).astype(F32) for at, perm in ((1, own_perm), (2, other_perm))
    ]
    hots = [[], []]
    for head in range(HALF):
        offset = offset_ref[base_ref[0] * HALF + head]
        for view in range(2):
            for part in range(2):
                chosen = one_hot(chosen_rows(view, offset, orders[part]), TOK)
                hots[part].append(chosen)
    for part, x_ref in enumerate((own_x, other_x)):
        rows = jnp.dot(
            jnp.concatenate(hots[part], axis=0), x_ref[...], preferred_element_type=F32
        ).astype(BF16)
        for block in range(2 * HALF):
            at = block * 2 * SPARSE + part * SPARSE
            picked_ref[at : at + SPARSE, :] = rows[block * SPARSE : block * SPARSE + SPARSE]


def unpack_head(flip, packed_ref, lanes, w_ref, at):
    lane = lax.broadcasted_iota(jnp.int32, (48, 128), 1)
    for entry in range(8):
        shard = (entry - entry % 2) + (entry % 2 ^ flip)
        row = pl.multiple_of(shard * 96, 16)
        w_ref[pl.ds(row, 96), at : at + 128] = packed_ref[entry, 0:96, lanes]
        folded = packed_ref[entry, 96:144, lanes].astype(F32)
        for first, part in ((0, folded), (48, swap_halves(folded))):
            w_ref[pl.ds(pl.multiple_of(row + first, 16), 48), at + 128 : at + 256] = jnp.where(
                lane < HEAD_DIM, part, 0.0
            ).astype(BF16)


def send_kernel(base_ref, picked_ref, packed_ref, send_ref, w_ref):
    for head in range(HALF):
        at = head * 256
        unpack_head(base_ref[3], packed_ref, slice(head * 128, head * 128 + 128), w_ref, at)
        far_rows = jnp.dot(
            picked_ref[head * 128 : head * 128 + 128, :],
            w_ref[:, at : at + 256],
            preferred_element_type=F32,
        ).astype(BF16)
        far_kv, far_q = far_rows[:, 0:128], far_rows[:, 128:256].astype(F32)
        for view in range(2):
            pair = (view * HALF + head) * 4
            for q_part in range(2):
                row = view * 2 * SPARSE + q_part * 16
                folded = (
                    far_q[row : row + 16] + swap_halves(far_q[SPARSE + row : SPARSE + row + 16])
                ).astype(BF16)
                for k_half in range(2):
                    peer = pair + q_part * 2 + k_half
                    first = view * 2 * SPARSE + k_half * SPARSE
                    send_ref[peer, 0:32, :] = far_kv[first : first + SPARSE]
                    send_ref[peer, 32:48, :] = folded
    for peer in range(4 * 2 * HALF, POS):
        send_ref[peer] = jnp.zeros((48, 128), BF16)


def near_kernel(base_ref, own_x, other_x, packed_ref, keep_ref, give_ref, outw_ref, w_ref, all_ref):
    flip = base_ref[3]

    @pl.when(pl.program_id(0) == 0)
    def _():
        for entry in range(8):
            shard = (entry - entry % 2) + (entry % 2 ^ flip)
            outw_ref[pl.ds(pl.multiple_of(shard * 48, 16), 48), :] = packed_ref[entry, 144:192, :]

    lanes = pl.ds(pl.multiple_of(pl.program_id(0) * 128, 128), 128)
    unpack_head(flip, packed_ref, lanes, w_ref, 0)
    for part, x_ref in enumerate((own_x, other_x)):
        all_ref[part * TOK : part * TOK + TOK, :] = jnp.dot(
            x_ref[...], w_ref[...], preferred_element_type=F32
        ).astype(BF16)
    keys = all_ref[:, 0:128]
    lane = lax.broadcasted_iota(jnp.int32, (SEG, 128), 1)
    values = jnp.where(lane < HEAD_DIM, swap_halves(keys.astype(F32)), 1.0).astype(BF16)
    tile = NEAR_TILE
    out_lane = lax.broadcasted_iota(jnp.int32, (tile, 128), 1)
    for at in range(0, SEG, tile):
        scores = lax.dot_general(
            all_ref[at : at + tile, 128:256],
            keys,
            (((1,), (1,)), ((), ())),
            preferred_element_type=F32,
        )
        row_max = jnp.max(scores, axis=1, keepdims=True)
        weights = jnp.exp2((scores - row_max) * EXP_SCALE).astype(BF16)
        summed = jnp.dot(weights, values, preferred_element_type=F32)
        result = jnp.where(
            out_lane < HEAD_DIM, summed / swap_halves(summed), row_max * SCALE + jnp.log(summed)
        )
        if tile == SEG:
            keep_ref[...] = result[:TOK]
            give_ref[...] = result[TOK:]
        else:
            out_ref = keep_ref if at < TOK else give_ref
            out_ref[at % TOK : at % TOK + tile, :] = result


def near_level(base, own_x, other_x, packed):
    half = shape_of(TOK, HALF * 128, dtype=F32)
    tiles = pl.BlockSpec((TOK, D), lambda h: (0, 0))
    part = pl.BlockSpec((TOK, 128), lambda h: (0, h))
    return pl.pallas_call(
        near_kernel,
        out_shape=[half, half, shape_of(INNER, INNER)],
        grid=(HALF,),
        in_specs=[SMEM, tiles, tiles, pl.BlockSpec((8, 192, INNER), lambda h: (0, 0, 0))],
        out_specs=[part, part, pl.BlockSpec((INNER, INNER), lambda h: (0, 0))],
        scratch_shapes=[pltpu.VMEM((D, 256), BF16), pltpu.VMEM((SEG, 256), BF16)],
        cost_estimate=pl.CostEstimate(
            flops=4 * HALF * SEG * SEG * 128, bytes_accessed=5 << 20, transcendentals=HALF * SEG * SEG
        ),
        compiler_params=pltpu.CompilerParams(vmem_limit_bytes=LIMITS[1]),
        interpret=INTERPRET,
    )(base, own_x, other_x, packed)


def far_kernel(core_ref, got_ref, back_ref):
    core = core_ref[0]
    keys = got_ref[:, 0:32, :].reshape(POS * 32, 128)
    wide = got_ref[:, 32:48, :].reshape(POS * 16, 128).astype(F32)
    lane = lax.broadcasted_iota(jnp.int32, (POS * 32, 128), 1)
    values = jnp.where(lane < HEAD_DIM, swap_halves(keys.astype(F32)), 1.0).astype(BF16)
    q_lane = lax.broadcasted_iota(jnp.int32, (POS * 16, 128), 1)
    q_row = lax.broadcasted_iota(jnp.int32, (POS * 16, 128), 0)
    place = jnp.right_shift(q_lane, 4)
    mine = jnp.bitwise_and(q_lane, 15) == jnp.bitwise_and(q_row, 15)
    source = lax.broadcasted_iota(jnp.int32, (POS, POS * 16), 0)
    member = jnp.right_shift(lax.broadcasted_iota(jnp.int32, (POS, POS * 16), 1), 4)
    spread = jnp.where(source == member, 1.0, 0.0).astype(BF16)
    queries = jnp.concatenate(
        [jnp.where(q_lane < HEAD_DIM, part, 0.0) for part in (wide, swap_halves(wide))], axis=0
    ).astype(BF16)
    scores = lax.dot_general(queries, keys, (((1,), (1,)), ((), ())), preferred_element_type=F32)
    row_max = jnp.max(scores, axis=1, keepdims=True)
    weights = jnp.exp2((scores - row_max) * EXP_SCALE).astype(BF16)
    summed = jnp.dot(weights, values, preferred_element_type=F32)
    swapped = swap_halves(summed)
    outs = summed / swapped
    logs = row_max * SCALE + jnp.log(swapped)
    for part in range(2):
        rows = slice(part * POS * 16, (part + 1) * POS * 16)
        out = outs[rows].reshape(POS, 16, 128)
        packed = jnp.concatenate([out[:, 0:8, :HEAD_DIM], out[:, 8:16, :HEAD_DIM]], axis=2)
        high, middle, low = parts3(logs[rows])
        stats = jnp.where(
            place == 0, high, jnp.where(place == 1, middle, jnp.where(place == 2, low, 0.0))
        )
        stats = jnp.where(mine, stats, 0.0).astype(BF16)
        means = jnp.dot(spread, stats, preferred_element_type=F32)
        means = jnp.broadcast_to(means[:, None, :], (POS, 8, 128))
        block = jnp.concatenate([packed, means], axis=1).astype(BF16)
        back_ref[:, pl.ds(core if part == 0 else 1 - core, 1)] = block[:, None]


def prepare_kernel(
    base_ref, offset_ref, keep_ref, got_ref, order_ref, gain_ref,
    dense_ref, rows_ref, spread_ref, scale_ref,
):
    core = base_ref[0]
    width = HALF * HEAD_DIM
    hots = [[], []]
    order = (order_ref[...] - base_ref[1]).astype(F32)
    for group, near_ref in enumerate((keep_ref, got_ref)):
        dense_ref[:, group * width : (group + 1) * width] = jnp.concatenate(
            [near_ref[:, head * 128 : head * 128 + HEAD_DIM] for head in range(HALF)], axis=1
        )
        heads = core if group == 0 else 1 - core
        for head in range(HALF):
            pieces = jnp.concatenate(parts3(near_ref[:, head * 128 : head * 128 + 128]), axis=1)
            offset = offset_ref[heads * HALF + head]
            for view in range(2):
                chosen = one_hot(chosen_rows(view, offset, order), TOK)
                hots[view].append(chosen)
                taken = jnp.dot(chosen, pieces, preferred_element_type=F32)
                at = group * 192 + (view * HALF + head) * SPARSE
                rows_ref[at : at + SPARSE, :] = taken[:, :128] + taken[:, 128:256] + taken[:, 256:]
    hots = [jnp.concatenate(part, axis=0) for part in hots]
    for at, part in enumerate(
        (hots[0][:128], jnp.concatenate([hots[0][128:], hots[1][128:]], axis=0), hots[1][:128])
    ):
        spread_ref[:, at * 128 : at * 128 + 128] = part.astype(F32).T.astype(BF16)
    gain = gain_ref[...].reshape(1, INNER)
    scale_ref[...] = jnp.where(
        core == 0, gain, jnp.concatenate([gain[:, width:], gain[:, :width]], axis=1)
    )


def output_kernel(
    core_ref, far_ref, dense_ref, rows_ref, spread_ref, gain_ref, own_w, other_w, plain_out, flip_out,
    plain_ref, flip_ref, sems,
):
    core = core_ref[0]
    lane = lax.broadcasted_iota(jnp.int32, (192, 128), 1)
    mine = jnp.bitwise_and(lane, 15) == jnp.bitwise_and(
        lax.broadcasted_iota(jnp.int32, (192, 128), 0), 15
    )
    deltas = []
    for group in range(2):
        outs, logs = [], []
        for k_half in range(2):
            blocks, stats = [], []
            for pair in range(2 * HALF):
                for q_part in range(2):
                    peer = (pair * 4 + q_part * 2 + k_half) * 2
                    block = far_ref[peer + (core if group == 0 else 1 - core)].astype(F32)
                    blocks += [block[0:8, :HEAD_DIM], block[0:8, HEAD_DIM:]]
                    stats += [block[8:16], block[8:16]]
            outs.append(jnp.concatenate(blocks, axis=0))
            found = jnp.where(mine, jnp.concatenate(stats, axis=0), 0.0)
            logs.append(jnp.sum(found, axis=1, keepdims=True))
        top = jnp.maximum(logs[0], logs[1])
        weight0, weight1 = jnp.exp(logs[0] - top), jnp.exp(logs[1] - top)
        joint = weight0 + weight1
        far = (weight0 * outs[0] + weight1 * outs[1]) / joint
        near = rows_ref[group * 192 : group * 192 + 192, :]
        gap = near[:, HEAD_DIM : HEAD_DIM + 1] - (top + jnp.log(joint))
        deltas.append((far - near[:, :HEAD_DIM]) / (1.0 + jnp.exp(gap)))
    width = HALF * HEAD_DIM
    row = jnp.right_shift(lax.broadcasted_iota(jnp.int32, (192, INNER), 0), 5)
    col = jnp.right_shift(lax.broadcasted_iota(jnp.int32, (192, INNER), 1), 6)
    none = jnp.zeros((HEAD_DIM, INNER), BF16)
    own_rows = pl.ds(pl.multiple_of(core * width, 64), width)
    other_rows = pl.ds(pl.multiple_of((1 - core) * width, 64), width)
    weights = [
        jnp.concatenate([part[own_rows, :], part[other_rows, :]], axis=0) for part in (own_w, other_w)
    ]
    copies = []
    for view, (out_ref, hbm_ref) in enumerate(((plain_ref, plain_out), (flip_ref, flip_out))):
        delta = jnp.concatenate([d[view * 96 : view * 96 + 96] for d in deltas], axis=0)
        blocks = jnp.where(row == col, jnp.concatenate([delta] * HEADS, axis=1), 0.0).astype(BF16)
        if view == 0:
            blocks = jnp.concatenate([blocks, none], axis=0)
        else:
            blocks = jnp.concatenate([none, blocks[128:], blocks[:128]], axis=0)
        for at in range(0, TOK, 256):
            attended = dense_ref[at : at + 256, :] + jnp.dot(
                spread_ref[at : at + 256, view * 128 : view * 128 + 256],
                blocks,
                preferred_element_type=F32,
            )
            average = jnp.mean(attended, axis=-1, keepdims=True)
            centred = attended - average
            variance = jnp.mean(centred * centred, axis=-1, keepdims=True)
            mixed = (centred * lax.rsqrt(variance + eps_norm) * gain_ref[...]).astype(BF16)
            for part, place in zip(weights, (core, 1 - core)):
                out_ref[at : at + 256, pl.ds(pl.multiple_of(place * INNER, 128), INNER)] = jnp.dot(
                    mixed, part, preferred_element_type=F32
                ).astype(BF16)
            rows = pl.ds(at, 256)
            copies.append(
                pltpu.make_async_copy(
                    out_ref.at[rows], hbm_ref.at[rows], sems.at[view * 2 + at // 256]
                )
            )
            copies[-1].start()
    for copy in copies:
        copy.wait()


def core_swap(block):
    return lax.ppermute(block, "core", [(0, 1), (1, 0)])


def layer(
    tile_features, flip_perm, head_offsets, input_gain, projection, output_gain, output_weight
):
    core = lax.axis_index("core").astype(jnp.int32)
    pos = lax.axis_index("pos").astype(jnp.int32)
    rank = pos * 2 + core
    core_id = core[None]
    base = jnp.stack([core, rank * TOK, (rank ^ 1) * TOK, lax.axis_index("yh").astype(jnp.int32)])

    last = 2 * POS - 1
    ctx = ("pos", "core")
    own_perm = lax.ppermute(flip_perm, ctx, [(last - r, r) for r in range(2 * POS)])
    packed = gather_weights(core_id, projection, output_weight)
    other_perm = core_swap(own_perm)
    own_x = call(norm_kernel, shape_of(TOK, D), [VMEM, VMEM], moved=2 << 20)(
        tile_features[0], input_gain
    )
    other_x = core_swap(own_x)

    picked = call(
        pick_kernel,
        shape_of(HALF * 128, D),
        [SMEM, SMEM, VMEM, VMEM, VMEM, VMEM],
        flops=2 * HALF * 128 * SEG * D,
        moved=3 << 20,
    )(base, head_offsets, own_x, other_x, own_perm, other_perm)
    send = call(
        send_kernel,
        shape_of(POS, 48, 128),
        [SMEM, VMEM, VMEM],
        [pltpu.VMEM((D, D), BF16)],
        flops=2 * HALF * 128 * D * 256,
        moved=2 << 20,
        limit=LIMITS[0],
    )(base, picked, packed)

    got = lax.all_to_all(send, "pos", 0, 0, tiled=True)
    keep, give, own_w = near_level(base, own_x, other_x, packed)
    near_got = core_swap(give)
    back = call(
        far_kernel, shape_of(POS, 2, 16, 128), [SMEM, VMEM], flops=4 * SEG * SEG * 128, moved=1 << 20,
        limit=LIMITS[2],
    )(core_id, got)
    far = lax.all_to_all(back.reshape(2 * POS, 16, 128), ctx, 0, 0, tiled=True)

    other_w = core_swap(own_w)
    prepared = call(
        prepare_kernel,
        [
            shape_of(TOK, INNER, dtype=F32),
            shape_of(INNER, 128, dtype=F32),
            shape_of(TOK, INNER),
            shape_of(1, INNER, dtype=F32),
        ],
        [SMEM, SMEM, VMEM, VMEM, VMEM, VMEM],
        flops=1 << 28,
        moved=4 << 20,
        limit=LIMITS[3],
    )(base, head_offsets, keep, near_got, own_perm, output_gain)

    plain_view, flipped_view = call(
        output_kernel,
        [shape_of(TOK, D), shape_of(TOK, D)],
        [SMEM] + [VMEM] * 7,
        [pltpu.VMEM((TOK, D), BF16), pltpu.VMEM((TOK, D), BF16), pltpu.SemaphoreType.DMA((4,))],
        outs=[ANY, ANY],
        flops=4 * SEG * INNER * D,
        moved=4 << 20,
        limit=LIMITS[4],
    )(core_id, far, *prepared, own_w, other_w)
    return (plain_view[None], flipped_view[None])


def solution(mesh):
    fine = Mesh(mesh.devices.reshape(DP_X, DP_Y, POS, 2), ("x", "yh", "pos", "core"))
    dp, ctx = ("x", "yh"), ("pos", "core")
    placed = (P(dp, ctx, None), P(dp, ctx), P(), P(), P(dp, None), P(), P(dp, None))
    return jax.shard_map(
        layer,
        mesh=fine,
        in_specs=placed,
        out_specs=(P(dp, ctx, None), P(dp, ctx, None)),
        check_vma=False,
    )
```

```python
import functools

import jax
import jax.numpy as jnp
from jax import lax
from jax.experimental import pallas as pl
from jax.experimental.pallas import tpu as pltpu
from jax.sharding import Mesh, PartitionSpec as P


HEADS = 6
HEAD_DIM = 64
INNER = 384
D = 768
RATIO = 16
TOK = 512
SEG = 1024
HALF = 3
SPARSE = TOK // RATIO
POS = 32
DP_X, DP_Y = 4, 2
INTERPRET = False
NEAR_TILE = 512
LIMITS = [24 << 20, 60 * 1024 * 1024, 24 << 20, 24 << 20, 24 << 20]

eps_norm = 1e-05
EXP_SCALE = HEAD_DIM ** (-0.5) * 1.4426950408889634
SCALE = HEAD_DIM ** (-0.5)

F32 = jnp.float32
BF16 = jnp.bfloat16
VMEM = pl.BlockSpec(memory_space=pltpu.VMEM)
SMEM = pl.BlockSpec(memory_space=pltpu.SMEM)
ANY = pl.BlockSpec(memory_space=pl.ANY)


def call(kernel, out_shape, specs, scratch=(), flops=0, moved=0, limit=24 << 20, outs=None):
    single = not isinstance(out_shape, (list, tuple))
    return pl.pallas_call(
        kernel,
        out_shape=out_shape,
        in_specs=specs,
        out_specs=outs or (VMEM if single else [VMEM] * len(out_shape)),
        scratch_shapes=list(scratch),
        cost_estimate=pl.CostEstimate(flops=flops, bytes_accessed=moved, transcendentals=0),
        compiler_params=pltpu.CompilerParams(vmem_limit_bytes=limit),
        interpret=INTERPRET,
    )


def shape_of(*dims, dtype=BF16):
    return jax.ShapeDtypeStruct(dims, dtype)


def swap_halves(block):
    return jnp.concatenate([block[:, HEAD_DIM:], block[:, :HEAD_DIM]], axis=1)


def parts3(value):
    high = value.astype(BF16)
    rest = value - high.astype(F32)
    middle = rest.astype(BF16)
    low = (rest - middle.astype(F32)).astype(BF16)
    return high, middle, low


def pack_kernel(core_ref, proj_ref, outw_ref, packed_ref):
    for core in range(2):

        @pl.when(core_ref[0] == core)
        def _():
            for head in range(HALF):
                col = (core * HALF + head) * HEAD_DIM
                lanes = slice(head * 128, head * 128 + 128)
                keys = proj_ref[:, INNER + col : INNER + col + HEAD_DIM].astype(F32)
                values = proj_ref[:, 2 * INNER + col : 2 * INNER + col + HEAD_DIM].astype(F32)
                queries = proj_ref[:, col : col + HEAD_DIM].astype(F32)
                packed_ref[0:96, lanes] = jnp.concatenate([keys, values], axis=1).astype(BF16)
                packed_ref[96:144, lanes] = jnp.concatenate(
                    [queries[:48], queries[48:]], axis=1
                ).astype(BF16)
            packed_ref[144:192, :] = outw_ref[:, core * INNER : (core + 1) * INNER]


def pack_weights(core, projection, output_weight):
    return call(pack_kernel, shape_of(192, INNER), [SMEM, VMEM, VMEM])(
        core, projection, output_weight
    )


def fan_kernel(at, part_ref, *refs):
    both_ref, sems = refs[-2:]
    copies = []
    for peer in range(DP_X):
        copies.append(pltpu.make_async_copy(part_ref, both_ref.at[peer, at], sems.at[peer]))
        copies[-1].start()
    for copy in copies:
        copy.wait()


def fan_out(at, part, *buffer):
    return pl.pallas_call(
        functools.partial(fan_kernel, at),
        out_shape=shape_of(DP_X, DP_Y, 192, INNER),
        in_specs=[VMEM] + [ANY] * len(buffer),
        out_specs=ANY,
        scratch_shapes=[pltpu.SemaphoreType.DMA((DP_X,))],
        input_output_aliases={1: 0} if buffer else {},
        compiler_params=pltpu.CompilerParams(vmem_limit_bytes=24 << 20),
        interpret=INTERPRET,
    )(part, *buffer)


def gather_weights(core, projection, output_weight):
    packed = pack_weights(core, projection, output_weight)
    other = lax.ppermute(packed, "yh", [(0, 1), (1, 0)])
    both = fan_out(0, packed)
    both = fan_out(1, other, both)
    got = lax.all_to_all(both, "x", 0, 0, tiled=True)
    return got.reshape(DP_X * DP_Y, 192, INNER)


def norm_kernel(x_ref, gain_ref, out_ref):
    gain = gain_ref[...].reshape(1, D)
    for row in range(0, TOK, 128):
        values = x_ref[row : row + 128, :].astype(F32)
        average = jnp.mean(values, axis=-1, keepdims=True)
        centred = values - average
        variance = jnp.mean(centred * centred, axis=-1, keepdims=True)
        out_ref[row : row + 128, :] = (
            centred * lax.rsqrt(variance + eps_norm) * gain
        ).astype(BF16)


def chosen_rows(view, offset, order):
    rows = lax.broadcasted_iota(jnp.int32, (SPARSE, 1), 0) * RATIO + offset
    if view == 0:
        return rows
    lane = lax.broadcasted_iota(jnp.int32, (SPARSE, TOK), 1)
    tiles = jnp.broadcast_to(order, (SPARSE, TOK))
    picked = jnp.sum(jnp.where(lane == rows, tiles, 0.0), axis=1, keepdims=True)
    return picked.astype(jnp.int32)


def one_hot(index, width):
    token = lax.broadcasted_iota(jnp.int32, (index.shape[0], width), 1)
    return jnp.where(token == index, 1.0, 0.0).astype(BF16)


def pick_kernel(base_ref, offset_ref, own_x, other_x, own_perm, other_perm, picked_ref):
    orders = [
        (perm[...] - base_ref[at]).astype(F32) for at, perm in ((1, own_perm), (2, other_perm))
    ]
    hots = [[], []]
    for head in range(HALF):
        offset = offset_ref[base_ref[0] * HALF + head]
        for view in range(2):
            for part in range(2):
                chosen = one_hot(chosen_rows(view, offset, orders[part]), TOK)
                hots[part].append(chosen)
    for part, x_ref in enumerate((own_x, other_x)):
        rows = jnp.dot(
            jnp.concatenate(hots[part], axis=0), x_ref[...], preferred_element_type=F32
        ).astype(BF16)
        for block in range(2 * HALF):
            at = block * 2 * SPARSE + part * SPARSE
            picked_ref[at : at + SPARSE, :] = rows[block * SPARSE : block * SPARSE + SPARSE]


def unpack_head(flip, packed_ref, lanes, w_ref, at):
    lane = lax.broadcasted_iota(jnp.int32, (48, 128), 1)
    for entry in range(8):
        shard = (entry - entry % 2) + (entry % 2 ^ flip)
        row = pl.multiple_of(shard * 96, 16)
        w_ref[pl.ds(row, 96), at : at + 128] = packed_ref[entry, 0:96, lanes]
        folded = packed_ref[entry, 96:144, lanes].astype(F32)
        for first, part in ((0, folded), (48, swap_halves(folded))):
            w_ref[pl.ds(pl.multiple_of(row + first, 16), 48), at + 128 : at + 256] = jnp.where(
                lane < HEAD_DIM, part, 0.0
            ).astype(BF16)


def send_kernel(base_ref, picked_ref, packed_ref, send_ref, w_ref):
    for head in range(HALF):
        at = head * 256
        unpack_head(base_ref[3], packed_ref, slice(head * 128, head * 128 + 128), w_ref, at)
        far_rows = jnp.dot(
            picked_ref[head * 128 : head * 128 + 128, :],
            w_ref[:, at : at + 256],
            preferred_element_type=F32,
        ).astype(BF16)
        far_kv, far_q = far_rows[:, 0:128], far_rows[:, 128:256].astype(F32)
        for view in range(2):
            pair = (view * HALF + head) * 4
            for q_part in range(2):
                row = view * 2 * SPARSE + q_part * 16
                folded = (
                    far_q[row : row + 16] + swap_halves(far_q[SPARSE + row : SPARSE + row + 16])
                ).astype(BF16)
                for k_half in range(2):
                    peer = pair + q_part * 2 + k_half
                    first = view * 2 * SPARSE + k_half * SPARSE
                    send_ref[peer, 0:32, :] = far_kv[first : first + SPARSE]
                    send_ref[peer, 32:48, :] = folded
    for peer in range(4 * 2 * HALF, POS):
        send_ref[peer] = jnp.zeros((48, 128), BF16)


def near_kernel(base_ref, own_x, other_x, packed_ref, keep_ref, give_ref, outw_ref, w_ref, all_ref):
    flip = base_ref[3]

    @pl.when(pl.program_id(0) == 0)
    def _():
        for entry in range(8):
            shard = (entry - entry % 2) + (entry % 2 ^ flip)
            outw_ref[pl.ds(pl.multiple_of(shard * 48, 16), 48), :] = packed_ref[entry, 144:192, :]

    lanes = pl.ds(pl.multiple_of(pl.program_id(0) * 128, 128), 128)
    unpack_head(flip, packed_ref, lanes, w_ref, 0)
    for part, x_ref in enumerate((own_x, other_x)):
        all_ref[part * TOK : part * TOK + TOK, :] = jnp.dot(
            x_ref[...], w_ref[...], preferred_element_type=F32
        ).astype(BF16)
    keys = all_ref[:, 0:128]
    lane = lax.broadcasted_iota(jnp.int32, (SEG, 128), 1)
    values = jnp.where(lane < HEAD_DIM, swap_halves(keys.astype(F32)), 1.0).astype(BF16)
    tile = NEAR_TILE
    out_lane = lax.broadcasted_iota(jnp.int32, (tile, 128), 1)
    for at in range(0, SEG, tile):
        scores = lax.dot_general(
            all_ref[at : at + tile, 128:256],
            keys,
            (((1,), (1,)), ((), ())),
            preferred_element_type=F32,
        )
        row_max = jnp.max(scores, axis=1, keepdims=True)
        weights = jnp.exp2((scores - row_max) * EXP_SCALE).astype(BF16)
        summed = jnp.dot(weights, values, preferred_element_type=F32)
        result = jnp.where(
            out_lane < HEAD_DIM, summed / swap_halves(summed), row_max * SCALE + jnp.log(summed)
        )
        if tile == SEG:
            keep_ref[...] = result[:TOK]
            give_ref[...] = result[TOK:]
        else:
            out_ref = keep_ref if at < TOK else give_ref
            out_ref[at % TOK : at % TOK + tile, :] = result


def near_level(base, own_x, other_x, packed):
    half = shape_of(TOK, HALF * 128, dtype=F32)
    tiles = pl.BlockSpec((TOK, D), lambda h: (0, 0))
    part = pl.BlockSpec((TOK, 128), lambda h: (0, h))
    return pl.pallas_call(
        near_kernel,
        out_shape=[half, half, shape_of(INNER, INNER)],
        grid=(HALF,),
        in_specs=[SMEM, tiles, tiles, pl.BlockSpec((8, 192, INNER), lambda h: (0, 0, 0))],
        out_specs=[part, part, pl.BlockSpec((INNER, INNER), lambda h: (0, 0))],
        scratch_shapes=[pltpu.VMEM((D, 256), BF16), pltpu.VMEM((SEG, 256), BF16)],
        cost_estimate=pl.CostEstimate(
            flops=4 * HALF * SEG * SEG * 128, bytes_accessed=5 << 20, transcendentals=HALF * SEG * SEG
        ),
        compiler_params=pltpu.CompilerParams(vmem_limit_bytes=LIMITS[1]),
        interpret=INTERPRET,
    )(base, own_x, other_x, packed)


def far_kernel(core_ref, got_ref, back_ref):
    core = core_ref[0]
    keys = got_ref[:, 0:32, :].reshape(POS * 32, 128)
    wide = got_ref[:, 32:48, :].reshape(POS * 16, 128).astype(F32)
    lane = lax.broadcasted_iota(jnp.int32, (POS * 32, 128), 1)
    values = jnp.where(lane < HEAD_DIM, swap_halves(keys.astype(F32)), 1.0).astype(BF16)
    q_lane = lax.broadcasted_iota(jnp.int32, (POS * 16, 128), 1)
    q_row = lax.broadcasted_iota(jnp.int32, (POS * 16, 128), 0)
    place = jnp.right_shift(q_lane, 4)
    mine = jnp.bitwise_and(q_lane, 15) == jnp.bitwise_and(q_row, 15)
    source = lax.broadcasted_iota(jnp.int32, (POS, POS * 16), 0)
    member = jnp.right_shift(lax.broadcasted_iota(jnp.int32, (POS, POS * 16), 1), 4)
    spread = jnp.where(source == member, 1.0, 0.0).astype(BF16)
    queries = jnp.concatenate(
        [jnp.where(q_lane < HEAD_DIM, part, 0.0) for part in (wide, swap_halves(wide))], axis=0
    ).astype(BF16)
    scores = lax.dot_general(queries, keys, (((1,), (1,)), ((), ())), preferred_element_type=F32)
    row_max = jnp.max(scores, axis=1, keepdims=True)
    weights = jnp.exp2((scores - row_max) * EXP_SCALE).astype(BF16)
    summed = jnp.dot(weights, values, preferred_element_type=F32)
    swapped = swap_halves(summed)
    outs = summed / swapped
    logs = row_max * SCALE + jnp.log(swapped)
    for part in range(2):
        rows = slice(part * POS * 16, (part + 1) * POS * 16)
        out = outs[rows].reshape(POS, 16, 128)
        packed = jnp.concatenate([out[:, 0:8, :HEAD_DIM], out[:, 8:16, :HEAD_DIM]], axis=2)
        high, middle, low = parts3(logs[rows])
        stats = jnp.where(
            place == 0, high, jnp.where(place == 1, middle, jnp.where(place == 2, low, 0.0))
        )
        stats = jnp.where(mine, stats, 0.0).astype(BF16)
        means = jnp.dot(spread, stats, preferred_element_type=F32)
        means = jnp.broadcast_to(means[:, None, :], (POS, 8, 128))
        block = jnp.concatenate([packed, means], axis=1).astype(BF16)
        back_ref[:, pl.ds(core if part == 0 else 1 - core, 1)] = block[:, None]


def prepare_kernel(
    base_ref, offset_ref, keep_ref, got_ref, order_ref, gain_ref,
    dense_ref, rows_ref, spread_ref, scale_ref,
):
    core = base_ref[0]
    width = HALF * HEAD_DIM
    hots = [[], []]
    order = (order_ref[...] - base_ref[1]).astype(F32)
    for group, near_ref in enumerate((keep_ref, got_ref)):
        dense_ref[:, group * width : (group + 1) * width] = jnp.concatenate(
            [near_ref[:, head * 128 : head * 128 + HEAD_DIM] for head in range(HALF)], axis=1
        )
        heads = core if group == 0 else 1 - core
        for head in range(HALF):
            pieces = jnp.concatenate(parts3(near_ref[:, head * 128 : head * 128 + 128]), axis=1)
            offset = offset_ref[heads * HALF + head]
            for view in range(2):
                chosen = one_hot(chosen_rows(view, offset, order), TOK)
                hots[view].append(chosen)
                taken = jnp.dot(chosen, pieces, preferred_element_type=F32)
                at = group * 192 + (view * HALF + head) * SPARSE
                rows_ref[at : at + SPARSE, :] = taken[:, :128] + taken[:, 128:256] + taken[:, 256:]
    hots = [jnp.concatenate(part, axis=0) for part in hots]
    for at, part in enumerate(
        (hots[0][:128], jnp.concatenate([hots[0][128:], hots[1][128:]], axis=0), hots[1][:128])
    ):
        spread_ref[:, at * 128 : at * 128 + 128] = part.astype(F32).T.astype(BF16)
    gain = gain_ref[...].reshape(1, INNER)
    scale_ref[...] = jnp.where(
        core == 0, gain, jnp.concatenate([gain[:, width:], gain[:, :width]], axis=1)
    )


def output_kernel(
    core_ref, far_ref, dense_ref, rows_ref, spread_ref, gain_ref, own_w, other_w, plain_out, flip_out,
    plain_ref, flip_ref, sems,
):
    core = core_ref[0]
    lane = lax.broadcasted_iota(jnp.int32, (192, 128), 1)
    mine = jnp.bitwise_and(lane, 15) == jnp.bitwise_and(
        lax.broadcasted_iota(jnp.int32, (192, 128), 0), 15
    )
    deltas = []
    for group in range(2):
        outs, logs = [], []
        for k_half in range(2):
            blocks, stats = [], []
            for pair in range(2 * HALF):
                for q_part in range(2):
                    peer = (pair * 4 + q_part * 2 + k_half) * 2
                    block = far_ref[peer + (core if group == 0 else 1 - core)].astype(F32)
                    blocks += [block[0:8, :HEAD_DIM], block[0:8, HEAD_DIM:]]
                    stats += [block[8:16], block[8:16]]
            outs.append(jnp.concatenate(blocks, axis=0))
            found = jnp.where(mine, jnp.concatenate(stats, axis=0), 0.0)
            logs.append(jnp.sum(found, axis=1, keepdims=True))
        top = jnp.maximum(logs[0], logs[1])
        weight0, weight1 = jnp.exp(logs[0] - top), jnp.exp(logs[1] - top)
        joint = weight0 + weight1
        far = (weight0 * outs[0] + weight1 * outs[1]) / joint
        near = rows_ref[group * 192 : group * 192 + 192, :]
        gap = near[:, HEAD_DIM : HEAD_DIM + 1] - (top + jnp.log(joint))
        deltas.append((far - near[:, :HEAD_DIM]) / (1.0 + jnp.exp(gap)))
    width = HALF * HEAD_DIM
    row = jnp.right_shift(lax.broadcasted_iota(jnp.int32, (192, INNER), 0), 5)
    col = jnp.right_shift(lax.broadcasted_iota(jnp.int32, (192, INNER), 1), 6)
    none = jnp.zeros((HEAD_DIM, INNER), BF16)
    own_rows = pl.ds(pl.multiple_of(core * width, 64), width)
    other_rows = pl.ds(pl.multiple_of((1 - core) * width, 64), width)
    weights = [
        jnp.concatenate([part[own_rows, :], part[other_rows, :]], axis=0) for part in (own_w, other_w)
    ]
    copies = []
    for view, (out_ref, hbm_ref) in enumerate(((plain_ref, plain_out), (flip_ref, flip_out))):
        delta = jnp.concatenate([d[view * 96 : view * 96 + 96] for d in deltas], axis=0)
        blocks = jnp.where(row == col, jnp.concatenate([delta] * HEADS, axis=1), 0.0).astype(BF16)
        if view == 0:
            blocks = jnp.concatenate([blocks, none], axis=0)
        else:
            blocks = jnp.concatenate([none, blocks[128:], blocks[:128]], axis=0)
        for at in range(0, TOK, 256):
            attended = dense_ref[at : at + 256, :] + jnp.dot(
                spread_ref[at : at + 256, view * 128 : view * 128 + 256],
                blocks,
                preferred_element_type=F32,
            )
            average = jnp.mean(attended, axis=-1, keepdims=True)
            centred = attended - average
            variance = jnp.mean(centred * centred, axis=-1, keepdims=True)
            mixed = (centred * lax.rsqrt(variance + eps_norm) * gain_ref[...]).astype(BF16)
            for part, place in zip(weights, (core, 1 - core)):
                out_ref[at : at + 256, pl.ds(pl.multiple_of(place * INNER, 128), INNER)] = jnp.dot(
                    mixed, part, preferred_element_type=F32
                ).astype(BF16)
            rows = pl.ds(at, 256)
            copies.append(
                pltpu.make_async_copy(
                    out_ref.at[rows], hbm_ref.at[rows], sems.at[view * 2 + at // 256]
                )
            )
            copies[-1].start()
    for copy in copies:
        copy.wait()


def core_swap(block):
    return lax.ppermute(block, "core", [(0, 1), (1, 0)])


def layer(
    tile_features, flip_perm, head_offsets, input_gain, projection, output_gain, output_weight
):
    core = lax.axis_index("core").astype(jnp.int32)
    pos = lax.axis_index("pos").astype(jnp.int32)
    rank = pos * 2 + core
    core_id = core[None]
    base = jnp.stack([core, rank * TOK, (rank ^ 1) * TOK, lax.axis_index("yh").astype(jnp.int32)])

    last = 2 * POS - 1
    ctx = ("pos", "core")
    own_perm = lax.ppermute(flip_perm, ctx, [(last - r, r) for r in range(2 * POS)])
    packed = gather_weights(core_id, projection, output_weight)
    other_perm = core_swap(own_perm)
    own_x = call(norm_kernel, shape_of(TOK, D), [VMEM, VMEM], moved=2 << 20)(
        tile_features[0], input_gain
    )
    other_x = core_swap(own_x)

    picked = call(
        pick_kernel,
        shape_of(HALF * 128, D),
        [SMEM, SMEM, VMEM, VMEM, VMEM, VMEM],
        flops=2 * HALF * 128 * SEG * D,
        moved=3 << 20,
    )(base, head_offsets, own_x, other_x, own_perm, other_perm)
    send = call(
        send_kernel,
        shape_of(POS, 48, 128),
        [SMEM, VMEM, VMEM],
        [pltpu.VMEM((D, D), BF16)],
        flops=2 * HALF * 128 * D * 256,
        moved=2 << 20,
        limit=LIMITS[0],
    )(base, picked, packed)

    got = lax.all_to_all(send, "pos", 0, 0, tiled=True)
    keep, give, own_w = near_level(base, own_x, other_x, packed)
    near_got = core_swap(give)
    back = call(
        far_kernel, shape_of(POS, 2, 16, 128), [SMEM, VMEM], flops=4 * SEG * SEG * 128, moved=1 << 20,
        limit=LIMITS[2],
    )(core_id, got)
    far = lax.all_to_all(back.reshape(2 * POS, 16, 128), ctx, 0, 0, tiled=True)

    other_w = core_swap(own_w)
    prepared = call(
        prepare_kernel,
        [
            shape_of(TOK, INNER, dtype=F32),
            shape_of(INNER, 128, dtype=F32),
            shape_of(TOK, INNER),
            shape_of(1, INNER, dtype=F32),
        ],
        [SMEM, SMEM, VMEM, VMEM, VMEM, VMEM],
        flops=1 << 28,
        moved=4 << 20,
        limit=LIMITS[3],
    )(base, head_offsets, keep, near_got, own_perm, output_gain)

    plain_view, flipped_view = call(
        output_kernel,
        [shape_of(TOK, D), shape_of(TOK, D)],
        [SMEM] + [VMEM] * 7,
        [pltpu.VMEM((TOK, D), BF16), pltpu.VMEM((TOK, D), BF16), pltpu.SemaphoreType.DMA((4,))],
        outs=[ANY, ANY],
        flops=4 * SEG * INNER * D,
        moved=4 << 20,
        limit=LIMITS[4],
    )(core_id, far, *prepared, own_w, other_w)
    return (plain_view[None], flipped_view[None])


def solution(mesh):
    fine = Mesh(mesh.devices.reshape(DP_X, DP_Y, POS, 2), ("x", "yh", "pos", "core"))
    dp, ctx = ("x", "yh"), ("pos", "core")
    placed = (P(dp, ctx, None), P(dp, ctx), P(), P(), P(dp, None), P(), P(dp, None))
    return jax.shard_map(
        layer,
        mesh=fine,
        in_specs=placed,
        out_specs=(P(dp, ctx, None), P(dp, ctx, None)),
        check_vma=False,
    )
```
